32 devices in a mesh: dp: 8 (over z, x), seq: 4 (over y, core).
Axes of the slice: x: 2, y: 2, z: 4, core: 2. Of those that a mesh axis runs over, the one named last changes fastest.
Arguments:
- inputs: bfloat16 [16, 2048, 768], P('dp', 'seq'), may hold values from -6 to 6
- out_grad: bfloat16 [16, 2048, 768], P('dp', 'seq'), may hold values from -6 to 6
- w_qkv: bfloat16 [768, 2304], P('dp'), may hold values from -0.21875 to 0.21875
- w_attn_out: bfloat16 [768, 768], P('dp'), may hold values from -1.75 to 1.75
- w_up: bfloat16 [768, 3072], P('dp'), may hold values from -0.21875 to 0.21875
- w_down: bfloat16 [3072, 768], P('dp'), may hold values from -0.109375 to 0.109375
- bias_qv: bfloat16 [2, 768], P(None, 'dp'), may hold values from -3 to 3
- bias_out: bfloat16 [768], P('dp'), may hold values from -2 to 2
- bias_up: bfloat16 [3072], P('dp'), may hold values from -3 to 3
- bias_down: bfloat16 [768], P('dp'), may hold values from -2 to 2
- norm_gain: bfloat16 [2, 768], P(None, 'dp'), may hold values from 0.5 to 1.5
- norm_shift: bfloat16 [2, 768], P(None, 'dp'), may hold values from -2 to 2
- rand_blocks: int32 [12, 30, 3], replicated, may hold values from 1 to 30, as said below
Outputs:
- output: bfloat16 [16, 2048, 768], P('dp', 'seq')
- grad_inputs: bfloat16 [16, 2048, 768], P('dp', 'seq')
- grad_w_qkv: float32 [768, 2304], P('dp')
- grad_w_attn_out: float32 [768, 768], P('dp')
- grad_w_up: float32 [768, 3072], P('dp')
- grad_w_down: float32 [3072, 768], P('dp')
- grad_bias_qv: float32 [2, 768], P(None, 'dp')
- grad_bias_out: float32 [768], P('dp')
- grad_bias_up: float32 [3072], P('dp')
- grad_bias_down: float32 [768], P('dp')
- grad_norm_gain: float32 [2, 768], P(None, 'dp')
- grad_norm_shift: float32 [2, 768], P(None, 'dp')
The draws below stay inside these ranges and needn't reach their ends.
Inputs may be any that keep to these rules, and one draw needn't show every extreme that they name: rand_blocks[h, i - 1, :] holds 3 distinct block numbers for block row i of head h, none of them 0, 31, i - 1, i or i + 1.
All inputs are finite; a program needn't handle non-finite values.
Results may differ from the reference program's by a relative error of at most 0.02.
Values may be sent and summed in bfloat16 or wider, within the bound.
No kernel may reach another device: no remote copies, remote signals or barrier semaphores. Data moves between devices by JAX's collectives and lax.ppermute only.
A program may use at most 192 MiB of HBM per device.

```python
import jax
import jax.numpy as jnp
from jax import lax

D = 768
HEADS = 12
HEAD_DIM = 64
FF = 3072
BLOCK = 64
RAND = 3
LEN = 2048
SEQS = 16


def draw_rand_blocks(key, part):
    nblocks = LEN // BLOCK
    middle = jnp.arange(1, nblocks - 1, dtype=jnp.int32)
    column = jnp.arange(nblocks, dtype=jnp.int32)
    scores = jax.random.randint(key, (HEADS, nblocks - 2, nblocks), 0, 1 << 20, dtype=jnp.int32)
    scores = scores * nblocks + column
    banned = (column[None, :] == 0) | (column[None, :] == nblocks - 1) | (jnp.abs(column[None, :] - middle[:, None]) <= 1)
    scores = jnp.where(banned[None], -1, scores)
    picked = lax.top_k(scores, RAND)[1]
    return picked.astype(jnp.int32)


def level_of(stream_key, shape, cuts, smallest, top_value):
    level, own = 1.0, jax.random.fold_in(stream_key, 6)
    for dim, parts in cuts:
        draws = jnp.exp(jax.random.uniform(jax.random.fold_in(own, dim), (parts,), jnp.float32, smallest / len(cuts), top_value / len(cuts)))
        level = level * jnp.repeat(draws, shape[dim] // parts).reshape([-1 if axis == dim else 1 for axis in range(len(shape))])
    return level


def noise(key, dims, width, limit, cuts=(), kind=jnp.bfloat16):
    values = width * jax.random.normal(key, dims, jnp.float32)
    if cuts:
        values = values * level_of(key, dims, cuts, -0.22, 0.18)
    return jnp.clip(values, -limit, limit).astype(kind)


def setup_inputs(seed: int = 0) -> dict:
    keys = jax.random.split(jax.random.key(seed), 14)
    inputs = noise(keys[0], (SEQS, LEN, D), 1.0, 6.0, ((0, 8), (1, 4)))
    out_grad = noise(keys[1], (SEQS, LEN, D), 1.0, 6.0, ((0, 8), (1, 4)))
    w_qkv = noise(keys[2], (D, 3 * D), D ** -0.5, 0.21875, ((0, 8),))
    w_attn_out = noise(keys[3], (D, D), (D // 64) ** -0.5, 1.75, ((0, 8),))
    w_up = noise(keys[4], (D, FF), D ** -0.5, 0.21875, ((0, 8),))
    w_down = noise(keys[5], (FF, D), FF ** -0.5, 0.109375, ((0, 8),))
    bias_qv = noise(keys[6], (2, D), 0.5, 3.0, ((1, 8),))
    bias_out = noise(keys[7], (D,), 0.3, 2.0, ((0, 8),))
    bias_up = noise(keys[8], (FF,), 0.5, 3.0, ((0, 8),))
    bias_down = noise(keys[9], (D,), 0.3, 2.0, ((0, 8),))
    norm_gain = jnp.clip(1.0 + 0.1 * jax.random.normal(keys[10], (2, D), jnp.float32), 0.5, 1.5).astype(jnp.bfloat16)
    norm_shift = noise(keys[11], (2, D), 0.3, 2.0, ((1, 8),))
    rand_blocks = draw_rand_blocks(jax.random.fold_in(keys[13], 71), 0)
    return dict(inputs=inputs, out_grad=out_grad, w_qkv=w_qkv, w_attn_out=w_attn_out, w_up=w_up, w_down=w_down, bias_qv=bias_qv, bias_out=bias_out, bias_up=bias_up, bias_down=bias_down, norm_gain=norm_gain, norm_shift=norm_shift, rand_blocks=rand_blocks)


@jax.custom_vjp
def low(v):
    return lax.optimization_barrier(v.astype(jnp.bfloat16)).astype(jnp.float32)

@jax.custom_vjp
def low_back(v):
    return v

def low_keep(v):
    return (low(v), None)

def low_pass(kept, grad):
    return (grad,)

def back_keep(v):
    return (v, None)

def back_low(kept, grad):
    return (low(grad),)
low.defvjp(low_keep, low_pass)
low_back.defvjp(back_keep, back_low)
norm_eps = 1e-06
highest = lax.Precision.HIGHEST

def layer_norm(values, gain_row, shift_row):
    center = values - lax.optimization_barrier(jnp.mean(values, axis=-1, keepdims=True))
    spread = lax.optimization_barrier(jnp.mean(center * center, axis=-1, keepdims=True))
    return center * lax.rsqrt(spread + norm_eps) * gain_row + shift_row

def gelu_tanh(values):
    return 0.5 * values * (1.0 + jnp.tanh(0.7978845608028654 * (values + 0.044715 * values * values * values)))

def softmax_rows(scores):
    peak = lax.optimization_barrier(jnp.max(scores, axis=-1, keepdims=True))
    powers = jnp.exp(scores - peak)
    return powers / lax.optimization_barrier(jnp.sum(powers, axis=-1, keepdims=True))

def block_table_of(rand_rows, nblocks):
    middle = jnp.arange(1, nblocks - 1, dtype=jnp.int32)
    fixed_ids = jnp.stack([middle * 0, middle * 0 + (nblocks - 1), middle - 1, middle, middle + 1], axis=1)
    head_count = rand_rows.shape[0]
    fixed_all = jnp.broadcast_to(fixed_ids[None], (head_count,) + fixed_ids.shape)
    block_ids = jnp.concatenate([fixed_all, rand_rows.astype(jnp.int32)], axis=2)
    always = middle >= 0
    usable = jnp.concatenate([jnp.stack([always, always, middle != 1, always, middle != nblocks - 2], axis=1), jnp.ones((nblocks - 2, rand_rows.shape[2]), dtype=jnp.bool_)], axis=1)
    return (block_ids, usable)

def head_attention(queries, key_rows, value_rows, block_ids, key_mask):
    nblocks = queries.shape[0] // BLOCK
    head_width = queries.shape[1]
    scaling = HEAD_DIM ** (-0.5)
    query_blocks = queries.reshape(nblocks, BLOCK, head_width)
    key_blocks = key_rows.reshape(nblocks, BLOCK, head_width)
    value_blocks = value_rows.reshape(nblocks, BLOCK, head_width)
    key_near = key_blocks[block_ids].reshape(nblocks - 2, -1, head_width)
    value_near = value_blocks[block_ids].reshape(nblocks - 2, -1, head_width)
    raw_scores = low_back(jnp.einsum('nqd,nkd->nqk', query_blocks[1:-1], key_near, precision=highest))
    scores = jnp.where(key_mask[:, None, :], raw_scores * scaling, -1e+30)
    attention = low(softmax_rows(scores))
    middle_ctx = jnp.einsum('nqk,nkd->nqd', attention, value_near, precision=highest)
    edge_rows = jnp.concatenate([query_blocks[0], query_blocks[-1]], axis=0)
    edge_raw = low_back(jnp.einsum('qd,kd->qk', edge_rows, key_rows, precision=highest))
    edge_attention = low(softmax_rows(edge_raw * scaling))
    edge_ctx = jnp.dot(edge_attention, value_rows, precision=highest)
    return jnp.concatenate([edge_ctx[:BLOCK], middle_ctx.reshape(-1, head_width), edge_ctx[BLOCK:]], axis=0)

def layer_forward(tokens, w_qkv, w_attn_out, w_up, w_down, bias_qv, bias_out, bias_up, bias_down, norm_gain, norm_shift, block_ids, key_mask):
    length = tokens.shape[0]
    model_width = tokens.shape[1]
    bias_all = jnp.concatenate([bias_qv[0], jnp.zeros_like(bias_qv[0]), bias_qv[1]])
    projected = low_back(low(jnp.dot(tokens, w_qkv, precision=highest) + bias_all))
    heads_view = projected.reshape(length, 3, HEADS, HEAD_DIM).transpose(1, 2, 0, 3)
    context = jax.vmap(head_attention, in_axes=(0, 0, 0, 0, None))(heads_view[0], heads_view[1], heads_view[2], block_ids, key_mask)
    context = low_back(low(context.transpose(1, 0, 2).reshape(length, model_width)))
    branch = low_back(jnp.dot(context, w_attn_out, precision=highest) + bias_out)
    normed = layer_norm(tokens + branch, norm_gain[0], norm_shift[0])
    hidden = low_back(jnp.dot(low(normed), w_up, precision=highest) + bias_up)
    active = low(gelu_tanh(hidden))
    ffn_out = low_back(jnp.dot(active, w_down, precision=highest) + bias_down)
    return layer_norm(normed + ffn_out, norm_gain[1], norm_shift[1])

def reference(inputs, out_grad, w_qkv, w_attn_out, w_up, w_down, bias_qv, bias_out, bias_up, bias_down, norm_gain, norm_shift, rand_blocks):
    params = tuple((param_arg.astype(jnp.float32) for param_arg in (w_qkv, w_attn_out, w_up, w_down, bias_qv, bias_out, bias_up, bias_down, norm_gain, norm_shift)))
    block_ids, usable = block_table_of(rand_blocks, LEN // BLOCK)
    key_mask = jnp.repeat(usable, BLOCK, axis=1)

    def closed(tokens_in, *weights):
        return layer_forward(tokens_in, *weights, block_ids, key_mask)

    def per_sequence(running, seq_pair):
        tokens, cotangent = seq_pair
        result, pullback = jax.vjp(closed, tokens.astype(jnp.float32), *params)
        grads = pullback(cotangent.astype(jnp.float32))
        running = tuple((total_now + grad_part for total_now, grad_part in zip(running, grads[1:])))
        return (running, (result.astype(jnp.bfloat16), grads[0].astype(jnp.bfloat16)))
    start = tuple((jnp.zeros(param_arg.shape, jnp.float32) for param_arg in params))
    totals, (outputs, input_grads) = lax.scan(per_sequence, start, (inputs, out_grad))
    return (outputs, input_grads, totals[0], totals[1], totals[2], totals[3], totals[4], totals[5], totals[6], totals[7], totals[8], totals[9])
```

```python
import functools

import jax
import jax.numpy as jnp
from jax import lax
from jax.experimental import pallas as pl
from jax.experimental.pallas import tpu as pltpu
from jax.sharding import PartitionSpec as P

HEADS = 12
HEAD_DIM = 64
BLOCK = 64
RAND = 3

norm_eps = 1e-06
bf16 = jnp.bfloat16
f32 = jnp.float32
NN = (((1,), (0,)), ((), ()))
NT = (((1,), (1,)), ((), ()))
TN = (((0,), (0,)), ((), ()))
VMEM_BYTES = 56 << 20


def dot(a, b, dims=NN):
    return lax.dot_general(a, b, dims, preferred_element_type=f32)


def layer_norm(values, gain_row, shift_row):
    center = values - jnp.mean(values, axis=-1, keepdims=True)
    spread = jnp.mean(center * center, axis=-1, keepdims=True)
    return center * lax.rsqrt(spread + norm_eps) * gain_row + shift_row


def gelu_tanh(values):
    return (
        0.5
        * values
        * (1.0 + jnp.tanh(0.7978845608028654 * (values + 0.044715 * values * values * values)))
    )


def row_of(block, y, c, chunk_blocks):
    chunk = block // chunk_blocks
    place = (((chunk & 1) ^ c) << 1) | ((chunk >> 1) ^ y)
    return pl.multiple_of((place * chunk_blocks + block % chunk_blocks) * BLOCK, BLOCK)


class Rows:
    def __init__(self, info_ref, rand_ref, first_pair, nblocks):
        self.y, self.c = info_ref[0], info_ref[1]
        self.rand_ref = rand_ref
        self.nblocks = nblocks
        self.head = self.c * info_ref[2] + 2 * first_pair
        self.low = lax.broadcasted_iota(jnp.int32, (BLOCK, 128), 1) < HEAD_DIM
        self.low_row = lax.broadcasted_iota(jnp.int32, (1, 128), 1) < HEAD_DIM

    def at(self, block):
        return pl.ds(row_of(block, self.y, self.c, self.nblocks // 4), BLOCK)

    def two(self, tile):
        zero = jnp.zeros_like(tile)
        return jnp.concatenate(
            [jnp.where(self.low, tile, zero), jnp.where(self.low, zero, tile)], axis=0
        )

    def one(self, both):
        return jnp.where(self.low, both[:BLOCK], both[BLOCK:])

    def rand(self, i):
        middle = self.nblocks - 2
        base = (self.head * middle + (i - 1)) * RAND
        return [
            (self.rand_ref[base + t], self.rand_ref[base + middle * RAND + t]) for t in range(RAND)
        ]

    def near(self, load, ends, i, rand):
        mixed = [jnp.where(self.low, load(a), load(b)) for a, b in rand]
        return jnp.concatenate([ends, load(i - 1), load(i + 1), load(i)] + mixed, axis=0)

    def mask(self, scores, i):
        first = jnp.where(i == 1, -1e30, 0.0)
        last = jnp.where(i == self.nblocks - 2, -1e30, 0.0)
        bias = jnp.where(self.low_row, first, last).astype(f32)
        return jnp.concatenate(
            [scores[:, :128], scores[:, 128:256] + bias, scores[:, 256:]], axis=1
        )


def forward_kernel(info_ref, rand_ref, qkv_ref, ctx_ref, lse_ref, *, nblocks, first, unroll):
    rows = Rows(info_ref, rand_ref, pl.program_id(0) + first, nblocks)

    def load(block, column):
        return qkv_ref[rows.at(block), column * 128 : (column + 1) * 128]

    def finish(block, scores, values):
        peak = jnp.max(scores, axis=1, keepdims=True)
        powers = jnp.exp(scores - peak)
        totals = jnp.sum(powers, axis=1, keepdims=True)
        context = dot(powers.astype(bf16), values) / totals
        lse = jnp.broadcast_to(peak + jnp.log(totals), context.shape)
        ctx_ref[rows.at(block), :] = rows.one(context).astype(bf16)
        lse_ref[rows.at(block), :] = rows.one(lse)

    for edge in (0, nblocks - 1):
        scores = dot(rows.two(load(edge, 0)), qkv_ref[:, 128:256], NT)
        finish(edge, scores, qkv_ref[:, 256:384])
    key_ends = jnp.concatenate([load(0, 1), load(nblocks - 1, 1)], axis=0)
    value_ends = jnp.concatenate([load(0, 2), load(nblocks - 1, 2)], axis=0)

    def row(i):
        rand = rows.rand(i)
        keys = rows.near(lambda b: load(b, 1), key_ends, i, rand)
        values = rows.near(lambda b: load(b, 2), value_ends, i, rand)
        finish(i, rows.mask(dot(rows.two(load(i, 0)), keys, NT), i), values)

    def step(t, carry):
        for u in range(unroll):
            row(1 + t * unroll + u)
        return carry

    lax.fori_loop(0, (nblocks - 2) // unroll, step, 0)


def backward_kernel(
    info_ref, rand_ref, qkv_ref, grad_ref, ctx_ref, lse_ref, out_ref, sum_ref, key_sum, value_sum,
    *, nblocks, first, unroll
):
    rows = Rows(info_ref, rand_ref, pl.program_id(0) + first, nblocks)
    zero = jnp.zeros((BLOCK, 128), f32)

    def load(block, column):
        return qkv_ref[rows.at(block), column * 128 : (column + 1) * 128]

    def finish(block, scores, keys, values):
        grad = grad_ref[rows.at(block), :]
        both = grad.astype(f32) * ctx_ref[rows.at(block), :].astype(f32)
        row_dot = jnp.concatenate(
            [
                jnp.sum(jnp.where(rows.low, both, zero), axis=1, keepdims=True),
                jnp.sum(jnp.where(rows.low, zero, both), axis=1, keepdims=True),
            ],
            axis=0,
        )
        lse = lse_ref[rows.at(block), :]
        lse = jnp.concatenate([lse[:, 0:1], lse[:, HEAD_DIM : HEAD_DIM + 1]], axis=0)
        grad = rows.two(grad)
        attention = jnp.exp(scores - lse)
        attn_grad = dot(grad, values, NT)
        score_grad = (attention * (attn_grad - row_dot)).astype(bf16)
        query_grad = dot(score_grad, keys) * HEAD_DIM ** (-0.5)
        out_ref[rows.at(block), 0:128] = rows.one(query_grad).astype(bf16)
        return grad, attention.astype(bf16), score_grad

    for edge in (0, nblocks - 1):
        query = rows.two(load(edge, 0))
        keys, values = qkv_ref[:, 128:256], qkv_ref[:, 256:384]
        grad, attention, score_grad = finish(edge, dot(query, keys, NT), keys, values)
        if edge == 0:
            key_sum[...] = dot(score_grad, query, TN)
            value_sum[...] = dot(attention, grad, TN)
        else:
            key_sum[...] += dot(score_grad, query, TN)
            value_sum[...] += dot(attention, grad, TN)
    key_ends = jnp.concatenate([load(0, 1), load(nblocks - 1, 1)], axis=0)
    value_ends = jnp.concatenate([load(0, 2), load(nblocks - 1, 2)], axis=0)

    def row(i):
        rand = rows.rand(i)
        keys = rows.near(lambda b: load(b, 1), key_ends, i, rand)
        values = rows.near(lambda b: load(b, 2), value_ends, i, rand)
        query = rows.two(load(i, 0))
        scores = rows.mask(dot(query, keys, NT), i)
        grad, attention, score_grad = finish(i, scores, keys, values)
        for total, part in (
            (key_sum, dot(score_grad, query, TN)),
            (value_sum, dot(attention, grad, TN)),
        ):
            for slot, block in enumerate((0, nblocks - 1, i - 1, i + 1, i)):
                total[rows.at(block), :] += part[slot * BLOCK : (slot + 1) * BLOCK]
            for slot, (a, b) in enumerate(rand):
                tile = part[(5 + slot) * BLOCK : (6 + slot) * BLOCK]
                total[rows.at(a), :] += jnp.where(rows.low, tile, zero)
                total[rows.at(b), :] += jnp.where(rows.low, zero, tile)

    def step(t, carry):
        for u in range(unroll):
            row(1 + t * unroll + u)
        return carry

    lax.fori_loop(0, (nblocks - 2) // unroll, step, 0)
    out_ref[:, 128:256] = key_sum[...].astype(bf16)
    out_ref[:, 256:384] = value_sum[...].astype(bf16)
    sum_ref[0] = jnp.broadcast_to(
        jnp.sum(out_ref[...].astype(f32), axis=0, keepdims=True), (8, 384)
    )


def attend_forward(info, rand, qkv, first, pairs):
    length = qkv.shape[0]
    wide = pl.BlockSpec((length, 384), lambda p, *_: (0, p + first))
    slim = pl.BlockSpec((length, 128), lambda p, *_: (0, p))
    return pl.pallas_call(
        functools.partial(forward_kernel, nblocks=length // BLOCK, first=first, unroll=6),
        grid_spec=pltpu.PrefetchScalarGridSpec(
            num_scalar_prefetch=2, grid=(pairs,), in_specs=[wide], out_specs=[slim, slim]
        ),
        out_shape=[
            jax.ShapeDtypeStruct((length, pairs * 128), bf16),
            jax.ShapeDtypeStruct((length, pairs * 128), f32),
        ],
        compiler_params=pltpu.CompilerParams(vmem_limit_bytes=VMEM_BYTES),
        name="attend_forward",
    )(info, rand, qkv)


def attend_backward(info, rand, qkv, grad, ctx, lse, first, place_in, pairs):
    length = qkv.shape[0]
    wide = pl.BlockSpec((length, 384), lambda p, *_: (0, p + first))
    late = pl.BlockSpec((length, 128), lambda p, *_: (0, p + first))
    slim = pl.BlockSpec((length, 128), lambda p, *_: (0, p + place_in))
    return pl.pallas_call(
        functools.partial(backward_kernel, nblocks=length // BLOCK, first=first, unroll=6),
        grid_spec=pltpu.PrefetchScalarGridSpec(
            num_scalar_prefetch=2,
            grid=(pairs,),
            in_specs=[wide, late, slim, slim],
            out_specs=[
                pl.BlockSpec((length, 384), lambda p, *_: (0, p)),
                pl.BlockSpec((1, 8, 384), lambda p, *_: (p, 0, 0)),
            ],
            scratch_shapes=[pltpu.VMEM((length, 128), f32)] * 2,
        ),
        out_shape=[
            jax.ShapeDtypeStruct((length, pairs * 384), bf16),
            jax.ShapeDtypeStruct((pairs, 8, 384), f32),
        ],
        compiler_params=pltpu.CompilerParams(vmem_limit_bytes=VMEM_BYTES),
        name="attend_backward",
    )(info, rand, qkv, grad, ctx, lse)


def swap_dp(value, bit):
    size = lax.axis_size("dp")
    return lax.ppermute(value, "dp", [(i, i ^ bit) for i in range(size)])


def swap_seq(value, bit):
    size = lax.axis_size("seq")
    return lax.ppermute(value, "seq", [(i, i ^ bit) for i in range(size)])


def bits_of(size):
    return [size >> (k + 1) for k in range(size.bit_length() - 1)]


def gather_pieces(shard):
    held = [(0, shard)]
    for bit in bits_of(lax.axis_size("dp")):
        held = held + [(offset ^ bit, swap_dp(part, bit)) for offset, part in held]
    return [([offset], part[None]) for offset, part in held]


class Gather:
    def __init__(self, shard):
        self.offsets, self.held = [0], shard[None]
        self.bits = bits_of(lax.axis_size("dp"))
        self.start()

    def start(self):
        self.bit = self.bits.pop(0)
        self.moved = swap_dp(self.held, self.bit)

    def step(self, *tied):
        self.moved, *tied = lax.optimization_barrier((self.moved, *tied))
        self.held = jnp.concatenate([self.held, self.moved], axis=0)
        self.offsets = self.offsets + [offset ^ self.bit for offset in self.offsets]
        self.start()
        return tied

    def groups(self):
        return [(self.offsets, self.held), ([o ^ self.bit for o in self.offsets], self.moved)]


class Reduce:
    def __init__(self, parts, index):
        self.held, self.index = parts, index
        self.bits = bits_of(lax.axis_size("dp"))[::-1] + [0]
        self.moved = None

    def start(self):
        bit = self.bits.pop(0)
        if bit:
            view = self.held.reshape(-1, 2, *self.held.shape[1:])
            mine = (self.index // bit) % 2
            self.held = lax.dynamic_slice_in_dim(view, mine, 1, 1)[:, 0]
            self.moved = swap_dp(lax.dynamic_slice_in_dim(view, 1 - mine, 1, 1)[:, 0], bit)
        else:
            self.held = self.held[0]
            self.moved = swap_seq(self.held, 2)

    def step(self, *tied):
        if tied:
            self.moved, *tied = lax.optimization_barrier((self.moved, *tied))
        self.held = (self.held.astype(f32) + self.moved.astype(f32)).astype(bf16)
        if self.bits:
            self.start()
        return tied

    def rest(self):
        while self.bits:
            self.step()
        self.step()
        return self.held


def place_kernel(info_ref, *refs, plan, n_in):
    ins, outs = refs[:n_in], refs[n_in:]
    index, c = info_ref[4], info_ref[1]
    for source, slot, offset, rows, width, out, half in plan:
        first = pl.multiple_of((index ^ offset) * rows[1], 8)
        if half is None:
            columns = pl.ds(0, width)
        else:
            columns = pl.ds(pl.multiple_of((c ^ half) * width, 128), width)
        outs[out][pl.ds(first, rows[1]), columns] = ins[source][slot, rows[0] : rows[0] + rows[1]]


def place(info, arrays, plan, out_shapes):
    return pl.pallas_call(
        functools.partial(place_kernel, plan=plan, n_in=len(arrays)),
        grid_spec=pltpu.PrefetchScalarGridSpec(
            num_scalar_prefetch=1,
            grid=(1,),
            in_specs=[pl.BlockSpec(a.shape, lambda i, *_: (0, 0, 0)) for a in arrays],
            out_specs=[pl.BlockSpec(shape, lambda i, *_: (0, 0)) for shape in out_shapes],
        ),
        out_shape=[jax.ShapeDtypeStruct(shape, bf16) for shape in out_shapes],
        compiler_params=pltpu.CompilerParams(vmem_limit_bytes=VMEM_BYTES),
        name="place",
    )(info, *arrays)


def body(
    inputs,
    out_grad,
    w_qkv,
    w_attn_out,
    w_up,
    w_down,
    bias_qv,
    bias_out,
    bias_up,
    bias_down,
    norm_gain,
    norm_shift,
    rand_blocks,
):
    seq_count, local_len, width = inputs.shape
    dp = lax.axis_size("dp")
    index = lax.axis_index("dp")
    seat = lax.axis_index("seq")
    y, c = seat // 2, seat % 2
    heads_here = HEADS // 2
    half = width // 2
    hidden_width = w_up.shape[1]
    own = 2 * local_len
    pairs = heads_here // 2
    info = jnp.stack(
        [y, c, jnp.int32(heads_here), jnp.int32(0), index]
    ).astype(jnp.int32)
    rand = rand_blocks.reshape(-1)

    def pick(values, which):
        return lax.dynamic_index_in_dim(values, which, 0, keepdims=False)

    def column(value, which):
        return lax.dynamic_slice_in_dim(value, which * (value.shape[1] // 2), value.shape[1] // 2, 1)

    def by_core(mine, other, axis):
        return jnp.where(
            c == 0,
            jnp.concatenate([mine, other], axis=axis),
            jnp.concatenate([other, mine], axis=axis),
        )

    from_chip = swap_seq(pick(inputs, 1 - y), 2)
    own_tokens = jnp.concatenate([pick(inputs, y), from_chip], axis=0)
    tokens = jnp.concatenate([own_tokens, swap_seq(own_tokens, 1)], axis=0)

    shard = width // dp
    ff_shard = hidden_width // dp
    small = jnp.concatenate(
        [
            bias_qv.reshape(-1),
            bias_out,
            bias_up,
            bias_down,
            norm_gain.reshape(-1),
            norm_shift.reshape(-1),
        ]
    )
    small_width = small.shape[0]
    qkv_width = 3 * half
    small_row = jnp.pad(small[None], ((0, 7), (0, qkv_width - small_width)))
    by_pair = w_qkv.reshape(shard, 3, 2, pairs, 128)
    qkv_half = lax.dynamic_index_in_dim(by_pair, c, 2, keepdims=False)
    qkv_half = qkv_half.transpose(0, 2, 1, 3).reshape(shard, qkv_width)
    groups = gather_pieces(jnp.concatenate([qkv_half, small_row], axis=0))
    plan = []
    for source, (offsets, part) in enumerate(groups):
        for slot, offset in enumerate(offsets):
            plan.append((source, slot, offset, (0, shard), qkv_width, 0, None))
            plan.append((source, slot, offset, (shard, 8), qkv_width, 1, None))
    full_qkv, full_small = place(
        info, [part for _, part in groups], plan, [(width, qkv_width), (8 * dp, qkv_width)]
    )
    full_small = full_small.reshape(dp, 8, qkv_width)[:, 0].astype(f32)

    up_out = jnp.concatenate([column(w_up, c), column(w_attn_out, c)], axis=1)
    up_out = lax.all_gather(up_out, "dp", axis=0, tiled=True)

    def unpack(start, count, lead):
        part = full_small[:, start : start + count]
        if lead == 1:
            return part.reshape(-1)
        return part.reshape(dp, lead, -1).transpose(1, 0, 2).reshape(lead, -1)

    marks, total = [], 0
    for count in (2 * shard, shard, ff_shard, shard, 2 * shard, 2 * shard):
        marks.append((total, count))
        total += count
    full_bias_qv = unpack(*marks[0], 2)
    full_bias_out = unpack(*marks[1], 1)
    full_bias_up = unpack(*marks[2], 1)
    full_bias_down = unpack(*marks[3], 1)
    full_gain = unpack(*marks[4], 2)
    full_shift = unpack(*marks[5], 2)

    my_bias = lax.dynamic_slice_in_dim(full_bias_qv, c * half, half, 1).reshape(2, pairs, 128)
    my_bias = jnp.stack([my_bias[0], jnp.zeros_like(my_bias[0]), my_bias[1]], axis=1).reshape(-1)
    scale = jnp.tile(
        jnp.concatenate([jnp.full((128,), HEAD_DIM ** (-0.5), f32), jnp.ones((256,), f32)]), pairs
    )
    down_shard = column(w_down, c)
    down_shard, _ = lax.optimization_barrier((down_shard, groups[dp // 2 - 1][1]))
    down_gather = Gather(down_shard)
    while len(down_gather.bits) > 2:
        down_gather.step()
    qkv = ((dot(tokens, full_qkv) + my_bias) * scale).astype(bf16)
    (qkv,) = down_gather.step(qkv)
    ctx_a, lse_a = attend_forward(info, rand, qkv, 0, 1)
    qkv, ctx_a = down_gather.step(qkv, ctx_a)
    ctx_b, lse_b = attend_forward(info, rand, qkv, 1, pairs - 1)
    ctx = jnp.concatenate([ctx_a, ctx_b], axis=1)
    down_groups = down_gather.groups()
    arrays, plan = [], []
    for group_offsets, part in down_groups:
        for flip, array in enumerate((part, swap_seq(part, 1))):
            for slot, offset in enumerate(group_offsets):
                plan.append((len(arrays), slot, offset, (0, ff_shard), half, 0, flip))
            arrays.append(array)
    (full_down,) = place(info, arrays, plan, [(hidden_width, width)])
    up_other = swap_seq(up_out, 1)
    middle = hidden_width // 2
    full_up = by_core(up_out[:, :middle], up_other[:, :middle], 1)
    full_out = by_core(up_out[:, middle:], up_other[:, middle:], 1)
    ctx_rows = by_core(ctx[:own], swap_seq(ctx[own:], 1), 1)
    branch = dot(ctx_rows, full_out) + full_bias_out
    normed, first_pull = jax.vjp(
        layer_norm, own_tokens.astype(f32) + branch, full_gain[0], full_shift[0]
    )
    normed_low = normed.astype(bf16)
    hidden = dot(normed_low, full_up) + full_bias_up
    active, gelu_pull = jax.vjp(gelu_tanh, hidden)
    active_low = active.astype(bf16)
    ffn_out = dot(active_low, full_down) + full_bias_down
    result, second_pull = jax.vjp(layer_norm, normed + ffn_out, full_gain[1], full_shift[1])

    def send_home(rows):
        moved = swap_seq(rows[local_len:], 2)
        kept = rows[:local_len]
        return jnp.where(y == 0, jnp.stack([kept, moved]), jnp.stack([moved, kept]))

    output = send_home(result.astype(bf16))

    cotangent = jnp.concatenate(
        [pick(out_grad, y), swap_seq(pick(out_grad, 1 - y), 2)], axis=0
    ).astype(f32)
    pre_second_grad, second_gain_grad, second_shift_grad = second_pull(cotangent)
    ffn_grad = pre_second_grad.astype(bf16)
    down_grad = dot(active_low, ffn_grad, TN).astype(bf16)
    bias_down_grad = jnp.sum(ffn_grad.astype(f32), axis=0)
    active_grad = dot(ffn_grad, full_down, NT)
    (hidden_grad,) = gelu_pull(active_grad)
    hidden_low = hidden_grad.astype(bf16)
    up_grad = dot(normed_low, hidden_low, TN).astype(bf16)
    bias_up_grad = jnp.sum(hidden_low.astype(f32), axis=0)
    normed_grad = pre_second_grad + dot(hidden_low, full_up, NT)
    pre_first_grad, first_gain_grad, first_shift_grad = first_pull(normed_grad)
    branch_grad = pre_first_grad.astype(bf16)
    attn_out_grad = dot(ctx_rows, branch_grad, TN).astype(bf16)
    bias_out_grad = jnp.sum(branch_grad.astype(f32), axis=0)
    context_grad = dot(branch_grad, full_out, NT).astype(bf16)
    ctx_grad = jnp.concatenate(
        [column(context_grad, c), swap_seq(column(context_grad, 1 - c), 1)], axis=0
    )

    def core_sum(grad):
        other = swap_seq(column(grad, 1 - c), 1)
        return (column(grad, c).astype(f32) + other.astype(f32)).astype(bf16)

    down_sum = lax.psum_scatter(core_sum(down_grad), "dp", scatter_dimension=0, tiled=True)
    up_out_grad = jnp.concatenate([core_sum(up_grad), core_sum(attn_out_grad)], axis=1)
    up_reduce = Reduce(up_out_grad.reshape(dp, shard, middle + half), index)
    up_reduce.start()
    ctx_grad, _ = lax.optimization_barrier((ctx_grad, up_reduce.held))

    lse_of = [(ctx_a, lse_a, 0), (ctx_b, lse_b, 0), (ctx_b, lse_b, 1)]

    def backward(pair):
        ctx_part, lse_part, place_in = lse_of[pair]
        return attend_backward(info, rand, qkv, ctx_grad, ctx_part, lse_part, pair, place_in, 1)

    proj_0, sums_0 = backward(0)
    ctx_grad, proj_0 = lax.optimization_barrier((ctx_grad, proj_0))
    proj_1, sums_1 = backward(1)
    proj_0, proj_1, ctx_grad = up_reduce.step(proj_0, proj_1, ctx_grad)
    first_grad = jnp.concatenate([dot(tokens, proj, TN).astype(bf16) for proj in (proj_0, proj_1)], axis=1)
    first_reduce = Reduce(first_grad.reshape(dp, shard, 768), index)
    first_reduce.start()
    ctx_grad, _ = lax.optimization_barrier((ctx_grad, first_reduce.held))
    proj_2, sums_2 = backward(2)
    (proj_2,) = first_reduce.step(proj_2)
    (proj_2,) = up_reduce.step(proj_2)
    last_grad = dot(tokens, proj_2, TN).astype(bf16)
    sums = jnp.stack([part[0, 0] for part in (sums_0, sums_1, sums_2)]).reshape(pairs, 3, 128)
    my_sums = jnp.stack([sums[:, 0].reshape(-1), sums[:, 2].reshape(-1)])
    bias_qv_grad = lax.dynamic_update_slice(
        jnp.zeros((2, width), f32), my_sums, (jnp.int32(0), c * half)
    )

    def split(value):
        lead = 1 if value.ndim == 1 else value.shape[0]
        return value.reshape(lead, dp, -1).transpose(1, 0, 2).reshape(dp, -1)

    small_grads = jnp.concatenate(
        [
            split(bias_qv_grad),
            split(bias_out_grad),
            split(bias_up_grad),
            split(bias_down_grad),
            split(jnp.stack([first_gain_grad, second_gain_grad])),
            split(jnp.stack([first_shift_grad, second_shift_grad])),
        ],
        axis=1,
    ).astype(bf16)
    small_rows = -(-small_width // (8 * 384)) * 8
    small_grads = jnp.pad(small_grads, ((0, 0), (0, small_rows * 384 - small_width)))
    last_reduce = Reduce(
        jnp.concatenate(
            [last_grad.reshape(dp, shard, 384), small_grads.reshape(dp, small_rows, 384)], axis=1
        ),
        index,
    )
    last_reduce.start()

    def input_part(rows):
        parts = [
            dot(proj[rows], full_qkv[:, pair * 384 : (pair + 1) * 384], NT)
            for pair, proj in enumerate((proj_0, proj_1, proj_2))
        ]
        return parts[0] + parts[1] + parts[2]

    part_other = input_part(slice(own, 2 * own)).astype(bf16)
    input_grad = pre_first_grad + input_part(slice(0, own))
    input_grad = input_grad + swap_seq(part_other, 1).astype(f32)
    grad_inputs = send_home(input_grad.astype(bf16))

    up_shard = up_reduce.rest()
    first_shard = first_reduce.rest()
    last_shard = last_reduce.rest()
    down_shard = (down_sum.astype(f32) + swap_seq(down_sum, 2).astype(f32)).astype(bf16)

    def cores(mine):
        other = swap_seq(mine, 1)
        return jnp.where(c == 0, jnp.stack([mine, other]), jnp.stack([other, mine]))

    grad_down = by_core(down_shard, swap_seq(down_shard, 1), 1).astype(f32)
    both = cores(up_shard)
    grad_up = jnp.concatenate([both[0, :, :middle], both[1, :, :middle]], axis=1).astype(f32)
    grad_out = jnp.concatenate([both[0, :, middle:], both[1, :, middle:]], axis=1).astype(f32)
    both_first = cores(first_shard).astype(f32)
    both_last = cores(last_shard).astype(f32)
    both = jnp.concatenate([both_first, both_last[:, :shard]], axis=2)
    grad_qkv = (
        both.reshape(2, shard, pairs, 3, 128).transpose(1, 3, 0, 2, 4).reshape(shard, 3 * width)
    )
    sums = both_last[0, shard:].reshape(-1) + both_last[1, shard:].reshape(-1)

    def home(mark, lead):
        part = sums[mark[0] : mark[0] + mark[1]]
        return part if lead == 1 else part.reshape(lead, -1)

    return (
        output,
        grad_inputs,
        grad_qkv,
        grad_out,
        grad_up,
        grad_down,
        home(marks[0], 2),
        home(marks[1], 1),
        home(marks[2], 1),
        home(marks[3], 1),
        home(marks[4], 2),
        home(marks[5], 2),
    )


def solution(mesh):
    in_specs = (
        P("dp", "seq", None),
        P("dp", "seq", None),
        P("dp", None),
        P("dp", None),
        P("dp", None),
        P("dp", None),
        P(None, "dp"),
        P("dp"),
        P("dp"),
        P("dp"),
        P(None, "dp"),
        P(None, "dp"),
        P(),
    )
    out_specs = (
        P("dp", "seq", None),
        P("dp", "seq", None),
        P("dp", None),
        P("dp", None),
        P("dp", None),
        P("dp", None),
        P(None, "dp"),
        P("dp"),
        P("dp"),
        P("dp"),
        P(None, "dp"),
        P(None, "dp"),
    )
    return jax.shard_map(body, mesh=mesh, in_specs=in_specs, out_specs=out_specs, check_vma=False)
```

```python
import functools

import jax
import jax.numpy as jnp
from jax import lax
from jax.experimental import pallas as pl
from jax.experimental.pallas import tpu as pltpu
from jax.sharding import PartitionSpec as P

HEADS = 12
HEAD_DIM = 64
BLOCK = 64
RAND = 3

norm_eps = 1e-06
bf16 = jnp.bfloat16
f32 = jnp.float32
NN = (((1,), (0,)), ((), ()))
NT = (((1,), (1,)), ((), ()))
TN = (((0,), (0,)), ((), ()))
VMEM_BYTES = 56 << 20


def dot(a, b, dims=NN):
    return lax.dot_general(a, b, dims, preferred_element_type=f32)


def row_of(block, y, c, chunk_blocks):
    chunk = block // chunk_blocks
    place = (((chunk & 1) ^ c) << 1) | ((chunk >> 1) ^ y)
    return pl.multiple_of((place * chunk_blocks + block % chunk_blocks) * BLOCK, BLOCK)


class Rows:
    def __init__(self, info_ref, rand_ref, first_pair, nblocks):
        self.y, self.c = info_ref[0], info_ref[1]
        self.rand_ref = rand_ref
        self.nblocks = nblocks
        self.head = self.c * info_ref[2] + 2 * first_pair
        self.low = lax.broadcasted_iota(jnp.int32, (BLOCK, 128), 1) < HEAD_DIM
        self.low_row = lax.broadcasted_iota(jnp.int32, (1, 128), 1) < HEAD_DIM

    def at(self, block):
        return pl.ds(row_of(block, self.y, self.c, self.nblocks // 4), BLOCK)

    def two(self, tile):
        zero = jnp.zeros_like(tile)
        return jnp.concatenate(
            [jnp.where(self.low, tile, zero), jnp.where(self.low, zero, tile)], axis=0
        )

    def one(self, both):
        return jnp.where(self.low, both[:BLOCK], both[BLOCK:])

    def rand(self, i):
        middle = self.nblocks - 2
        base = (self.head * middle + (i - 1)) * RAND
        return [
            (self.rand_ref[base + t], self.rand_ref[base + middle * RAND + t]) for t in range(RAND)
        ]

    def near(self, load, ends, i, rand):
        mixed = [jnp.where(self.low, load(a), load(b)) for a, b in rand]
        return jnp.concatenate([ends, load(i - 1), load(i + 1), load(i)] + mixed, axis=0)

    def mask(self, scores, i):
        first = jnp.where(i == 1, -1e30, 0.0)
        last = jnp.where(i == self.nblocks - 2, -1e30, 0.0)
        bias = jnp.where(self.low_row, first, last).astype(f32)
        return jnp.concatenate(
            [scores[:, :128], scores[:, 128:256] + bias, scores[:, 256:]], axis=1
        )


def forward_kernel(info_ref, rand_ref, qkv_ref, *refs, nblocks, first, unroll):
    ctx_ref, lse_ref = refs[-2:]
    rows = Rows(info_ref, rand_ref, pl.program_id(0) + first, nblocks)

    def load(block, column):
        return qkv_ref[rows.at(block), column * 128 : (column + 1) * 128]

    def finish(block, scores, values):
        peak = jnp.max(scores, axis=1, keepdims=True)
        powers = jnp.exp(scores - peak)
        totals = jnp.sum(powers, axis=1, keepdims=True)
        context = dot(powers.astype(bf16), values) / totals
        lse = jnp.broadcast_to(peak + jnp.log(totals), context.shape)
        ctx_ref[rows.at(block), :] = rows.one(context).astype(bf16)
        lse_ref[rows.at(block), :] = rows.one(lse)

    for edge in (0, nblocks - 1):
        scores = dot(rows.two(load(edge, 0)), qkv_ref[:, 128:256], NT)
        finish(edge, scores, qkv_ref[:, 256:384])
    key_ends = jnp.concatenate([load(0, 1), load(nblocks - 1, 1)], axis=0)
    value_ends = jnp.concatenate([load(0, 2), load(nblocks - 1, 2)], axis=0)

    def row(i):
        rand = rows.rand(i)
        keys = rows.near(lambda b: load(b, 1), key_ends, i, rand)
        values = rows.near(lambda b: load(b, 2), value_ends, i, rand)
        finish(i, rows.mask(dot(rows.two(load(i, 0)), keys, NT), i), values)

    def step(t, carry):
        for u in range(unroll):
            row(1 + t * unroll + u)
        return carry

    lax.fori_loop(0, (nblocks - 2) // unroll, step, 0)


def backward_kernel(
    info_ref, rand_ref, qkv_ref, own_ref, other_ref, ctx_ref, lse_ref, out_ref, sum_ref,
    key_sum, value_sum, grad_ref,
    *, nblocks, first, unroll
):
    rows = Rows(info_ref, rand_ref, pl.program_id(0) + first, nblocks)
    zero = jnp.zeros((BLOCK, 128), f32)
    half_rows = own_ref.shape[0]
    grad_ref[:half_rows] = own_ref[...]
    grad_ref[half_rows:] = other_ref[...]

    def load(block, column):
        return qkv_ref[rows.at(block), column * 128 : (column + 1) * 128]

    def finish(block, scores, keys, values):
        grad = grad_ref[rows.at(block), :]
        both = grad.astype(f32) * ctx_ref[rows.at(block), :].astype(f32)
        row_dot = jnp.concatenate(
            [
                jnp.sum(jnp.where(rows.low, both, zero), axis=1, keepdims=True),
                jnp.sum(jnp.where(rows.low, zero, both), axis=1, keepdims=True),
            ],
            axis=0,
        )
        lse = lse_ref[rows.at(block), :]
        lse = jnp.concatenate([lse[:, 0:1], lse[:, HEAD_DIM : HEAD_DIM + 1]], axis=0)
        grad = rows.two(grad)
        attention = jnp.exp(scores - lse)
        attn_grad = dot(grad, values, NT)
        score_grad = (attention * (attn_grad - row_dot)).astype(bf16)
        query_grad = dot(score_grad, keys) * HEAD_DIM ** (-0.5)
        out_ref[rows.at(block), 0:128] = rows.one(query_grad).astype(bf16)
        return grad, attention.astype(bf16), score_grad

    for edge in (0, nblocks - 1):
        query = rows.two(load(edge, 0))
        keys, values = qkv_ref[:, 128:256], qkv_ref[:, 256:384]
        grad, attention, score_grad = finish(edge, dot(query, keys, NT), keys, values)
        if edge == 0:
            key_sum[...] = dot(score_grad, query, TN)
            value_sum[...] = dot(attention, grad, TN)
        else:
            key_sum[...] += dot(score_grad, query, TN)
            value_sum[...] += dot(attention, grad, TN)
    key_ends = jnp.concatenate([load(0, 1), load(nblocks - 1, 1)], axis=0)
    value_ends = jnp.concatenate([load(0, 2), load(nblocks - 1, 2)], axis=0)

    def row(i):
        rand = rows.rand(i)
        keys = rows.near(lambda b: load(b, 1), key_ends, i, rand)
        values = rows.near(lambda b: load(b, 2), value_ends, i, rand)
        query = rows.two(load(i, 0))
        scores = rows.mask(dot(query, keys, NT), i)
        grad, attention, score_grad = finish(i, scores, keys, values)
        for total, part in (
            (key_sum, dot(score_grad, query, TN)),
            (value_sum, dot(attention, grad, TN)),
        ):
            for slot, block in enumerate((0, nblocks - 1, i - 1, i + 1, i)):
                total[rows.at(block), :] += part[slot * BLOCK : (slot + 1) * BLOCK]
            for slot, (a, b) in enumerate(rand):
                tile = part[(5 + slot) * BLOCK : (6 + slot) * BLOCK]
                total[rows.at(a), :] += jnp.where(rows.low, tile, zero)
                total[rows.at(b), :] += jnp.where(rows.low, zero, tile)

    def step(t, carry):
        for u in range(unroll):
            row(1 + t * unroll + u)
        return carry

    lax.fori_loop(0, (nblocks - 2) // unroll, step, 0)
    out_ref[:, 128:256] = key_sum[...].astype(bf16)
    out_ref[:, 256:384] = value_sum[...].astype(bf16)
    sum_ref[0] = jnp.broadcast_to(
        jnp.sum(out_ref[...].astype(f32), axis=0, keepdims=True), (8, 384)
    )


def attend_forward(info, rand, qkv, first, pairs, total, into=()):
    length = qkv.shape[0]
    wide = pl.BlockSpec((length, 384), lambda p, *_: (0, p + first))
    slim = pl.BlockSpec((length, 128), lambda p, *_: (0, p + first))
    return pl.pallas_call(
        functools.partial(forward_kernel, nblocks=length // BLOCK, first=first, unroll=6),
        grid_spec=pltpu.PrefetchScalarGridSpec(
            num_scalar_prefetch=2,
            grid=(pairs,),
            in_specs=[wide] + [pl.BlockSpec(memory_space=pl.ANY)] * len(into),
            out_specs=[slim, slim],
        ),
        out_shape=[
            jax.ShapeDtypeStruct((length, total * 128), bf16),
            jax.ShapeDtypeStruct((length, total * 128), f32),
        ],
        input_output_aliases={3 + k: k for k in range(len(into))},
        compiler_params=pltpu.CompilerParams(vmem_limit_bytes=VMEM_BYTES),
        name="attend_forward",
    )(info, rand, qkv, *into)


def attend_backward(info, rand, qkv, own_grad, other_grad, ctx, lse, first, pairs):
    length = qkv.shape[0]
    wide = pl.BlockSpec((length, 384), lambda p, *_: (0, p + first))
    slim = pl.BlockSpec((length, 128), lambda p, *_: (0, p + first))
    part = pl.BlockSpec((length // 2, 128), lambda p, *_: (0, p + first))
    return pl.pallas_call(
        functools.partial(backward_kernel, nblocks=length // BLOCK, first=first, unroll=6),
        grid_spec=pltpu.PrefetchScalarGridSpec(
            num_scalar_prefetch=2,
            grid=(pairs,),
            in_specs=[wide, part, part, slim, slim],
            out_specs=[
                pl.BlockSpec((length, 384), lambda p, *_: (0, p)),
                pl.BlockSpec((1, 8, 384), lambda p, *_: (p, 0, 0)),
            ],
            scratch_shapes=[pltpu.VMEM((length, 128), f32)] * 2 + [pltpu.VMEM((length, 128), bf16)],
        ),
        out_shape=[
            jax.ShapeDtypeStruct((length, pairs * 384), bf16),
            jax.ShapeDtypeStruct((pairs, 8, 384), f32),
        ],
        compiler_params=pltpu.CompilerParams(vmem_limit_bytes=VMEM_BYTES),
        name="attend_backward",
    )(info, rand, qkv, own_grad, other_grad, ctx, lse)


def swap_dp(value, bit):
    size = lax.axis_size("dp")
    return lax.ppermute(value, "dp", [(i, i ^ bit) for i in range(size)])


def swap_seq(value, bit):
    size = lax.axis_size("seq")
    return lax.ppermute(value, "seq", [(i, i ^ bit) for i in range(size)])


def bits_of(size):
    return [size >> (k + 1) for k in range(size.bit_length() - 1)]


class Gather:
    def __init__(self, shard):
        self.offsets, self.held = [0], shard[None]
        self.bits = bits_of(lax.axis_size("dp")) + [0]
        self.start()

    def start(self):
        self.bit = self.bits.pop(0)
        self.moved = swap_dp(self.held, self.bit) if self.bit else swap_seq(self.held, 2)

    def step(self, *tied):
        self.moved, *tied = lax.optimization_barrier((self.moved, *tied))
        self.held = jnp.concatenate([self.held, self.moved], axis=0)
        self.offsets = self.offsets + [offset ^ self.bit for offset in self.offsets]
        self.start()
        return tied


class Reduce:
    def __init__(self, parts, index, y):
        count, rows, columns = parts.shape
        self.held, self.index, self.y = parts.reshape(count, 2, rows // 2, columns), index, y
        self.bits = [0] + bits_of(lax.axis_size("dp"))[::-1]

    def start(self):
        bit = self.bits.pop(0)
        if bit:
            view = self.held.reshape(-1, 2, *self.held.shape[1:])
            mine = (self.index // bit) % 2
        else:
            view, mine = self.held, self.y
        self.held = lax.dynamic_slice_in_dim(view, mine, 1, 1)[:, 0]
        give = lax.dynamic_slice_in_dim(view, 1 - mine, 1, 1)[:, 0]
        self.moved = swap_dp(give, bit) if bit else swap_seq(give, 2)

    def add(self):
        self.held = (self.held.astype(f32) + self.moved.astype(f32)).astype(bf16)

    def step(self):
        self.add()
        if self.bits:
            self.start()
        else:
            self.held = self.held[0]
            self.moved = swap_seq(self.held, 2)

    def join(self):
        first = jnp.where(self.y == 0, self.held, self.moved)
        second = jnp.where(self.y == 0, self.moved, self.held)
        return jnp.concatenate([first, second], axis=0)


def prepare_kernel(info_ref, w_ref, qv_ref, gain_ref, shift_ref, out_ref, down_ref, up_ref, shard_ref):
    c = info_ref[1]
    third = w_ref.shape[1] // 3
    half = third // 2
    depth, few = qv_ref.shape[1], up_ref.shape[1]
    for kind in range(3):
        columns = pl.ds(pl.multiple_of(kind * third + c * half, 128), half)
        part = w_ref[:, columns]
        for pair in range(half // 128):
            at = (pair * 3 + kind) * 128
            shard_ref[0:depth, at : at + 128] = part[:, pair * 128 : (pair + 1) * 128]
    shard_ref[depth:] = jnp.zeros((8, 3 * half), bf16)
    shard_ref[depth : depth + 2, 0:depth] = qv_ref[...]
    shard_ref[depth + 2 : depth + 4, 0:depth] = gain_ref[...]
    shard_ref[depth + 4 : depth + 6, 0:depth] = shift_ref[...]
    shard_ref[depth + 6 : depth + 7, 0:depth] = out_ref[...]
    shard_ref[depth + 7 : depth + 8, 0:depth] = down_ref[...]
    shard_ref[depth : depth + 1, 128 : 128 + few] = up_ref[...]


def prepare(info, w_qkv, *small):
    depth, columns = w_qkv.shape
    arrays = (w_qkv, *small)
    return pl.pallas_call(
        prepare_kernel,
        grid_spec=pltpu.PrefetchScalarGridSpec(
            num_scalar_prefetch=1,
            grid=(1,),
            in_specs=[pl.BlockSpec(a.shape, lambda i, *_: (0, 0)) for a in arrays],
            out_specs=pl.BlockSpec((depth + 8, columns // 2), lambda i, *_: (0, 0)),
        ),
        out_shape=jax.ShapeDtypeStruct((depth + 8, columns // 2), bf16),
        compiler_params=pltpu.CompilerParams(vmem_limit_bytes=VMEM_BYTES),
        name="prepare",
    )(info, *arrays)


def project_kernel(info_ref, inputs_ref, *refs, offsets, shard, ff_shard):
    more, refs = refs[:3], refs[3:]
    pieces, refs = refs[: len(offsets)], refs[len(offsets) :]
    qkv_ref, tokens_ref, weight_ref, norms_ref, up_ref, bias_ref = refs
    step = pl.program_id(0)
    width = weight_ref.shape[0]
    half = width // 2

    def spread(part, size, target, at):
        shape = (part.shape[1], target)
        lane = lax.broadcasted_iota(jnp.int32, shape, 1) - at
        source = lax.broadcasted_iota(jnp.int32, shape, 0)
        return dot(part, jnp.where((lane == source) & (source < size), 1.0, 0.0).astype(bf16))

    @pl.when(step == 0)
    def _():
        norms = jnp.zeros((8, width), f32)
        for offset, piece in zip(offsets, pieces):
            place = info_ref[4] ^ offset
            at = pl.ds(pl.multiple_of(place * shard, 8), shard)
            weight_ref[at, :] = piece[0:shard]
            tail = piece[shard : shard + 8]
            norms = norms + spread(tail[:, :128], shard, width, place * shard)
            if ff_shard % 128 == 0:
                lanes = pl.ds(pl.multiple_of(place * ff_shard, 128), ff_shard)
                up_ref[:, lanes] = tail[:, 128 : 128 + ff_shard].astype(f32)
            else:
                part = spread(tail[:, 128:256], ff_shard, up_ref.shape[1], place * ff_shard)
                if offset == offsets[0]:
                    up_ref[...] = part
                else:
                    up_ref[...] += part
        norms_ref[...] = norms
        bias_ref[...] = jnp.zeros_like(bias_ref)
        for pair in range(half // 128):
            lanes = pl.ds(pl.multiple_of(info_ref[1] * half + pair * 128, 128), 128)
            bias_ref[0:1, pair * 384 : pair * 384 + 128] = norms_ref[0:1, lanes]
            bias_ref[0:1, pair * 384 + 256 : pair * 384 + 384] = norms_ref[1:2, lanes]
        tokens_ref[...] = inputs_ref[0]

    for k in range(3):

        @pl.when(step == k + 1)
        def _():
            tokens_ref[...] = more[k][...]

    wide = dot(tokens_ref[...], weight_ref[...]) + bias_ref[0:1]
    for pair in range(wide.shape[1] // 384):
        at = pair * 384
        query = wide[:, at : at + 128].astype(bf16).astype(f32) * HEAD_DIM ** (-0.5)
        qkv_ref[:, at : at + 128] = query.astype(bf16)
        qkv_ref[:, at + 128 : at + 384] = wide[:, at + 128 : at + 384].astype(bf16)


def project(info, inputs, more, pieces, offsets, shard, ff_shard):
    _, local_len, width = inputs.shape
    columns = pieces[0].shape[1]
    hidden = ff_shard * len(pieces)

    def whole(array):
        return pl.BlockSpec(array.shape, lambda i, *_: (0, 0), pipeline_mode=pl.Buffered(1))

    fixed = [((width, columns), bf16), ((8, width), f32), ((8, hidden), f32)]
    return pl.pallas_call(
        functools.partial(project_kernel, offsets=offsets, shard=shard, ff_shard=ff_shard),
        grid_spec=pltpu.PrefetchScalarGridSpec(
            num_scalar_prefetch=1,
            grid=(4,),
            in_specs=[pl.BlockSpec((1, local_len, width), lambda i, info: (info[0], 0, 0))]
            + [whole(array) for array in (*more, *pieces)],
            out_specs=[
                pl.BlockSpec((local_len, columns), lambda i, *_: (i, 0)),
                pl.BlockSpec((local_len, width), lambda i, *_: (i, 0)),
            ]
            + [pl.BlockSpec(shape, lambda i, *_: (0, 0)) for shape, _ in fixed],
            scratch_shapes=[pltpu.VMEM((8, columns), f32)],
        ),
        out_shape=[
            jax.ShapeDtypeStruct((4 * local_len, columns), bf16),
            jax.ShapeDtypeStruct((4 * local_len, width), bf16),
        ]
        + [jax.ShapeDtypeStruct(shape, kind) for shape, kind in fixed],
        compiler_params=pltpu.CompilerParams(vmem_limit_bytes=VMEM_BYTES),
        name="project",
    )(info, inputs, *more, *pieces)


CHUNK = 512


def gelu_pair(values):
    inner = 0.7978845608028654 * (values + 0.044715 * values * values * values)
    bend = jnp.tanh(inner)
    slope = 0.7978845608028654 * (1.0 + 3.0 * 0.044715 * values * values)
    active = 0.5 * values * (1.0 + bend)
    change = 0.5 * (1.0 + bend) + 0.5 * values * (1.0 - bend * bend) * slope
    return active, change


def norm_parts(values):
    center = values - jnp.mean(values, axis=-1, keepdims=True)
    spread = jnp.mean(center * center, axis=-1, keepdims=True)
    inverse = lax.rsqrt(spread + norm_eps)
    return center * inverse, inverse


def norm_back(grad, unit, inverse, gain):
    scaled = grad * gain
    return inverse * (
        scaled
        - jnp.mean(scaled, axis=-1, keepdims=True)
        - unit * jnp.mean(scaled * unit, axis=-1, keepdims=True)
    )


def middle_kernel(
    info_ref,
    tokens_ref,
    ctx_ref,
    ctx_other_ref,
    cotangent_ref,
    up_ref,
    up_other_ref,
    *refs,
    down_plan,
    steps,
):
    n_down = 1 + max(entry[0] for entry in down_plan)
    down_refs, refs = refs[:n_down], refs[n_down:]
    (
        norm_ref,
        bias_up_ref,
        keep_ref,
        send_ref,
        ctx_all_ref,
        normed_ref,
        active_ref,
        hidden_mine_ref,
        hidden_other_ref,
        ffn_mine_ref,
        ffn_other_ref,
        first_ref,
        branch_mine_ref,
        branch_other_ref,
        ctx_grad_ref,
        ctx_send_ref,
        sums_ref,
        up_sums_ref,
        up_all,
        down_all,
        out_all,
        change_all,
        wide,
    ) = refs
    c, index, flip = info_ref[1], info_ref[4], info_ref[5]
    step = pl.program_id(0)
    half = ctx_ref.shape[1]
    middle = up_ref.shape[1] - half
    hidden = 2 * middle

    def lanes(which, size):
        return pl.ds(pl.multiple_of(which * size, 128), size)

    def rows(which, size):
        return pl.ds(pl.multiple_of(which * size, 16), size)

    @pl.when(step == 0)
    def _():
        up_all[:, :middle] = up_ref[:, :middle]
        up_all[:, middle:] = up_other_ref[:, :middle]
        out_all[:, lanes(c, half)] = up_ref[:, middle:]
        out_all[:, lanes(1 - c, half)] = up_other_ref[:, middle:]
        for source, slot, offset, which in down_plan:
            size = down_refs[source].shape[1]
            block = (index ^ offset ^ flip) * 2 + (info_ref[0] ^ (which // 2))
            down_all[rows(block, size), lanes(c ^ (which % 2), half)] = down_refs[source][slot]
        sums_ref[...] = jnp.zeros_like(sums_ref)
        up_sums_ref[...] = jnp.zeros_like(up_sums_ref)

    bias_out, bias_down = norm_ref[6:7], norm_ref[7:8]
    gain_1, gain_2, shift_1, shift_2 = (norm_ref[k : k + 1] for k in (2, 3, 4, 5))
    ctx_all_ref[:, lanes(c, half)] = ctx_ref[...]
    ctx_all_ref[:, lanes(1 - c, half)] = ctx_other_ref[...]
    branch = dot(ctx_all_ref[...], out_all[...]) + bias_out
    unit_1, inverse_1 = norm_parts(tokens_ref[...].astype(f32) + branch)
    normed = unit_1 * gain_1 + shift_1
    normed_low = normed.astype(bf16)
    normed_ref[...] = normed_low

    total = jnp.zeros_like(branch)
    for k in range(hidden // CHUNK):
        part = slice(k * CHUNK, (k + 1) * CHUNK)
        which = c ^ (k * CHUNK // middle)
        inside = k * CHUNK % middle
        at = pl.ds(pl.multiple_of(which * middle + inside, 128), CHUNK)
        bias = bias_up_ref[0:1, at]
        active, change = gelu_pair(dot(normed_low, up_all[:, part]) + bias)
        active = active.astype(bf16)
        active_ref[:, at] = active
        change_all[:, part] = change
        total = total + dot(active, down_all[part])

    unit_2, inverse_2 = norm_parts(normed + total + bias_down)
    result = (unit_2 * gain_2 + shift_2).astype(bf16)

    @pl.when(step < steps // 2)
    def _():
        keep_ref[0] = result

    @pl.when(step >= steps // 2)
    def _():
        send_ref[...] = result


    cotangent = cotangent_ref[...].astype(f32)
    pre_second = norm_back(cotangent, unit_2, inverse_2, gain_2)
    ffn_grad = pre_second.astype(bf16)
    wide[...] = ffn_grad
    ffn_mine_ref[...] = wide[:, lanes(c, half)]
    ffn_other_ref[...] = wide[:, lanes(1 - c, half)]

    def add(row, values):
        sums_ref[row : row + 1] += jnp.sum(values, axis=0, keepdims=True)

    add(1, ffn_grad.astype(f32))
    add(3, cotangent * unit_2)
    add(5, cotangent)

    total = jnp.zeros_like(branch)
    for k in range(hidden // CHUNK):
        part = slice(k * CHUNK, (k + 1) * CHUNK)
        grad = (dot(ffn_grad, down_all[part], NT) * change_all[:, part]).astype(bf16)
        target = hidden_mine_ref if k * CHUNK < middle else hidden_other_ref
        inside = k * CHUNK % middle
        target[:, inside : inside + CHUNK] = grad
        which = c ^ (k * CHUNK // middle)
        at = pl.ds(pl.multiple_of(which * middle + inside, 128), CHUNK)
        up_sums_ref[0:1, at] += jnp.sum(grad.astype(f32), axis=0, keepdims=True)
        total = total + dot(grad, up_all[:, part], NT)

    normed_grad = pre_second + total
    pre_first = norm_back(normed_grad, unit_1, inverse_1, gain_1)
    first_ref[...] = pre_first
    branch_grad = pre_first.astype(bf16)
    wide[...] = branch_grad
    branch_mine_ref[...] = wide[:, lanes(c, half)]
    branch_other_ref[...] = wide[:, lanes(1 - c, half)]
    add(0, branch_grad.astype(f32))
    add(2, normed_grad * unit_1)
    add(4, normed_grad)
    ctx_grad = dot(branch_grad, out_all[...], NT).astype(bf16)
    wide[...] = ctx_grad
    ctx_grad_ref[...] = wide[:, lanes(c, half)]
    ctx_send_ref[...] = wide[:, lanes(1 - c, half)]


def feed_forward(info, tokens, ctx, ctx_other, cotangent, up, up_other, down_groups, norms, bias_up):
    count, width = cotangent.shape
    half = ctx.shape[1]
    middle = up.shape[1] - half
    hidden = 2 * middle
    tile = 256
    steps = count // tile
    arrays, plan = [], []
    for offsets, which, array in down_groups:
        for slot, offset in enumerate(offsets):
            plan.append((len(arrays), slot, offset, which))
        arrays.append(array)

    def tiled(columns):
        return pl.BlockSpec((tile, columns), lambda i, *_: (i, 0))

    def whole(array):
        rank = len(array.shape)
        return pl.BlockSpec(
            array.shape, lambda i, *_: (0,) * rank, pipeline_mode=pl.Buffered(1)
        )

    outs = [
        ((count, width), bf16),
        ((count, width), bf16),
        ((count, hidden), bf16),
        ((count, middle), bf16),
        ((count, middle), bf16),
        ((count, half), bf16),
        ((count, half), bf16),
        ((count, width), f32),
        ((count, half), bf16),
        ((count, half), bf16),
        ((count, half), bf16),
        ((count, half), bf16),
    ]
    sums = [((8, width), f32), ((8, hidden), f32)]
    return pl.pallas_call(
        functools.partial(middle_kernel, down_plan=plan, steps=steps),
        grid_spec=pltpu.PrefetchScalarGridSpec(
            num_scalar_prefetch=1,
            grid=(steps,),
            in_specs=[tiled(width), tiled(half), tiled(half), tiled(width), whole(up), whole(up_other)]
            + [whole(array) for array in arrays]
            + [whole(norms), whole(bias_up)],
            out_specs=[
                pl.BlockSpec(
                    (1, tile, width), lambda i, info: (info[0], jnp.minimum(i, steps // 2 - 1), 0)
                ),
                pl.BlockSpec((tile, width), lambda i, *_: (jnp.maximum(i - steps // 2, 0), 0)),
            ]
            + [tiled(shape[1]) for shape, _ in outs]
            + [pl.BlockSpec(shape, lambda i, *_: (0, 0)) for shape, _ in sums],
            scratch_shapes=[
                pltpu.VMEM((width, hidden), bf16),
                pltpu.VMEM((hidden, width), bf16),
                pltpu.VMEM((width, width), bf16),
                pltpu.VMEM((tile, hidden), f32),
                pltpu.VMEM((tile, width), bf16),
            ],
        ),
        out_shape=[jax.ShapeDtypeStruct((2, count // 2, width), bf16)]
        + [jax.ShapeDtypeStruct((count // 2, width), bf16)]
        + [jax.ShapeDtypeStruct(shape, kind) for shape, kind in outs + sums],
        compiler_params=pltpu.CompilerParams(vmem_limit_bytes=VMEM_BYTES),
        name="feed_forward",
    )(info, tokens, ctx, ctx_other, cotangent, up, up_other, *arrays, norms, bias_up)


def home_kernel(info_ref, *refs):
    refs[-1][0] = refs[0][...]


def home_rows(info, rows, which, into=()):
    return pl.pallas_call(
        home_kernel,
        grid_spec=pltpu.PrefetchScalarGridSpec(
            num_scalar_prefetch=1,
            grid=(1,),
            in_specs=[pl.BlockSpec(rows.shape, lambda i, *_: (0, 0))]
            + [pl.BlockSpec(memory_space=pl.ANY)] * len(into),
            out_specs=pl.BlockSpec((1, *rows.shape), lambda i, info: (info[0] ^ which, 0, 0)),
        ),
        out_shape=jax.ShapeDtypeStruct((2, *rows.shape), bf16),
        input_output_aliases={2: 0} if into else {},
        name="home_rows",
    )(info, rows, *into)


def widen_kernel(info_ref, *refs, plan, n_in):
    ins, outs = refs[:n_in], refs[n_in:]
    c = info_ref[1]
    for source, row, rows, column, width, out, base, stride, which in plan:
        at = pl.ds(pl.multiple_of(base + (c ^ which) * stride, 128), width)
        outs[out][:, at] = ins[source][row : row + rows, column : column + width].astype(f32)


def widen(info, arrays, plan, shapes):
    return pl.pallas_call(
        functools.partial(widen_kernel, plan=plan, n_in=len(arrays)),
        grid_spec=pltpu.PrefetchScalarGridSpec(
            num_scalar_prefetch=1,
            grid=(1,),
            in_specs=[pl.BlockSpec(a.shape, lambda i, *_: (0, 0)) for a in arrays],
            out_specs=[pl.BlockSpec(shape, lambda i, *_: (0, 0)) for shape in shapes],
        ),
        out_shape=[jax.ShapeDtypeStruct(shape, f32) for shape in shapes],
        compiler_params=pltpu.CompilerParams(vmem_limit_bytes=VMEM_BYTES),
        name="widen",
    )(info, *arrays)


def body(
    inputs,
    out_grad,
    w_qkv,
    w_attn_out,
    w_up,
    w_down,
    bias_qv,
    bias_out,
    bias_up,
    bias_down,
    norm_gain,
    norm_shift,
    rand_blocks,
):
    _, local_len, width = inputs.shape
    dp = lax.axis_size("dp")
    index = lax.axis_index("dp")
    seat = lax.axis_index("seq")
    y, c = seat // 2, seat % 2
    heads_here = HEADS // 2
    pairs = heads_here // 2
    half = width // 2
    hidden_width = w_up.shape[1]
    middle = hidden_width // 2
    own = 2 * local_len
    shard = width // dp
    ff_shard = hidden_width // dp
    qkv_width = 3 * half
    flip = c * (dp // 2)
    info = jnp.stack([y, c, jnp.int32(heads_here), jnp.int32(0), index, flip]).astype(jnp.int32)
    rand = rand_blocks.reshape(-1)

    def pick(values, which):
        return lax.dynamic_index_in_dim(values, which, 0, keepdims=False)

    def column(value, which):
        return lax.dynamic_slice_in_dim(value, which * (value.shape[1] // 2), value.shape[1] // 2, 1)

    tie = lax.optimization_barrier

    given = pick(inputs, 1 - y)
    qkv_shard = prepare(
        info, w_qkv, bias_qv, norm_gain, norm_shift, bias_out[None], bias_down[None], bias_up[None]
    )
    bits = bits_of(dp)
    cut = local_len // 2
    chip_a = swap_seq(given[:cut], 2)
    mine = pick(inputs, y)
    first_moves = [swap_dp(qkv_shard, bit) for bit in bits]
    chip_a, rest, *first_moves = tie((chip_a, given[cut:], *first_moves))
    chip_b = swap_seq(rest, 2)
    other_mine = swap_seq(mine, 1)
    held = [(0, qkv_shard), (bits[0], first_moves[0])]
    for k, bit in enumerate(bits[1:]):
        later = [(o ^ bit, swap_dp(part, bit)) for o, part in held[1:]]
        held = held + [(bit, first_moves[k + 1])] + later
        if k == 0:
            offsets = [offset for offset, _ in held]
            chip_b, other_mine, down_shard, up_out, *parts = tie(
                (
                    chip_b,
                    other_mine,
                    lax.dynamic_slice(
                        w_down, (y * (ff_shard // 2), c * half), (ff_shard // 2, half)
                    ),
                    jnp.concatenate([column(w_up, c), column(w_attn_out, c)], axis=1),
                    *[part for _, part in held],
                )
            )
            held = list(zip(offsets, parts))
    from_chip = jnp.concatenate([chip_a, chip_b], axis=0)
    other_chip = swap_seq(from_chip, 1)
    offsets = [offset for offset, _ in held]
    pieces = [part for _, part in held]
    up_out = lax.all_gather(up_out, "dp", axis=0, tiled=True)
    down_gather = Gather(down_shard)
    while len(down_gather.bits) > 2:
        down_gather.step()

    marks, total = [], 0
    for count in (2 * shard, shard, ff_shard, shard, 2 * shard, 2 * shard):
        marks.append((total, count))
        total += count
    small_width = total
    cotangent_chip = swap_seq(pick(out_grad, 1 - y), 2)
    qkv, tokens, full_qkv, norms, bias_up_row = project(
        info, inputs, (from_chip, other_mine, other_chip), pieces, offsets, shard, ff_shard
    )
    (qkv,) = down_gather.step(qkv)
    ctx, lse = attend_forward(info, rand, qkv, 0, 1, pairs)
    qkv, ctx, lse, up_out, cotangent_chip = down_gather.step(
        qkv, ctx, lse, up_out, cotangent_chip
    )
    up_other = swap_seq(up_out, 1)
    held = down_gather.held
    held_other = swap_seq(held, 1)
    ctx, lse = attend_forward(info, rand, qkv, 1, pairs - 1, pairs, (ctx, lse))
    ctx, lse, moved, held_other, up_other = tie((ctx, lse, down_gather.moved, held_other, up_other))
    ctx_other = swap_seq(ctx[own:], 1)
    down_groups = [
        (down_gather.offsets, which, part)
        for which, part in enumerate((held, held_other, moved, swap_seq(moved, 1)))
    ]
    cotangent = jnp.concatenate([pick(out_grad, y), cotangent_chip], axis=0)
    (
        out_keep,
        out_send,
        ctx_all,
        normed,
        active,
        hidden_mine,
        hidden_other,
        ffn_mine,
        ffn_other,
        pre_first,
        branch_mine,
        branch_other,
        ctx_grad,
        ctx_send,
        sums,
        up_sums,
    ) = feed_forward(
        info, tokens, ctx, ctx_other, cotangent, up_out, up_other, down_groups, norms, bias_up_row
    )
    ctx_other_grad = swap_seq(ctx_send, 1)

    def grad_of(left, right):
        return dot(left, right, TN)

    up_give = swap_seq(grad_of(normed, hidden_other).astype(bf16), 1)
    down_give = swap_seq(grad_of(active, ffn_other).astype(bf16), 1)
    out_give = swap_seq(grad_of(ctx_all, branch_other).astype(bf16), 1)
    up_grad = (grad_of(normed, hidden_mine) + up_give.astype(f32)).astype(bf16)
    up_sum = lax.psum_scatter(up_grad, "dp", scatter_dimension=0, tiled=True)
    down_grad = (grad_of(active, ffn_mine) + down_give.astype(f32)).astype(bf16)
    out_weight_grad = (grad_of(ctx_all, branch_mine) + out_give.astype(f32)).astype(bf16)
    down_reduce = Reduce(
        jnp.concatenate(
            [down_grad.reshape(dp, ff_shard, half), out_weight_grad.reshape(dp, shard, half)],
            axis=1,
        ),
        index,
        y,
    )
    down_reduce.start()
    ctx_grad, ctx_other_grad, _ = tie((ctx_grad, ctx_other_grad, down_reduce.held))

    proj_a, proj_sums_a = attend_backward(
        info, rand, qkv, ctx_grad, ctx_other_grad, ctx, lse, 0, pairs - 1
    )
    proj_a, ctx_grad, down_reduce.moved = tie((proj_a, ctx_grad, down_reduce.moved))
    down_reduce.step()
    out_home = swap_seq(out_send, 2)
    wide_a = 384 * (pairs - 1)
    grad_a = grad_of(tokens, proj_a).astype(bf16)
    reduce_a = Reduce(grad_a.reshape(dp, shard, wide_a), index, y)
    reduce_a.start()
    weight_a, weight_b = full_qkv[:, :wide_a], full_qkv[:, wide_a:]
    input_a = dot(proj_a, weight_a, NT)
    ctx_grad, input_a, _ = tie((ctx_grad, input_a, reduce_a.held))
    proj_b, proj_sums_b = attend_backward(
        info, rand, qkv, ctx_grad, ctx_other_grad, ctx, lse, pairs - 1, 1
    )
    proj_b, reduce_a.moved, down_reduce.moved, out_home = tie(
        (proj_b, reduce_a.moved, down_reduce.moved, out_home)
    )
    output = home_rows(info, out_home, 1, (out_keep,))
    down_reduce.step()
    reduce_a.step()

    def input_part(start):
        rows = slice(start, start + local_len)
        return input_a[rows] + dot(proj_b[rows], weight_b, NT)

    give_send = swap_seq(input_part(own + local_len).astype(bf16), 1)
    give_keep = swap_seq(input_part(own).astype(bf16), 1)
    grad_b = grad_of(tokens, proj_b).astype(bf16)
    proj_sums = jnp.concatenate([proj_sums_a, proj_sums_b])[:, 0].reshape(pairs, 3, 128)
    my_sums = jnp.stack([proj_sums[:, 0].reshape(-1), proj_sums[:, 2].reshape(-1)])
    bias_qv_grad = lax.dynamic_update_slice(
        jnp.zeros((2, width), f32), my_sums, (jnp.int32(0), c * half)
    )

    def split(value):
        return value.reshape(-1, dp, value.shape[-1] // dp).transpose(1, 0, 2).reshape(dp, -1)

    small_grads = jnp.concatenate(
        [
            split(bias_qv_grad),
            split(sums[0:1]),
            split(up_sums[0:1]),
            split(sums[1:2]),
            split(sums[2:4]),
            split(sums[4:6]),
        ],
        axis=1,
    ).astype(bf16)
    small_rows = -(-small_width // (16 * 384)) * 16
    small_grads = jnp.pad(small_grads, ((0, 0), (0, small_rows * 384 - small_width)))
    reduce_b = Reduce(
        jnp.concatenate(
            [grad_b.reshape(dp, shard, 384), small_grads.reshape(dp, small_rows, 384)], axis=1
        ),
        index,
        y,
    )
    reduce_b.start()
    own_send = pre_first[local_len:] + input_part(local_len)
    own_keep = pre_first[:local_len] + input_part(0)
    give_send, give_keep, own_send, own_keep, _ = tie(
        (give_send, give_keep, own_send, own_keep, reduce_b.held)
    )
    grad_moved = swap_seq((own_send + give_send.astype(f32)).astype(bf16), 2)
    grad_keep = (own_keep + give_keep.astype(f32)).astype(bf16)
    grad_inputs = home_rows(info, grad_keep, 0)
    reduces = (reduce_b, reduce_a, down_reduce)

    def settle(*tied):
        moved = tie(tuple(part.moved for part in reduces) + tied)
        for part, value in zip(reduces, moved):
            part.moved = value
        return moved[len(reduces) :]

    grad_inputs, up_sum = settle(grad_inputs, up_sum)
    up_moved = swap_seq(up_sum, 2)
    bits_left = len(reduce_b.bits) + 1
    for k in range(bits_left):
        for part in reduces:
            if part.bits or part.held.ndim > 2:
                part.step()
        settle()
    shard_a, down_out, shard_b = reduce_a.join(), down_reduce.join(), reduce_b.join()
    up_shard = (up_sum.astype(f32) + up_moved.astype(f32)).astype(bf16)
    grad_moved, _ = tie((grad_moved, shard_b))
    grad_inputs = home_rows(info, grad_moved, 1, (grad_inputs,))

    grad_up, grad_out, grad_down = widen(
        info,
        [up_shard, swap_seq(up_shard, 1), down_out, swap_seq(down_out, 1)],
        [
            entry
            for which in (0, 1)
            for entry in (
                (which, 0, shard, 0, middle, 0, 0, middle, which),
                (2 + which, ff_shard, shard, 0, half, 1, 0, half, which),
                (2 + which, 0, ff_shard, 0, half, 2, 0, half, which),
            )
        ],
        [(shard, hidden_width), (shard, width), (ff_shard, width)],
    )
    plan = []
    for which in (0, 1):
        for pair in range(pairs):
            for kind in range(3):
                last = pair == pairs - 1
                source = 2 * last + which
                at = kind * 128 if last else (pair * 3 + kind) * 128
                plan.append(
                    (source, 0, shard, at, 128, 0, kind * width + pair * 128, half, which)
                )
        plan.append((2 + which, shard, small_rows, 0, 384, 1, 0, 384, which))
    grad_qkv, small_sums = widen(
        info,
        [shard_a, swap_seq(shard_a, 1), shard_b, swap_seq(shard_b, 1)],
        plan,
        [(shard, 3 * width), (small_rows, 2 * 384)],
    )
    small_sums = (small_sums[:, :384] + small_sums[:, 384:]).reshape(-1)

    def home(mark, lead):
        part = small_sums[mark[0] : mark[0] + mark[1]]
        return part if lead == 1 else part.reshape(lead, -1)

    return (
        output,
        grad_inputs,
        grad_qkv,
        grad_out,
        grad_up,
        grad_down,
        home(marks[0], 2),
        home(marks[1], 1),
        home(marks[2], 1),
        home(marks[3], 1),
        home(marks[4], 2),
        home(marks[5], 2),
    )


def solution(mesh):
    in_specs = (
        P("dp", "seq", None),
        P("dp", "seq", None),
        P("dp", None),
        P("dp", None),
        P("dp", None),
        P("dp", None),
        P(None, "dp"),
        P("dp"),
        P("dp"),
        P("dp"),
        P(None, "dp"),
        P(None, "dp"),
        P(),
    )
    out_specs = (
        P("dp", "seq", None),
        P("dp", "seq", None),
        P("dp", None),
        P("dp", None),
        P("dp", None),
        P("dp", None),
        P(None, "dp"),
        P("dp"),
        P("dp"),
        P("dp"),
        P(None, "dp"),
        P(None, "dp"),
    )
    return jax.shard_map(body, mesh=mesh, in_specs=in_specs, out_specs=out_specs, check_vma=False)
```

```python
import functools

import jax
import jax.numpy as jnp
from jax import lax
from jax.experimental import pallas as pl
from jax.experimental.pallas import tpu as pltpu
from jax.sharding import PartitionSpec as P

HEADS = 12
HEAD_DIM = 64
BLOCK = 64
RAND = 3

norm_eps = 1e-06
bf16 = jnp.bfloat16
f32 = jnp.float32
NN = (((1,), (0,)), ((), ()))
NT = (((1,), (1,)), ((), ()))
TN = (((0,), (0,)), ((), ()))
VMEM_BYTES = 60 << 20


def dot(a, b, dims=NN):
    return lax.dot_general(a, b, dims, preferred_element_type=f32)


def row_of(block, y, c, chunk_blocks):
    chunk = block // chunk_blocks
    place = (((chunk & 1) ^ c) << 1) | ((chunk >> 1) ^ y)
    return pl.multiple_of((place * chunk_blocks + block % chunk_blocks) * BLOCK, BLOCK)


class Rows:
    def __init__(self, info_ref, rand_ref, first_pair, nblocks):
        self.y, self.c = info_ref[0], info_ref[1]
        self.rand_ref = rand_ref
        self.nblocks = nblocks
        self.head = self.c * info_ref[2] + 2 * first_pair
        self.low = lax.broadcasted_iota(jnp.int32, (BLOCK, 128), 1) < HEAD_DIM
        self.low_row = lax.broadcasted_iota(jnp.int32, (1, 128), 1) < HEAD_DIM

    def at(self, block):
        return pl.ds(row_of(block, self.y, self.c, self.nblocks // 4), BLOCK)

    def two(self, tile):
        zero = jnp.zeros_like(tile)
        return jnp.concatenate(
            [jnp.where(self.low, tile, zero), jnp.where(self.low, zero, tile)], axis=0
        )

    def one(self, both):
        return jnp.where(self.low, both[:BLOCK], both[BLOCK:])

    def rand(self, i):
        middle = self.nblocks - 2
        base = (self.head * middle + (i - 1)) * RAND
        return [
            (self.rand_ref[base + t], self.rand_ref[base + middle * RAND + t]) for t in range(RAND)
        ]

    def near(self, load, ends, i, rand):
        mixed = [jnp.where(self.low, load(a), load(b)) for a, b in rand]
        return jnp.concatenate([ends, load(i - 1), load(i + 1), load(i)] + mixed, axis=0)

    def mask(self, scores, i):
        first = jnp.where(i == 1, -1e30, 0.0)
        last = jnp.where(i == self.nblocks - 2, -1e30, 0.0)
        bias = jnp.where(self.low_row, first, last).astype(f32)
        return jnp.concatenate(
            [scores[:, :128], scores[:, 128:256] + bias, scores[:, 256:]], axis=1
        )


def forward_kernel(info_ref, rand_ref, qkv_ref, *refs, nblocks, first, unroll):
    ctx_ref, lse_ref = refs[-2:]
    rows = Rows(info_ref, rand_ref, pl.program_id(0) + first, nblocks)

    def load(block, column):
        return qkv_ref[rows.at(block), column * 128 : (column + 1) * 128]

    def finish(block, scores, values):
        peak = jnp.max(scores, axis=1, keepdims=True)
        powers = jnp.exp(scores - peak)
        totals = jnp.sum(powers, axis=1, keepdims=True)
        context = dot(powers.astype(bf16), values) / totals
        lse = jnp.broadcast_to(peak + jnp.log(totals), context.shape)
        ctx_ref[rows.at(block), :] = rows.one(context).astype(bf16)
        lse_ref[rows.at(block), :] = rows.one(lse)

    for edge in (0, nblocks - 1):
        scores = dot(rows.two(load(edge, 0)), qkv_ref[:, 128:256], NT)
        finish(edge, scores, qkv_ref[:, 256:384])
    key_ends = jnp.concatenate([load(0, 1), load(nblocks - 1, 1)], axis=0)
    value_ends = jnp.concatenate([load(0, 2), load(nblocks - 1, 2)], axis=0)

    def row(i):
        rand = rows.rand(i)
        keys = rows.near(lambda b: load(b, 1), key_ends, i, rand)
        values = rows.near(lambda b: load(b, 2), value_ends, i, rand)
        finish(i, rows.mask(dot(rows.two(load(i, 0)), keys, NT), i), values)

    def step(t, carry):
        for u in range(unroll):
            row(1 + t * unroll + u)
        return carry

    lax.fori_loop(0, (nblocks - 2) // unroll, step, 0)


def backward_kernel(
    info_ref, rand_ref, qkv_ref, own_ref, other_ref, ctx_ref, lse_ref, out_ref, sum_ref,
    key_sum, value_sum, grad_ref,
    *, nblocks, first, unroll
):
    rows = Rows(info_ref, rand_ref, pl.program_id(0) + first, nblocks)
    zero = jnp.zeros((BLOCK, 128), f32)
    half_rows = own_ref.shape[0]
    grad_ref[:half_rows] = own_ref[...]
    grad_ref[half_rows:] = other_ref[...]

    def load(block, column):
        return qkv_ref[rows.at(block), column * 128 : (column + 1) * 128]

    def finish(block, scores, keys, values):
        grad = grad_ref[rows.at(block), :]
        both = grad.astype(f32) * ctx_ref[rows.at(block), :].astype(f32)
        row_dot = jnp.concatenate(
            [
                jnp.sum(jnp.where(rows.low, both, zero), axis=1, keepdims=True),
                jnp.sum(jnp.where(rows.low, zero, both), axis=1, keepdims=True),
            ],
            axis=0,
        )
        lse = lse_ref[rows.at(block), :]
        lse = jnp.concatenate([lse[:, 0:1], lse[:, HEAD_DIM : HEAD_DIM + 1]], axis=0)
        grad = rows.two(grad)
        attention = jnp.exp(scores - lse)
        attn_grad = dot(grad, values, NT)
        score_grad = (attention * (attn_grad - row_dot)).astype(bf16)
        query_grad = dot(score_grad, keys) * HEAD_DIM ** (-0.5)
        out_ref[rows.at(block), 0:128] = rows.one(query_grad).astype(bf16)
        return grad, attention.astype(bf16), score_grad

    for edge in (0, nblocks - 1):
        query = rows.two(load(edge, 0))
        keys, values = qkv_ref[:, 128:256], qkv_ref[:, 256:384]
        grad, attention, score_grad = finish(edge, dot(query, keys, NT), keys, values)
        if edge == 0:
            key_sum[...] = dot(score_grad, query, TN)
            value_sum[...] = dot(attention, grad, TN)
        else:
            key_sum[...] += dot(score_grad, query, TN)
            value_sum[...] += dot(attention, grad, TN)
    key_ends = jnp.concatenate([load(0, 1), load(nblocks - 1, 1)], axis=0)
    value_ends = jnp.concatenate([load(0, 2), load(nblocks - 1, 2)], axis=0)

    def row(i):
        rand = rows.rand(i)
        keys = rows.near(lambda b: load(b, 1), key_ends, i, rand)
        values = rows.near(lambda b: load(b, 2), value_ends, i, rand)
        query = rows.two(load(i, 0))
        scores = rows.mask(dot(query, keys, NT), i)
        grad, attention, score_grad = finish(i, scores, keys, values)
        for total, part in (
            (key_sum, dot(score_grad, query, TN)),
            (value_sum, dot(attention, grad, TN)),
        ):
            for slot, block in enumerate((0, nblocks - 1, i - 1, i + 1, i)):
                total[rows.at(block), :] += part[slot * BLOCK : (slot + 1) * BLOCK]
            for slot, (a, b) in enumerate(rand):
                tile = part[(5 + slot) * BLOCK : (6 + slot) * BLOCK]
                total[rows.at(a), :] += jnp.where(rows.low, tile, zero)
                total[rows.at(b), :] += jnp.where(rows.low, zero, tile)

    def step(t, carry):
        for u in range(unroll):
            row(1 + t * unroll + u)
        return carry

    lax.fori_loop(0, (nblocks - 2) // unroll, step, 0)
    out_ref[:, 128:256] = key_sum[...].astype(bf16)
    out_ref[:, 256:384] = value_sum[...].astype(bf16)
    sum_ref[0] = jnp.broadcast_to(
        jnp.sum(out_ref[...].astype(f32), axis=0, keepdims=True), (8, 384)
    )


def attend_forward(info, rand, qkv, first, pairs, total, into=()):
    length = qkv.shape[0]
    wide = pl.BlockSpec((length, 384), lambda p, *_: (0, p + first))
    slim = pl.BlockSpec((length, 128), lambda p, *_: (0, p + first))
    return pl.pallas_call(
        functools.partial(forward_kernel, nblocks=length // BLOCK, first=first, unroll=6),
        grid_spec=pltpu.PrefetchScalarGridSpec(
            num_scalar_prefetch=2,
            grid=(pairs,),
            in_specs=[wide] + [pl.BlockSpec(memory_space=pl.ANY)] * len(into),
            out_specs=[slim, slim],
        ),
        out_shape=[
            jax.ShapeDtypeStruct((length, total * 128), bf16),
            jax.ShapeDtypeStruct((length, total * 128), f32),
        ],
        input_output_aliases={3 + k: k for k in range(len(into))},
        compiler_params=pltpu.CompilerParams(vmem_limit_bytes=VMEM_BYTES),
        name="attend_forward",
    )(info, rand, qkv, *into)


def attend_backward(info, rand, qkv, own_grad, other_grad, ctx, lse, first, pairs):
    length = qkv.shape[0]
    wide = pl.BlockSpec((length, 384), lambda p, *_: (0, p + first))
    slim = pl.BlockSpec((length, 128), lambda p, *_: (0, p + first))
    part = pl.BlockSpec((length // 2, 128), lambda p, *_: (0, p + first))
    return pl.pallas_call(
        functools.partial(backward_kernel, nblocks=length // BLOCK, first=first, unroll=6),
        grid_spec=pltpu.PrefetchScalarGridSpec(
            num_scalar_prefetch=2,
            grid=(pairs,),
            in_specs=[wide, part, part, slim, slim],
            out_specs=[
                pl.BlockSpec((length, 384), lambda p, *_: (0, p)),
                pl.BlockSpec((1, 8, 384), lambda p, *_: (p, 0, 0)),
            ],
            scratch_shapes=[pltpu.VMEM((length, 128), f32)] * 2 + [pltpu.VMEM((length, 128), bf16)],
        ),
        out_shape=[
            jax.ShapeDtypeStruct((length, pairs * 384), bf16),
            jax.ShapeDtypeStruct((pairs, 8, 384), f32),
        ],
        compiler_params=pltpu.CompilerParams(vmem_limit_bytes=VMEM_BYTES),
        name="attend_backward",
    )(info, rand, qkv, own_grad, other_grad, ctx, lse)


def swap_dp(value, bit):
    size = lax.axis_size("dp")
    return lax.ppermute(value, "dp", [(i, i ^ bit) for i in range(size)])


def swap_seq(value, bit):
    size = lax.axis_size("seq")
    return lax.ppermute(value, "seq", [(i, i ^ bit) for i in range(size)])


def bits_of(size):
    return [size >> (k + 1) for k in range(size.bit_length() - 1)]


class Gather:
    def __init__(self, shard):
        self.offsets, self.held = [0], shard[None]
        self.bits = bits_of(lax.axis_size("dp")) + [0]
        self.start()

    def start(self):
        self.bit = self.bits.pop(0)
        self.moved = swap_dp(self.held, self.bit) if self.bit else swap_seq(self.held, 2)

    def step(self, *tied):
        self.moved, *tied = lax.optimization_barrier((self.moved, *tied))
        self.held = jnp.concatenate([self.held, self.moved], axis=0)
        self.offsets = self.offsets + [offset ^ self.bit for offset in self.offsets]
        self.start()
        return tied


class Reduce:
    def __init__(self, parts, index, y):
        count, rows, columns = parts.shape
        self.held, self.index, self.y = parts.reshape(count, 2, rows // 2, columns), index, y
        self.bits = [0] + bits_of(lax.axis_size("dp"))[::-1]

    def start(self):
        bit = self.bits.pop(0)
        if bit:
            view = self.held.reshape(-1, 2, *self.held.shape[1:])
            mine = (self.index // bit) % 2
        else:
            view, mine = self.held, self.y
        self.held = lax.dynamic_slice_in_dim(view, mine, 1, 1)[:, 0]
        give = lax.dynamic_slice_in_dim(view, 1 - mine, 1, 1)[:, 0]
        self.moved = swap_dp(give, bit) if bit else swap_seq(give, 2)

    def add(self):
        self.held = (self.held.astype(f32) + self.moved.astype(f32)).astype(bf16)

    def step(self):
        self.add()
        self.start()


def exchange_four(held, index):
    unit = lax.axis_size("dp") // 4
    me = index // unit
    mine = lax.dynamic_index_in_dim(held, me, 0, keepdims=False)
    moved = [
        swap_dp(lax.dynamic_index_in_dim(held, me ^ k, 0, keepdims=False), k * unit)
        for k in (1, 2, 3)
    ]
    return mine, moved


def prepare_kernel(info_ref, w_ref, qv_ref, gain_ref, shift_ref, out_ref, down_ref, up_ref, shard_ref):
    c = info_ref[1]
    third = w_ref.shape[1] // 3
    half = third // 2
    depth, few = qv_ref.shape[1], up_ref.shape[1]
    for kind in range(3):
        columns = pl.ds(pl.multiple_of(kind * third + c * half, 128), half)
        part = w_ref[:, columns]
        for pair in range(half // 128):
            at = (pair * 3 + kind) * 128
            shard_ref[0:depth, at : at + 128] = part[:, pair * 128 : (pair + 1) * 128]
    shard_ref[depth:] = jnp.zeros((8, 3 * half), bf16)
    shard_ref[depth : depth + 2, 0:depth] = qv_ref[...]
    shard_ref[depth + 2 : depth + 4, 0:depth] = gain_ref[...]
    shard_ref[depth + 4 : depth + 6, 0:depth] = shift_ref[...]
    shard_ref[depth + 6 : depth + 7, 0:depth] = out_ref[...]
    shard_ref[depth + 7 : depth + 8, 0:depth] = down_ref[...]
    shard_ref[depth : depth + 1, 128 : 128 + few] = up_ref[...]


def prepare(info, w_qkv, *small):
    depth, columns = w_qkv.shape
    arrays = (w_qkv, *small)
    return pl.pallas_call(
        prepare_kernel,
        grid_spec=pltpu.PrefetchScalarGridSpec(
            num_scalar_prefetch=1,
            grid=(1,),
            in_specs=[pl.BlockSpec(a.shape, lambda i, *_: (0, 0)) for a in arrays],
            out_specs=pl.BlockSpec((depth + 8, columns // 2), lambda i, *_: (0, 0)),
        ),
        out_shape=jax.ShapeDtypeStruct((depth + 8, columns // 2), bf16),
        compiler_params=pltpu.CompilerParams(vmem_limit_bytes=VMEM_BYTES),
        name="prepare",
    )(info, *arrays)


def project_kernel(info_ref, inputs_ref, *refs, offsets, shard, ff_shard):
    more, refs = refs[:3], refs[3:]
    pieces, refs = refs[: len(offsets)], refs[len(offsets) :]
    qkv_ref, tokens_ref, weight_ref, norms_ref, up_ref, bias_ref = refs
    step = pl.program_id(0)
    width = weight_ref.shape[0]
    half = width // 2

    def spread(part, size, target, at):
        shape = (part.shape[1], target)
        lane = lax.broadcasted_iota(jnp.int32, shape, 1) - at
        source = lax.broadcasted_iota(jnp.int32, shape, 0)
        return dot(part, jnp.where((lane == source) & (source < size), 1.0, 0.0).astype(bf16))

    @pl.when(step == 0)
    def _():
        norms = jnp.zeros((8, width), f32)
        for offset, piece in zip(offsets, pieces):
            place = info_ref[4] ^ offset
            at = pl.ds(pl.multiple_of(place * shard, 8), shard)
            weight_ref[at, :] = piece[0:shard]
            tail = piece[shard : shard + 8]
            norms = norms + spread(tail[:, :128], shard, width, place * shard)
            if ff_shard % 128 == 0:
                lanes = pl.ds(pl.multiple_of(place * ff_shard, 128), ff_shard)
                up_ref[:, lanes] = tail[:, 128 : 128 + ff_shard].astype(f32)
            else:
                part = spread(tail[:, 128:256], ff_shard, up_ref.shape[1], place * ff_shard)
                if offset == offsets[0]:
                    up_ref[...] = part
                else:
                    up_ref[...] += part
        norms_ref[...] = norms
        bias_ref[...] = jnp.zeros_like(bias_ref)
        for pair in range(half // 128):
            lanes = pl.ds(pl.multiple_of(info_ref[1] * half + pair * 128, 128), 128)
            bias_ref[0:1, pair * 384 : pair * 384 + 128] = norms_ref[0:1, lanes]
            bias_ref[0:1, pair * 384 + 256 : pair * 384 + 384] = norms_ref[1:2, lanes]
        tokens_ref[...] = inputs_ref[0]

    for k in range(3):

        @pl.when(step == k + 1)
        def _():
            tokens_ref[...] = more[k][...]

    wide = dot(tokens_ref[...], weight_ref[...]) + bias_ref[0:1]
    for pair in range(wide.shape[1] // 384):
        at = pair * 384
        query = wide[:, at : at + 128].astype(bf16).astype(f32) * HEAD_DIM ** (-0.5)
        qkv_ref[:, at : at + 128] = query.astype(bf16)
        qkv_ref[:, at + 128 : at + 384] = wide[:, at + 128 : at + 384].astype(bf16)


def project(info, inputs, more, pieces, offsets, shard, ff_shard):
    _, local_len, width = inputs.shape
    columns = pieces[0].shape[1]
    hidden = ff_shard * len(pieces)

    def whole(array):
        return pl.BlockSpec(array.shape, lambda i, *_: (0, 0), pipeline_mode=pl.Buffered(1))

    fixed = [((width, columns), bf16), ((8, width), f32), ((8, hidden), f32)]
    return pl.pallas_call(
        functools.partial(project_kernel, offsets=offsets, shard=shard, ff_shard=ff_shard),
        grid_spec=pltpu.PrefetchScalarGridSpec(
            num_scalar_prefetch=1,
            grid=(4,),
            in_specs=[pl.BlockSpec((1, local_len, width), lambda i, info: (info[0], 0, 0))]
            + [whole(array) for array in (*more, *pieces)],
            out_specs=[
                pl.BlockSpec((local_len, columns), lambda i, *_: (i, 0)),
                pl.BlockSpec((local_len, width), lambda i, *_: (i, 0)),
            ]
            + [pl.BlockSpec(shape, lambda i, *_: (0, 0)) for shape, _ in fixed],
            scratch_shapes=[pltpu.VMEM((8, columns), f32)],
        ),
        out_shape=[
            jax.ShapeDtypeStruct((4 * local_len, columns), bf16),
            jax.ShapeDtypeStruct((4 * local_len, width), bf16),
        ]
        + [jax.ShapeDtypeStruct(shape, kind) for shape, kind in fixed],
        compiler_params=pltpu.CompilerParams(vmem_limit_bytes=VMEM_BYTES),
        name="project",
    )(info, inputs, *more, *pieces)


CHUNK = 768


def gelu_pair(values):
    square = values * values
    inner = values * (0.7978845608028654 + 0.7978845608028654 * 0.044715 * square)
    gate = 0.5 + 0.5 * jnp.tanh(inner)
    active = values * gate
    slope = 2 * 0.7978845608028654 + 6 * 0.7978845608028654 * 0.044715 * square
    return active, gate + (active - active * gate) * slope


def norm_parts(values):
    center = values - jnp.mean(values, axis=-1, keepdims=True)
    spread = jnp.mean(center * center, axis=-1, keepdims=True)
    inverse = lax.rsqrt(spread + norm_eps)
    return center * inverse, inverse


def norm_back(grad, unit, inverse, gain):
    scaled = grad * gain
    return inverse * (
        scaled
        - jnp.mean(scaled, axis=-1, keepdims=True)
        - unit * jnp.mean(scaled * unit, axis=-1, keepdims=True)
    )


def middle_kernel(
    info_ref,
    tokens_ref,
    ctx_ref,
    ctx_other_ref,
    cotangent_ref,
    up_ref,
    up_other_ref,
    *refs,
    down_plan,
    steps,
):
    n_down = 1 + max(entry[0] for entry in down_plan)
    down_refs, refs = refs[:n_down], refs[n_down:]
    (
        norm_ref,
        bias_up_ref,
        keep_ref,
        send_ref,
        ctx_all_ref,
        normed_ref,
        active_ref,
        hidden_mine_ref,
        hidden_other_ref,
        ffn_mine_ref,
        ffn_other_ref,
        first_ref,
        branch_mine_ref,
        branch_other_ref,
        ctx_grad_ref,
        ctx_send_ref,
        sums_ref,
        up_sums_ref,
        down_all,
        out_all,
        change_all,
        wide,
    ) = refs
    c, index, flip = info_ref[1], info_ref[4], info_ref[5]
    step = pl.program_id(0)
    half = ctx_ref.shape[1]
    middle = up_ref.shape[1] - half
    hidden = 2 * middle

    def up_part(k):
        inside = k * CHUNK % middle
        return (up_ref if k * CHUNK < middle else up_other_ref)[:, inside : inside + CHUNK]

    def lanes(which, size):
        return pl.ds(pl.multiple_of(which * size, 128), size)

    def rows(which, size):
        return pl.ds(pl.multiple_of(which * size, 16), size)

    @pl.when(step == 0)
    def _():
        out_all[:, lanes(c, half)] = up_ref[:, middle:]
        out_all[:, lanes(1 - c, half)] = up_other_ref[:, middle:]
        for source, slot, offset, which in down_plan:
            size = down_refs[source].shape[1]
            block = (index ^ offset ^ flip) * 2 + (info_ref[0] ^ (which // 2))
            down_all[rows(block, size), lanes(c ^ (which % 2), half)] = down_refs[source][slot]
        sums_ref[...] = jnp.zeros_like(sums_ref)
        up_sums_ref[...] = jnp.zeros_like(up_sums_ref)

    bias_out, bias_down = norm_ref[6:7], norm_ref[7:8]
    gain_1, gain_2, shift_1, shift_2 = (norm_ref[k : k + 1] for k in (2, 3, 4, 5))
    ctx_all_ref[:, lanes(c, half)] = ctx_ref[...]
    ctx_all_ref[:, lanes(1 - c, half)] = ctx_other_ref[...]
    branch = dot(ctx_all_ref[...], out_all[...]) + bias_out
    unit_1, inverse_1 = norm_parts(tokens_ref[...].astype(f32) + branch)
    normed = unit_1 * gain_1 + shift_1
    normed_low = normed.astype(bf16)
    normed_ref[...] = normed_low

    total = jnp.zeros_like(branch)
    for k in range(hidden // CHUNK):
        part = slice(k * CHUNK, (k + 1) * CHUNK)
        which = c ^ (k * CHUNK // middle)
        inside = k * CHUNK % middle
        at = pl.ds(pl.multiple_of(which * middle + inside, 128), CHUNK)
        bias = bias_up_ref[0:1, at]
        active, change = gelu_pair(dot(normed_low, up_part(k)) + bias)
        active = active.astype(bf16)
        active_ref[:, at] = active
        change_all[:, part] = change.astype(bf16)
        total = total + dot(active, down_all[part])

    unit_2, inverse_2 = norm_parts(normed + total + bias_down)
    result = (unit_2 * gain_2 + shift_2).astype(bf16)

    @pl.when(step < steps // 2)
    def _():
        keep_ref[0] = result

    @pl.when(step >= steps // 2)
    def _():
        send_ref[...] = result


    cotangent = cotangent_ref[...].astype(f32)
    pre_second = norm_back(cotangent, unit_2, inverse_2, gain_2)
    ffn_grad = pre_second.astype(bf16)
    wide[...] = ffn_grad
    ffn_mine_ref[...] = wide[:, lanes(c, half)]
    ffn_other_ref[...] = wide[:, lanes(1 - c, half)]

    def add(row, values):
        sums_ref[row : row + 1] += jnp.sum(values, axis=0, keepdims=True)

    add(1, ffn_grad.astype(f32))
    add(3, cotangent * unit_2)
    add(5, cotangent)

    total = jnp.zeros_like(branch)
    for k in range(hidden // CHUNK):
        part = slice(k * CHUNK, (k + 1) * CHUNK)
        grad = (dot(ffn_grad, down_all[part], NT) * change_all[:, part]).astype(bf16)
        target = hidden_mine_ref if k * CHUNK < middle else hidden_other_ref
        inside = k * CHUNK % middle
        target[:, inside : inside + CHUNK] = grad
        which = c ^ (k * CHUNK // middle)
        at = pl.ds(pl.multiple_of(which * middle + inside, 128), CHUNK)
        up_sums_ref[0:1, at] += jnp.sum(grad.astype(f32), axis=0, keepdims=True)
        total = total + dot(grad, up_part(k), NT)

    normed_grad = pre_second + total
    pre_first = norm_back(normed_grad, unit_1, inverse_1, gain_1)
    first_ref[...] = pre_first
    branch_grad = pre_first.astype(bf16)
    wide[...] = branch_grad
    branch_mine_ref[...] = wide[:, lanes(c, half)]
    branch_other_ref[...] = wide[:, lanes(1 - c, half)]
    add(0, branch_grad.astype(f32))
    add(2, normed_grad * unit_1)
    add(4, normed_grad)
    ctx_grad = dot(branch_grad, out_all[...], NT).astype(bf16)
    wide[...] = ctx_grad
    ctx_grad_ref[...] = wide[:, lanes(c, half)]
    ctx_send_ref[...] = wide[:, lanes(1 - c, half)]


def feed_forward(info, tokens, ctx, ctx_other, cotangent, up, up_other, down_groups, norms, bias_up):
    count, width = cotangent.shape
    half = ctx.shape[1]
    middle = up.shape[1] - half
    hidden = 2 * middle
    tile = 256
    steps = count // tile
    arrays, plan = [], []
    for offsets, which, array in down_groups:
        for slot, offset in enumerate(offsets):
            plan.append((len(arrays), slot, offset, which))
        arrays.append(array)

    def tiled(columns):
        return pl.BlockSpec((tile, columns), lambda i, *_: (i, 0))

    def whole(array):
        rank = len(array.shape)
        return pl.BlockSpec(
            array.shape, lambda i, *_: (0,) * rank, pipeline_mode=pl.Buffered(1)
        )

    outs = [
        ((count, width), bf16),
        ((count, width), bf16),
        ((count, hidden), bf16),
        ((count, middle), bf16),
        ((count, middle), bf16),
        ((count, half), bf16),
        ((count, half), bf16),
        ((count, width), f32),
        ((count, half), bf16),
        ((count, half), bf16),
        ((count, half), bf16),
        ((count, half), bf16),
    ]
    sums = [((8, width), f32), ((8, hidden), f32)]
    return pl.pallas_call(
        functools.partial(middle_kernel, down_plan=plan, steps=steps),
        grid_spec=pltpu.PrefetchScalarGridSpec(
            num_scalar_prefetch=1,
            grid=(steps,),
            in_specs=[tiled(width), tiled(half), tiled(half), tiled(width), whole(up), whole(up_other)]
            + [whole(array) for array in arrays]
            + [whole(norms), whole(bias_up)],
            out_specs=[
                pl.BlockSpec(
                    (1, tile, width), lambda i, info: (info[0], jnp.minimum(i, steps // 2 - 1), 0)
                ),
                pl.BlockSpec((tile, width), lambda i, *_: (jnp.maximum(i - steps // 2, 0), 0)),
            ]
            + [tiled(shape[1]) for shape, _ in outs]
            + [pl.BlockSpec(shape, lambda i, *_: (0, 0)) for shape, _ in sums],
            scratch_shapes=[
                pltpu.VMEM((hidden, width), bf16),
                pltpu.VMEM((width, width), bf16),
                pltpu.VMEM((tile, hidden), bf16),
                pltpu.VMEM((tile, width), bf16),
            ],
        ),
        out_shape=[jax.ShapeDtypeStruct((2, count // 2, width), bf16)]
        + [jax.ShapeDtypeStruct((count // 2, width), bf16)]
        + [jax.ShapeDtypeStruct(shape, kind) for shape, kind in outs + sums],
        compiler_params=pltpu.CompilerParams(vmem_limit_bytes=VMEM_BYTES),
        name="feed_forward",
    )(info, tokens, ctx, ctx_other, cotangent, up, up_other, *arrays, norms, bias_up)


def home_kernel(info_ref, *refs, count):
    start = 0
    for ref in refs[:count]:
        refs[-1][0, start : start + ref.shape[0]] = ref[...]
        start += ref.shape[0]


def home_rows(info, pieces, which, into=()):
    rows = sum(piece.shape[0] for piece in pieces)
    width = pieces[0].shape[1]
    return pl.pallas_call(
        functools.partial(home_kernel, count=len(pieces)),
        grid_spec=pltpu.PrefetchScalarGridSpec(
            num_scalar_prefetch=1,
            grid=(1,),
            in_specs=[pl.BlockSpec(piece.shape, lambda i, *_: (0, 0)) for piece in pieces]
            + [pl.BlockSpec(memory_space=pl.ANY)] * len(into),
            out_specs=pl.BlockSpec((1, rows, width), lambda i, info: (info[0] ^ which, 0, 0)),
        ),
        out_shape=jax.ShapeDtypeStruct((2, rows, width), bf16),
        input_output_aliases={1 + len(pieces): 0} if into else {},
        name="home_rows",
    )(info, *pieces, *into)


def widen_kernel(info_ref, *refs, plan, n_in):
    ins, outs = refs[:n_in], refs[n_in:]
    c = info_ref[1]
    for source, slot, row, rows, column, width, out, out_row, base, stride, which in plan:
        at = pl.ds(pl.multiple_of(base + (c ^ which) * stride, 128), width)
        outs[out][out_row : out_row + rows, at] = ins[source][
            slot, row : row + rows, column : column + width
        ].astype(f32)


def widen(info, arrays, plan, shapes):
    return pl.pallas_call(
        functools.partial(widen_kernel, plan=plan, n_in=len(arrays)),
        grid_spec=pltpu.PrefetchScalarGridSpec(
            num_scalar_prefetch=1,
            grid=(1,),
            in_specs=[pl.BlockSpec(a.shape, lambda i, *_: (0, 0, 0)) for a in arrays],
            out_specs=[pl.BlockSpec(shape, lambda i, *_: (0, 0)) for shape in shapes],
        ),
        out_shape=[jax.ShapeDtypeStruct(shape, f32) for shape in shapes],
        compiler_params=pltpu.CompilerParams(vmem_limit_bytes=VMEM_BYTES),
        name="widen",
    )(info, *arrays)


def body(
    inputs,
    out_grad,
    w_qkv,
    w_attn_out,
    w_up,
    w_down,
    bias_qv,
    bias_out,
    bias_up,
    bias_down,
    norm_gain,
    norm_shift,
    rand_blocks,
):
    _, local_len, width = inputs.shape
    dp = lax.axis_size("dp")
    index = lax.axis_index("dp")
    seat = lax.axis_index("seq")
    y, c = seat // 2, seat % 2
    heads_here = HEADS // 2
    pairs = heads_here // 2
    half = width // 2
    hidden_width = w_up.shape[1]
    middle = hidden_width // 2
    own = 2 * local_len
    shard = width // dp
    ff_shard = hidden_width // dp
    qkv_width = 3 * half
    flip = c * (dp // 2)
    info = jnp.stack([y, c, jnp.int32(heads_here), jnp.int32(0), index, flip]).astype(jnp.int32)
    rand = rand_blocks.reshape(-1)

    def pick(values, which):
        return lax.dynamic_index_in_dim(values, which, 0, keepdims=False)

    def column(value, which):
        return lax.dynamic_slice_in_dim(value, which * (value.shape[1] // 2), value.shape[1] // 2, 1)

    tie = lax.optimization_barrier

    given = pick(inputs, 1 - y)
    qkv_shard = prepare(
        info, w_qkv, bias_qv, norm_gain, norm_shift, bias_out[None], bias_down[None], bias_up[None]
    )
    bits = bits_of(dp)
    cut = local_len // 2
    chip_a = swap_seq(given[:cut], 2)
    mine = pick(inputs, y)
    first_moves = [swap_dp(qkv_shard, bit) for bit in bits]
    chip_a, rest, *first_moves = tie((chip_a, given[cut:], *first_moves))
    chip_b = swap_seq(rest, 2)
    other_mine = swap_seq(mine, 1)
    held = [(0, qkv_shard)] + list(zip(bits, first_moves))
    if dp == 8:
        held = held + [
            (o ^ bit, swap_dp(part, bit))
            for o, part, bit in (
                (bits[0], first_moves[0], bits[1]),
                (bits[1], first_moves[1], bits[2]),
                (bits[0], first_moves[0], bits[2]),
            )
        ]
    else:
        held = [(0, qkv_shard)]
        for bit in bits:
            held = held + [(o ^ bit, swap_dp(part, bit)) for o, part in held]
    offsets = [offset for offset, _ in held]
    chip_b, other_mine, down_shard, up_out, *parts = tie(
        (
            chip_b,
            other_mine,
            lax.dynamic_slice(w_down, (y * (ff_shard // 2), c * half), (ff_shard // 2, half)),
            jnp.concatenate([column(w_up, c), column(w_attn_out, c)], axis=1),
            *[part for _, part in held],
        )
    )
    held = list(zip(offsets, parts))
    if dp == 8:
        offset, part = held[4]
        held = held + [(offset ^ bits[2], swap_dp(part, bits[2]))]
    from_chip = jnp.concatenate([chip_a, chip_b], axis=0)
    other_chip = swap_seq(from_chip, 1)
    offsets = [offset for offset, _ in held]
    pieces = [part for _, part in held]
    up_out = lax.all_gather(up_out, "dp", axis=0, tiled=True)
    down_gather = Gather(down_shard)
    while len(down_gather.bits) > 2:
        down_gather.step()

    cotangent_chip = swap_seq(pick(out_grad, 1 - y), 2)
    qkv, tokens, full_qkv, norms, bias_up_row = project(
        info, inputs, (from_chip, other_mine, other_chip), pieces, offsets, shard, ff_shard
    )
    (qkv,) = down_gather.step(qkv)
    ctx, lse = attend_forward(info, rand, qkv, 0, 1, pairs)
    qkv, ctx, lse, up_out, cotangent_chip = down_gather.step(
        qkv, ctx, lse, up_out, cotangent_chip
    )
    up_other = swap_seq(up_out, 1)
    held = down_gather.held
    held_other = swap_seq(held, 1)
    ctx, lse = attend_forward(info, rand, qkv, 1, pairs - 1, pairs, (ctx, lse))
    ctx, lse, moved, held_other, up_other = tie((ctx, lse, down_gather.moved, held_other, up_other))
    ctx_other = swap_seq(ctx[own:], 1)
    down_groups = [
        (down_gather.offsets, which, part)
        for which, part in enumerate((held, held_other, moved, swap_seq(moved, 1)))
    ]
    cotangent = jnp.concatenate([pick(out_grad, y), cotangent_chip], axis=0)
    (
        out_keep,
        out_send,
        ctx_all,
        normed,
        active,
        hidden_mine,
        hidden_other,
        ffn_mine,
        ffn_other,
        pre_first,
        branch_mine,
        branch_other,
        ctx_grad,
        ctx_send,
        sums,
        up_sums,
    ) = feed_forward(
        info, tokens, ctx, ctx_other, cotangent, up_out, up_other, down_groups, norms, bias_up_row
    )
    ctx_other_grad = swap_seq(ctx_send, 1)

    def grad_of(left, right):
        return dot(left, right, TN)

    up_give = swap_seq(grad_of(normed, hidden_other).astype(bf16), 1)
    down_give = swap_seq(grad_of(active, ffn_other).astype(bf16), 1)
    out_give = swap_seq(grad_of(ctx_all, branch_other).astype(bf16), 1)
    up_grad = (grad_of(normed, hidden_mine) + up_give.astype(f32)).astype(bf16)
    up_sum = lax.psum_scatter(up_grad, "dp", scatter_dimension=0, tiled=True)
    down_grad = (grad_of(active, ffn_mine) + down_give.astype(f32)).astype(bf16)
    out_weight_grad = (grad_of(ctx_all, branch_mine) + out_give.astype(f32)).astype(bf16)
    down_reduce = Reduce(
        jnp.concatenate(
            [down_grad.reshape(dp, ff_shard, half), out_weight_grad.reshape(dp, shard, half)],
            axis=1,
        ),
        index,
        y,
    )
    down_reduce.start()
    ctx_grad, ctx_other_grad, _ = tie((ctx_grad, ctx_other_grad, down_reduce.held))

    proj_a, proj_sums_a = attend_backward(
        info, rand, qkv, ctx_grad, ctx_other_grad, ctx, lse, 0, pairs - 1
    )
    proj_a, ctx_grad, down_reduce.moved = tie((proj_a, ctx_grad, down_reduce.moved))
    down_reduce.step()
    out_home = swap_seq(out_send, 2)
    wide_a = 384 * (pairs - 1)
    grad_a = grad_of(tokens, proj_a).astype(bf16)
    reduce_a = Reduce(grad_a.reshape(dp, shard, wide_a), index, y)
    reduce_a.start()
    weight_a, weight_b = full_qkv[:, :wide_a], full_qkv[:, wide_a:]
    input_a = dot(proj_a, weight_a, NT)
    ctx_grad, input_a, _ = tie((ctx_grad, input_a, reduce_a.held))
    proj_b, proj_sums_b = attend_backward(
        info, rand, qkv, ctx_grad, ctx_other_grad, ctx, lse, pairs - 1, 1
    )
    proj_b, reduce_a.moved, down_reduce.moved, out_home = tie(
        (proj_b, reduce_a.moved, down_reduce.moved, out_home)
    )
    output = home_rows(info, [out_home], 1, (out_keep,))
    while len(down_reduce.bits) > 1:
        down_reduce.step()
    while len(reduce_a.bits) > 2:
        reduce_a.step()

    def input_part(start, rows):
        return input_a[start : start + rows] + dot(proj_b[start : start + rows], weight_b, NT)

    give_send = swap_seq(input_part(own + local_len, local_len).astype(bf16), 1)
    give_keep = swap_seq(input_part(own, local_len).astype(bf16), 1)
    grad_b = grad_of(tokens, proj_b).astype(bf16)
    proj_sums = jnp.concatenate([proj_sums_a, proj_sums_b])[:, 0].reshape(pairs, 3, 128)
    my_sums = jnp.stack([proj_sums[:, 0].reshape(-1), proj_sums[:, 2].reshape(-1)])
    bias_qv_grad = lax.dynamic_update_slice(
        jnp.zeros((2, width), f32), my_sums, (jnp.int32(0), c * half)
    )

    rows = jnp.concatenate([bias_qv_grad, sums[2:6], sums[0:2]], axis=0)
    rows = rows.reshape(8, dp, shard).transpose(1, 0, 2)
    small_rows = 16
    small_grads = jnp.concatenate(
        [
            jnp.pad(rows, ((0, 0), (0, 0), (0, 384 - shard))),
            jnp.pad(up_sums[0].reshape(dp, 1, ff_shard), ((0, 0), (0, 7), (0, 384 - ff_shard))),
        ],
        axis=1,
    ).astype(bf16)
    reduce_b = Reduce(
        jnp.concatenate(
            [grad_b.reshape(dp, shard, 384), small_grads], axis=1
        ),
        index,
        y,
    )
    reduce_b.start()
    own_send = pre_first[local_len:] + input_part(local_len, local_len)
    own_keep = pre_first[:local_len] + input_part(0, local_len)
    (
        give_send,
        give_keep,
        own_send,
        own_keep,
        reduce_a.moved,
        reduce_b.moved,
        down_reduce.moved,
        up_sum,
    ) = tie(
        (
            give_send,
            give_keep,
            own_send,
            own_keep,
            reduce_a.moved,
            reduce_b.moved,
            down_reduce.moved,
            up_sum,
        )
    )
    grad_send = (own_send + give_send.astype(f32)).astype(bf16)
    moved_a = swap_seq(grad_send[:cut], 2)
    while len(reduce_b.bits) > 2:
        reduce_b.step()
    down_reduce.step()
    up_moved = swap_seq(up_sum, 2)
    reduce_a.add()
    grad_inputs = home_rows(info, [(own_keep + give_keep.astype(f32)).astype(bf16)], 0)
    (
        moved_a,
        grad_rest,
        reduce_a.held,
        reduce_b.moved,
        down_reduce.moved,
        up_moved,
        grad_inputs,
    ) = tie(
        (
            moved_a,
            grad_send[cut:],
            reduce_a.held,
            reduce_b.moved,
            down_reduce.moved,
            up_moved,
            grad_inputs,
        )
    )
    moved_b = swap_seq(grad_rest, 2)
    reduce_b.add()
    down_reduce.add()
    mine, moves = exchange_four(
        jnp.concatenate(
            [reduce_a.held[:, :, k * 384 : (k + 1) * 384] for k in range(pairs - 1)]
            + [reduce_b.held],
            axis=1,
        ),
        index,
    )
    up_shard = (up_sum.astype(f32) + up_moved.astype(f32)).astype(bf16)
    mine, up_shard, down_held, moved_b, *moves = tie(
        (mine, up_shard, down_reduce.held[0], moved_b, *moves)
    )
    up_shard_other = swap_seq(up_shard, 1)
    total = mine.astype(f32)
    for part in moves:
        total = total + part.astype(f32)
    last = jnp.concatenate([down_held, total.astype(bf16)], axis=0)
    last_chip = swap_seq(last, 2)
    (grad_up,) = widen(
        info,
        [up_shard[None], up_shard_other[None]],
        [(which, 0, 0, shard, 0, middle, 0, 0, 0, middle, which) for which in (0, 1)],
        [(shard, hidden_width)],
    )
    grad_inputs = home_rows(info, [moved_a, moved_b], 1, (grad_inputs,))
    last_chip, grad_up, grad_inputs = tie((last_chip, grad_up, grad_inputs))
    last = jnp.where(y == 0, jnp.stack([last, last_chip]), jnp.stack([last_chip, last]))

    plan = []
    part_rows = (ff_shard + shard) // 2
    few = shard // 2
    b_rows = (shard + small_rows) // 2
    for which in (0, 1):
        for slot in (0, 1):

            def put(row, count, out, out_row, base, stride, column=0, wide=384):
                if count > 0:
                    plan.append(
                        (which, slot, row, count, column, wide, out, out_row, base, stride, which)
                    )

            low, high = slot * part_rows, (slot + 1) * part_rows
            cutoff = min(high, ff_shard)
            put(0, cutoff - low, 2, low, 0, half)
            put(cutoff - low, high - cutoff, 1, cutoff - ff_shard, 0, half)
            for pair in range(pairs):
                for kind in range(3):
                    base = kind * width + pair * 128
                    if pair < pairs - 1:
                        row, count, out_row = part_rows + pair * few, few, slot * few
                    else:
                        row, out_row = part_rows + (pairs - 1) * few, slot * b_rows
                        count = min(b_rows, shard - out_row)
                    put(row, count, 0, out_row, base, half, kind * 128, 128)
            start = part_rows + (pairs - 1) * few
            first = max(shard - slot * b_rows, 0)
            put(start + first, b_rows - first, 3, slot * b_rows + first - shard, 0, 384)
    grad_qkv, grad_out, grad_down, small_sums = widen(
        info,
        [last, swap_seq(last, 1)],
        plan,
        [(shard, 3 * width), (shard, width), (ff_shard, width), (small_rows, 2 * 384)],
    )
    small_sums = small_sums[:, :384] + small_sums[:, 384:]

    return (
        output,
        grad_inputs,
        grad_qkv,
        grad_out,
        grad_up,
        grad_down,
        small_sums[0:2, :shard],
        small_sums[6, :shard],
        small_sums[8, :ff_shard],
        small_sums[7, :shard],
        small_sums[2:4, :shard],
        small_sums[4:6, :shard],
    )


def solution(mesh):
    in_specs = (
        P("dp", "seq", None),
        P("dp", "seq", None),
        P("dp", None),
        P("dp", None),
        P("dp", None),
        P("dp", None),
        P(None, "dp"),
        P("dp"),
        P("dp"),
        P("dp"),
        P(None, "dp"),
        P(None, "dp"),
        P(),
    )
    out_specs = (
        P("dp", "seq", None),
        P("dp", "seq", None),
        P("dp", None),
        P("dp", None),
        P("dp", None),
        P("dp", None),
        P(None, "dp"),
        P("dp"),
        P("dp"),
        P("dp"),
        P(None, "dp"),
        P(None, "dp"),
    )
    return jax.shard_map(body, mesh=mesh, in_specs=in_specs, out_specs=out_specs, check_vma=False)
```

```python
import functools

import jax
import jax.numpy as jnp
from jax import lax
from jax.experimental import pallas as pl
from jax.experimental.pallas import tpu as pltpu
from jax.sharding import PartitionSpec as P

HEADS = 12
HEAD_DIM = 64
BLOCK = 64
RAND = 3

norm_eps = 1e-06
bf16 = jnp.bfloat16
f32 = jnp.float32
NN = (((1,), (0,)), ((), ()))
NT = (((1,), (1,)), ((), ()))
TN = (((0,), (0,)), ((), ()))
VMEM_BYTES = 60 << 20


def dot(a, b, dims=NN):
    return lax.dot_general(a, b, dims, preferred_element_type=f32)


def row_of(block, y, c, chunk_blocks):
    chunk = block // chunk_blocks
    place = (((chunk & 1) ^ c) << 1) | ((chunk >> 1) ^ y)
    return pl.multiple_of((place * chunk_blocks + block % chunk_blocks) * BLOCK, BLOCK)


class Rows:
    def __init__(self, info_ref, rand_ref, first_pair, nblocks):
        self.y, self.c = info_ref[0], info_ref[1]
        self.rand_ref = rand_ref
        self.nblocks = nblocks
        self.head = self.c * info_ref[2] + 2 * first_pair
        self.low = lax.broadcasted_iota(jnp.int32, (BLOCK, 128), 1) < HEAD_DIM
        self.low_row = lax.broadcasted_iota(jnp.int32, (1, 128), 1) < HEAD_DIM

    def at(self, block):
        return pl.ds(row_of(block, self.y, self.c, self.nblocks // 4), BLOCK)

    def two(self, tile):
        zero = jnp.zeros_like(tile)
        return jnp.concatenate(
            [jnp.where(self.low, tile, zero), jnp.where(self.low, zero, tile)], axis=0
        )

    def one(self, both):
        return jnp.where(self.low, both[:BLOCK], both[BLOCK:])

    def rand(self, i):
        middle = self.nblocks - 2
        base = (self.head * middle + (i - 1)) * RAND
        return [
            (self.rand_ref[base + t], self.rand_ref[base + middle * RAND + t]) for t in range(RAND)
        ]

    def near(self, load, ends, i, rand):
        mixed = [jnp.where(self.low, load(a), load(b)) for a, b in rand]
        return jnp.concatenate([ends, load(i - 1), load(i + 1), load(i)] + mixed, axis=0)

    def mask(self, scores, i):
        first = jnp.where(i == 1, -1e30, 0.0)
        last = jnp.where(i == self.nblocks - 2, -1e30, 0.0)
        bias = jnp.where(self.low_row, first, last).astype(f32)
        return jnp.concatenate(
            [scores[:, :128], scores[:, 128:256] + bias, scores[:, 256:]], axis=1
        )


def forward_kernel(info_ref, rand_ref, qkv_ref, *refs, nblocks, first, unroll):
    ctx_ref, lse_ref = refs[-2:]
    rows = Rows(info_ref, rand_ref, pl.program_id(0) + first, nblocks)

    def load(block, column):
        return qkv_ref[rows.at(block), column * 128 : (column + 1) * 128]

    def finish(block, scores, values):
        peak = jnp.max(scores, axis=1, keepdims=True)
        powers = jnp.exp(scores - peak).astype(bf16)
        both = dot(powers, jnp.concatenate([values, jnp.ones_like(values)], axis=1))
        totals = both[:, 128:]
        lse = peak + jnp.log(totals)
        ctx_ref[rows.at(block), :] = rows.one(both[:, :128] / totals).astype(bf16)
        lse_ref[rows.at(block), :128] = lse[:BLOCK]
        lse_ref[rows.at(block), 128:] = lse[BLOCK:]

    for edge in (0, nblocks - 1):
        scores = dot(rows.two(load(edge, 0)), qkv_ref[:, 128:256], NT)
        finish(edge, scores, qkv_ref[:, 256:384])
    key_ends = jnp.concatenate([load(0, 1), load(nblocks - 1, 1)], axis=0)
    value_ends = jnp.concatenate([load(0, 2), load(nblocks - 1, 2)], axis=0)

    def row(i):
        rand = rows.rand(i)
        keys = rows.near(lambda b: load(b, 1), key_ends, i, rand)
        values = rows.near(lambda b: load(b, 2), value_ends, i, rand)
        finish(i, rows.mask(dot(rows.two(load(i, 0)), keys, NT), i), values)

    def step(t, carry):
        for u in range(unroll):
            row(1 + t * unroll + u)
        return carry

    lax.fori_loop(0, (nblocks - 2) // unroll, step, 0)


def backward_kernel(
    info_ref, rand_ref, qkv_ref, own_ref, other_ref, ctx_ref, lse_ref, out_ref, sum_ref,
    key_sum, value_sum, grad_ref,
    *, nblocks, first, unroll
):
    rows = Rows(info_ref, rand_ref, pl.program_id(0) + first, nblocks)
    zero = jnp.zeros((BLOCK, 128), f32)
    half_rows = own_ref.shape[0]
    grad_ref[:half_rows] = own_ref[...]
    grad_ref[half_rows:] = other_ref[...]

    def load(block, column):
        return qkv_ref[rows.at(block), column * 128 : (column + 1) * 128]

    ones = jnp.ones((256, 128), bf16)

    def finish(block, scores, keys, values):
        grad = grad_ref[rows.at(block), :]
        both = grad.astype(f32) * ctx_ref[rows.at(block), :].astype(f32)
        high = both.astype(bf16)
        rest = (both - high.astype(f32)).astype(bf16)
        row_dot = dot(jnp.concatenate([rows.two(high), rows.two(rest)], axis=1), ones)
        lse = jnp.concatenate(
            [lse_ref[rows.at(block), :128], lse_ref[rows.at(block), 128:]], axis=0
        )
        grad = rows.two(grad)
        attn_grad = dot(grad, values, NT)
        attention, score_grad = [], []
        for k in range(scores.shape[1] // 128):
            part = slice(k * 128, (k + 1) * 128)
            probs = jnp.exp(scores[:, part] - lse)
            score_grad.append((probs * (attn_grad[:, part] - row_dot)).astype(bf16))
            attention.append(probs.astype(bf16))
        attention = jnp.concatenate(attention, axis=1)
        score_grad = jnp.concatenate(score_grad, axis=1)
        query_grad = dot(score_grad, keys) * HEAD_DIM ** (-0.5)
        out_ref[rows.at(block), 0:128] = rows.one(query_grad).astype(bf16)
        return grad, attention, score_grad

    for edge in (0, nblocks - 1):
        query = rows.two(load(edge, 0))
        keys, values = qkv_ref[:, 128:256], qkv_ref[:, 256:384]
        grad, attention, score_grad = finish(edge, dot(query, keys, NT), keys, values)
        if edge == 0:
            key_sum[...] = dot(score_grad, query, TN)
            value_sum[...] = dot(attention, grad, TN)
        else:
            key_sum[...] += dot(score_grad, query, TN)
            value_sum[...] += dot(attention, grad, TN)
    key_ends = jnp.concatenate([load(0, 1), load(nblocks - 1, 1)], axis=0)
    value_ends = jnp.concatenate([load(0, 2), load(nblocks - 1, 2)], axis=0)

    def row(i):
        rand = rows.rand(i)
        keys = rows.near(lambda b: load(b, 1), key_ends, i, rand)
        values = rows.near(lambda b: load(b, 2), value_ends, i, rand)
        query = rows.two(load(i, 0))
        scores = rows.mask(dot(query, keys, NT), i)
        grad, attention, score_grad = finish(i, scores, keys, values)
        for total, part in (
            (key_sum, dot(score_grad, query, TN)),
            (value_sum, dot(attention, grad, TN)),
        ):
            for slot, block in enumerate((0, nblocks - 1, i - 1, i + 1, i)):
                total[rows.at(block), :] += part[slot * BLOCK : (slot + 1) * BLOCK]
            for slot, (a, b) in enumerate(rand):
                tile = part[(5 + slot) * BLOCK : (6 + slot) * BLOCK]
                total[rows.at(a), :] += jnp.where(rows.low, tile, zero)
                total[rows.at(b), :] += jnp.where(rows.low, zero, tile)

    def step(t, carry):
        for u in range(unroll):
            row(1 + t * unroll + u)
        return carry

    lax.fori_loop(0, (nblocks - 2) // unroll, step, 0)
    out_ref[:, 128:256] = key_sum[...].astype(bf16)
    out_ref[:, 256:384] = value_sum[...].astype(bf16)
    sum_ref[0] = jnp.broadcast_to(
        jnp.sum(out_ref[...].astype(f32), axis=0, keepdims=True), (8, 384)
    )


def attend_forward(info, rand, qkv, first, pairs, total, into=()):
    length = qkv.shape[0]
    wide = pl.BlockSpec((length, 384), lambda p, *_: (0, p + first))
    slim = pl.BlockSpec((length, 128), lambda p, *_: (0, p + first))
    twin = pl.BlockSpec((length, 256), lambda p, *_: (0, p + first))
    return pl.pallas_call(
        functools.partial(forward_kernel, nblocks=length // BLOCK, first=first, unroll=10),
        grid_spec=pltpu.PrefetchScalarGridSpec(
            num_scalar_prefetch=2,
            grid=(pairs,),
            in_specs=[wide] + [pl.BlockSpec(memory_space=pl.ANY)] * len(into),
            out_specs=[slim, twin],
        ),
        out_shape=[
            jax.ShapeDtypeStruct((length, total * 128), bf16),
            jax.ShapeDtypeStruct((length, total * 256), f32),
        ],
        input_output_aliases={3 + k: k for k in range(len(into))},
        compiler_params=pltpu.CompilerParams(vmem_limit_bytes=VMEM_BYTES),
        name="attend_forward",
    )(info, rand, qkv, *into)


def attend_backward(info, rand, qkv, own_grad, other_grad, ctx, lse, first, pairs):
    length = qkv.shape[0]
    wide = pl.BlockSpec((length, 384), lambda p, *_: (0, p + first))
    slim = pl.BlockSpec((length, 128), lambda p, *_: (0, p + first))
    part = pl.BlockSpec((length // 2, 128), lambda p, *_: (0, p + first))
    twin = pl.BlockSpec((length, 256), lambda p, *_: (0, p + first))
    return pl.pallas_call(
        functools.partial(backward_kernel, nblocks=length // BLOCK, first=first, unroll=6),
        grid_spec=pltpu.PrefetchScalarGridSpec(
            num_scalar_prefetch=2,
            grid=(pairs,),
            in_specs=[wide, part, part, slim, twin],
            out_specs=[
                pl.BlockSpec((length, 384), lambda p, *_: (0, p)),
                pl.BlockSpec((1, 8, 384), lambda p, *_: (p, 0, 0)),
            ],
            scratch_shapes=[pltpu.VMEM((length, 128), f32)] * 2 + [pltpu.VMEM((length, 128), bf16)],
        ),
        out_shape=[
            jax.ShapeDtypeStruct((length, pairs * 384), bf16),
            jax.ShapeDtypeStruct((pairs, 8, 384), f32),
        ],
        compiler_params=pltpu.CompilerParams(vmem_limit_bytes=VMEM_BYTES),
        name="attend_backward",
    )(info, rand, qkv, own_grad, other_grad, ctx, lse)


def swap_dp(value, bit):
    size = lax.axis_size("dp")
    return lax.ppermute(value, "dp", [(i, i ^ bit) for i in range(size)])


def swap_seq(value, bit):
    size = lax.axis_size("seq")
    return lax.ppermute(value, "seq", [(i, i ^ bit) for i in range(size)])


def bits_of(size):
    return [size >> (k + 1) for k in range(size.bit_length() - 1)]


def widened(blocks):
    return sum((o for o, _ in blocks), []), jnp.concatenate([a for _, a in blocks], axis=0)


def across(block, bit):
    offsets, array = block
    return [offset ^ bit for offset in offsets], swap_dp(array, bit)


def first_bits(shard):
    block = ([0], shard[None])
    for bit in bits_of(lax.axis_size("dp"))[:-2]:
        block = widened([block, across(block, bit)])
    return block


def tied(blocks, *values):
    arrays = lax.optimization_barrier((*[array for _, array in blocks], *values))
    count = len(blocks)
    return [(blocks[k][0], arrays[k]) for k in range(count)] + list(arrays[count:])


class Reduce:
    def __init__(self, parts, index, y):
        count, rows, columns = parts.shape
        self.held, self.index, self.y = parts.reshape(count, 2, rows // 2, columns), index, y
        self.bits = [0] + bits_of(lax.axis_size("dp"))[::-1]

    def start(self):
        bit = self.bits.pop(0)
        if bit:
            view = self.held.reshape(-1, 2, *self.held.shape[1:])
            mine = (self.index // bit) % 2
        else:
            view, mine = self.held, self.y
        self.held = lax.dynamic_slice_in_dim(view, mine, 1, 1)[:, 0]
        give = lax.dynamic_slice_in_dim(view, 1 - mine, 1, 1)[:, 0]
        self.moved = swap_dp(give, bit) if bit else swap_seq(give, 2)

    def add(self):
        self.held = (self.held.astype(f32) + self.moved.astype(f32)).astype(bf16)

    def step(self):
        self.add()
        self.start()


def exchange_four(held, index):
    unit = lax.axis_size("dp") // 4
    me = index // unit
    mine = lax.dynamic_index_in_dim(held, me, 0, keepdims=False)
    moved = [
        swap_dp(lax.dynamic_index_in_dim(held, me ^ k, 0, keepdims=False), k * unit)
        for k in (1, 2, 3)
    ]
    return mine, moved


def prepare_kernel(info_ref, w_ref, qv_ref, gain_ref, shift_ref, out_ref, down_ref, up_ref, shard_ref):
    c = info_ref[1]
    third = w_ref.shape[1] // 3
    half = third // 2
    depth, few = qv_ref.shape[1], up_ref.shape[1]
    for kind in range(3):
        columns = pl.ds(pl.multiple_of(kind * third + c * half, 128), half)
        part = w_ref[:, columns]
        for pair in range(half // 128):
            at = (pair * 3 + kind) * 128
            shard_ref[0:depth, at : at + 128] = part[:, pair * 128 : (pair + 1) * 128]
    shard_ref[depth:] = jnp.zeros((8, 3 * half), bf16)
    shard_ref[depth : depth + 2, 0:depth] = qv_ref[...]
    shard_ref[depth + 2 : depth + 4, 0:depth] = gain_ref[...]
    shard_ref[depth + 4 : depth + 6, 0:depth] = shift_ref[...]
    shard_ref[depth + 6 : depth + 7, 0:depth] = out_ref[...]
    shard_ref[depth + 7 : depth + 8, 0:depth] = down_ref[...]
    shard_ref[depth : depth + 1, 128 : 128 + few] = up_ref[...]


def prepare(info, w_qkv, *small):
    depth, columns = w_qkv.shape
    arrays = (w_qkv, *small)
    return pl.pallas_call(
        prepare_kernel,
        grid_spec=pltpu.PrefetchScalarGridSpec(
            num_scalar_prefetch=1,
            grid=(1,),
            in_specs=[pl.BlockSpec(a.shape, lambda i, *_: (0, 0)) for a in arrays],
            out_specs=pl.BlockSpec((depth + 8, columns // 2), lambda i, *_: (0, 0)),
        ),
        out_shape=jax.ShapeDtypeStruct((depth + 8, columns // 2), bf16),
        compiler_params=pltpu.CompilerParams(vmem_limit_bytes=VMEM_BYTES),
        name="prepare",
    )(info, *arrays)


def project_kernel(info_ref, inputs_ref, *refs, offsets, shard, ff_shard):
    more, refs = refs[:3], refs[3:]
    pieces, refs = refs[: len(offsets)], refs[len(offsets) :]
    qkv_ref, tokens_ref, weight_ref, norms_ref, up_ref, bias_ref = refs
    step = pl.program_id(0)
    width = weight_ref.shape[0]
    half = width // 2

    def spread(part, size, target, at):
        shape = (part.shape[1], target)
        lane = lax.broadcasted_iota(jnp.int32, shape, 1) - at
        source = lax.broadcasted_iota(jnp.int32, shape, 0)
        return dot(part, jnp.where((lane == source) & (source < size), 1.0, 0.0).astype(bf16))

    @pl.when(step == 0)
    def _():
        norms = jnp.zeros((8, width), f32)
        for offset, piece in zip(offsets, pieces):
            place = info_ref[4] ^ offset
            at = pl.ds(pl.multiple_of(place * shard, 8), shard)
            weight_ref[at, :] = piece[0:shard]
            tail = piece[shard : shard + 8]
            norms = norms + spread(tail[:, :128], shard, width, place * shard)
            if ff_shard % 128 == 0:
                lanes = pl.ds(pl.multiple_of(place * ff_shard, 128), ff_shard)
                up_ref[:, lanes] = tail[:, 128 : 128 + ff_shard].astype(f32)
            else:
                part = spread(tail[:, 128:256], ff_shard, up_ref.shape[1], place * ff_shard)
                if offset == offsets[0]:
                    up_ref[...] = part
                else:
                    up_ref[...] += part
        norms_ref[...] = norms
        bias_ref[...] = jnp.zeros_like(bias_ref)
        for pair in range(half // 128):
            lanes = pl.ds(pl.multiple_of(info_ref[1] * half + pair * 128, 128), 128)
            bias_ref[0:1, pair * 384 : pair * 384 + 128] = norms_ref[0:1, lanes]
            bias_ref[0:1, pair * 384 + 256 : pair * 384 + 384] = norms_ref[1:2, lanes]
        tokens_ref[...] = inputs_ref[0]

    for k in range(3):

        @pl.when(step == k + 1)
        def _():
            tokens_ref[...] = more[k][...]

    wide = dot(tokens_ref[...], weight_ref[...]) + bias_ref[0:1]
    for pair in range(wide.shape[1] // 384):
        at = pair * 384
        query = wide[:, at : at + 128].astype(bf16).astype(f32) * HEAD_DIM ** (-0.5)
        qkv_ref[:, at : at + 128] = query.astype(bf16)
        qkv_ref[:, at + 128 : at + 384] = wide[:, at + 128 : at + 384].astype(bf16)


def project(info, inputs, more, pieces, offsets, shard, ff_shard):
    _, local_len, width = inputs.shape
    columns = pieces[0].shape[1]
    hidden = ff_shard * len(pieces)

    def whole(array):
        return pl.BlockSpec(array.shape, lambda i, *_: (0, 0), pipeline_mode=pl.Buffered(1))

    fixed = [((width, columns), bf16), ((8, width), f32), ((8, hidden), f32)]
    return pl.pallas_call(
        functools.partial(project_kernel, offsets=offsets, shard=shard, ff_shard=ff_shard),
        grid_spec=pltpu.PrefetchScalarGridSpec(
            num_scalar_prefetch=1,
            grid=(4,),
            in_specs=[pl.BlockSpec((1, local_len, width), lambda i, info: (info[0], 0, 0))]
            + [whole(array) for array in (*more, *pieces)],
            out_specs=[
                pl.BlockSpec((local_len, columns), lambda i, *_: (i, 0)),
                pl.BlockSpec((local_len, width), lambda i, *_: (i, 0)),
            ]
            + [pl.BlockSpec(shape, lambda i, *_: (0, 0)) for shape, _ in fixed],
            scratch_shapes=[pltpu.VMEM((8, columns), f32)],
        ),
        out_shape=[
            jax.ShapeDtypeStruct((4 * local_len, columns), bf16),
            jax.ShapeDtypeStruct((4 * local_len, width), bf16),
        ]
        + [jax.ShapeDtypeStruct(shape, kind) for shape, kind in fixed],
        compiler_params=pltpu.CompilerParams(vmem_limit_bytes=VMEM_BYTES),
        name="project",
    )(info, inputs, *more, *pieces)


CHUNK = 768


def gelu_pair(values):
    square = values * values
    inner = values * (0.7978845608028654 + 0.7978845608028654 * 0.044715 * square)
    gate = 0.5 + 0.5 * jnp.tanh(inner)
    active = values * gate
    slope = 2 * 0.7978845608028654 + 6 * 0.7978845608028654 * 0.044715 * square
    return active, gate + (active - active * gate) * slope


def norm_parts(values):
    center = values - jnp.mean(values, axis=-1, keepdims=True)
    spread = jnp.mean(center * center, axis=-1, keepdims=True)
    inverse = lax.rsqrt(spread + norm_eps)
    return center * inverse, inverse


def norm_back(grad, unit, inverse, gain):
    scaled = grad * gain
    return inverse * (
        scaled
        - jnp.mean(scaled, axis=-1, keepdims=True)
        - unit * jnp.mean(scaled * unit, axis=-1, keepdims=True)
    )


def middle_kernel(
    info_ref,
    tokens_ref,
    ctx_ref,
    ctx_other_ref,
    cotangent_ref,
    up_ref,
    up_other_ref,
    *refs,
    down_plan,
    steps,
):
    n_down = 1 + max(entry[0] for entry in down_plan)
    down_refs, refs = refs[:n_down], refs[n_down:]
    (
        norm_ref,
        bias_up_ref,
        keep_ref,
        send_ref,
        ctx_all_ref,
        normed_ref,
        active_ref,
        hidden_mine_ref,
        hidden_other_ref,
        ffn_mine_ref,
        ffn_other_ref,
        first_ref,
        branch_mine_ref,
        branch_other_ref,
        ctx_grad_ref,
        ctx_send_ref,
        sums_ref,
        up_sums_ref,
        down_all,
        out_all,
        change_all,
        wide,
    ) = refs
    c, index, flip = info_ref[1], info_ref[4], info_ref[5]
    step = pl.program_id(0)
    half = ctx_ref.shape[1]
    middle = up_ref.shape[1] - half
    hidden = 2 * middle

    def up_part(k):
        inside = k * CHUNK % middle
        return (up_ref if k * CHUNK < middle else up_other_ref)[:, inside : inside + CHUNK]

    def lanes(which, size):
        return pl.ds(pl.multiple_of(which * size, 128), size)

    def rows(which, size):
        return pl.ds(pl.multiple_of(which * size, 16), size)

    @pl.when(step == 0)
    def _():
        out_all[:, lanes(c, half)] = up_ref[:, middle:]
        out_all[:, lanes(1 - c, half)] = up_other_ref[:, middle:]
        for source, slot, offset, which in down_plan:
            size = down_refs[source].shape[1]
            block = (index ^ offset ^ flip) * 2 + (info_ref[0] ^ (which // 2))
            down_all[rows(block, size), lanes(c ^ (which % 2), half)] = down_refs[source][slot]
        sums_ref[...] = jnp.zeros_like(sums_ref)
        up_sums_ref[...] = jnp.zeros_like(up_sums_ref)

    bias_out, bias_down = norm_ref[6:7], norm_ref[7:8]
    gain_1, gain_2, shift_1, shift_2 = (norm_ref[k : k + 1] for k in (2, 3, 4, 5))
    ctx_all_ref[:, lanes(c, half)] = ctx_ref[...]
    ctx_all_ref[:, lanes(1 - c, half)] = ctx_other_ref[...]
    branch = dot(ctx_all_ref[...], out_all[...]) + bias_out
    unit_1, inverse_1 = norm_parts(tokens_ref[...].astype(f32) + branch)
    normed = unit_1 * gain_1 + shift_1
    normed_low = normed.astype(bf16)
    normed_ref[...] = normed_low

    total = jnp.zeros_like(branch)
    for k in range(hidden // CHUNK):
        part = slice(k * CHUNK, (k + 1) * CHUNK)
        which = c ^ (k * CHUNK // middle)
        inside = k * CHUNK % middle
        at = pl.ds(pl.multiple_of(which * middle + inside, 128), CHUNK)
        bias = bias_up_ref[0:1, at]
        active, change = gelu_pair(dot(normed_low, up_part(k)) + bias)
        active = active.astype(bf16)
        active_ref[:, at] = active
        change_all[:, part] = change.astype(bf16)
        total = total + dot(active, down_all[part])

    unit_2, inverse_2 = norm_parts(normed + total + bias_down)
    result = (unit_2 * gain_2 + shift_2).astype(bf16)

    @pl.when(step < steps // 2)
    def _():
        keep_ref[0] = result

    @pl.when(step >= steps // 2)
    def _():
        send_ref[...] = result


    cotangent = cotangent_ref[...].astype(f32)
    pre_second = norm_back(cotangent, unit_2, inverse_2, gain_2)
    ffn_grad = pre_second.astype(bf16)
    wide[...] = ffn_grad
    ffn_mine_ref[...] = wide[:, lanes(c, half)]
    ffn_other_ref[...] = wide[:, lanes(1 - c, half)]

    def add(row, values):
        sums_ref[row : row + 1] += jnp.sum(values, axis=0, keepdims=True)

    add(1, ffn_grad.astype(f32))
    add(3, cotangent * unit_2)
    add(5, cotangent)

    total = jnp.zeros_like(branch)
    for k in range(hidden // CHUNK):
        part = slice(k * CHUNK, (k + 1) * CHUNK)
        grad = (dot(ffn_grad, down_all[part], NT) * change_all[:, part]).astype(bf16)
        target = hidden_mine_ref if k * CHUNK < middle else hidden_other_ref
        inside = k * CHUNK % middle
        target[:, inside : inside + CHUNK] = grad
        which = c ^ (k * CHUNK // middle)
        at = pl.ds(pl.multiple_of(which * middle + inside, 128), CHUNK)
        up_sums_ref[0:1, at] += jnp.sum(grad.astype(f32), axis=0, keepdims=True)
        total = total + dot(grad, up_part(k), NT)

    normed_grad = pre_second + total
    pre_first = norm_back(normed_grad, unit_1, inverse_1, gain_1)
    first_ref[...] = pre_first
    branch_grad = pre_first.astype(bf16)
    wide[...] = branch_grad
    branch_mine_ref[...] = wide[:, lanes(c, half)]
    branch_other_ref[...] = wide[:, lanes(1 - c, half)]
    add(0, branch_grad.astype(f32))
    add(2, normed_grad * unit_1)
    add(4, normed_grad)
    ctx_grad = dot(branch_grad, out_all[...], NT).astype(bf16)
    wide[...] = ctx_grad
    ctx_grad_ref[...] = wide[:, lanes(c, half)]
    ctx_send_ref[...] = wide[:, lanes(1 - c, half)]


def feed_forward(info, tokens, ctx, ctx_other, cotangent, up, up_other, down_groups, norms, bias_up):
    count, width = cotangent.shape
    half = ctx.shape[1]
    middle = up.shape[1] - half
    hidden = 2 * middle
    tile = 256
    steps = count // tile
    arrays, plan = [], []
    for offsets, which, array in down_groups:
        for slot, offset in enumerate(offsets):
            plan.append((len(arrays), slot, offset, which))
        arrays.append(array)

    def tiled(columns):
        return pl.BlockSpec((tile, columns), lambda i, *_: (i, 0))

    def whole(array):
        rank = len(array.shape)
        return pl.BlockSpec(
            array.shape, lambda i, *_: (0,) * rank, pipeline_mode=pl.Buffered(1)
        )

    outs = [
        ((count, width), bf16),
        ((count, width), bf16),
        ((count, hidden), bf16),
        ((count, middle), bf16),
        ((count, middle), bf16),
        ((count, half), bf16),
        ((count, half), bf16),
        ((count, width), f32),
        ((count, half), bf16),
        ((count, half), bf16),
        ((count, half), bf16),
        ((count, half), bf16),
    ]
    sums = [((8, width), f32), ((8, hidden), f32)]
    return pl.pallas_call(
        functools.partial(middle_kernel, down_plan=plan, steps=steps),
        grid_spec=pltpu.PrefetchScalarGridSpec(
            num_scalar_prefetch=1,
            grid=(steps,),
            in_specs=[tiled(width), tiled(half), tiled(half), tiled(width), whole(up), whole(up_other)]
            + [whole(array) for array in arrays]
            + [whole(norms), whole(bias_up)],
            out_specs=[
                pl.BlockSpec(
                    (1, tile, width), lambda i, info: (info[0], jnp.minimum(i, steps // 2 - 1), 0)
                ),
                pl.BlockSpec((tile, width), lambda i, *_: (jnp.maximum(i - steps // 2, 0), 0)),
            ]
            + [tiled(shape[1]) for shape, _ in outs]
            + [pl.BlockSpec(shape, lambda i, *_: (0, 0)) for shape, _ in sums],
            scratch_shapes=[
                pltpu.VMEM((hidden, width), bf16),
                pltpu.VMEM((width, width), bf16),
                pltpu.VMEM((tile, hidden), bf16),
                pltpu.VMEM((tile, width), bf16),
            ],
        ),
        out_shape=[jax.ShapeDtypeStruct((2, count // 2, width), bf16)]
        + [jax.ShapeDtypeStruct((count // 2, width), bf16)]
        + [jax.ShapeDtypeStruct(shape, kind) for shape, kind in outs + sums],
        compiler_params=pltpu.CompilerParams(vmem_limit_bytes=VMEM_BYTES),
        name="feed_forward",
    )(info, tokens, ctx, ctx_other, cotangent, up, up_other, *arrays, norms, bias_up)


def home_kernel(info_ref, *refs, count):
    start = 0
    for ref in refs[:count]:
        refs[-1][0, start : start + ref.shape[0]] = ref[...]
        start += ref.shape[0]


def home_rows(info, pieces, which, into=()):
    rows = sum(piece.shape[0] for piece in pieces)
    width = pieces[0].shape[1]
    return pl.pallas_call(
        functools.partial(home_kernel, count=len(pieces)),
        grid_spec=pltpu.PrefetchScalarGridSpec(
            num_scalar_prefetch=1,
            grid=(1,),
            in_specs=[pl.BlockSpec(piece.shape, lambda i, *_: (0, 0)) for piece in pieces]
            + [pl.BlockSpec(memory_space=pl.ANY)] * len(into),
            out_specs=pl.BlockSpec((1, rows, width), lambda i, info: (info[0] ^ which, 0, 0)),
        ),
        out_shape=jax.ShapeDtypeStruct((2, rows, width), bf16),
        input_output_aliases={1 + len(pieces): 0} if into else {},
        name="home_rows",
    )(info, *pieces, *into)


def widen_kernel(info_ref, *refs, plan, n_in):
    ins, outs = refs[:n_in], refs[n_in:]
    c = info_ref[1]
    for source, slot, row, rows, column, width, out, out_row, base, stride, which in plan:
        at = pl.ds(pl.multiple_of(base + (c ^ which) * stride, 128), width)
        outs[out][out_row : out_row + rows, at] = ins[source][
            slot, row : row + rows, column : column + width
        ].astype(f32)


def widen(info, arrays, plan, shapes):
    return pl.pallas_call(
        functools.partial(widen_kernel, plan=plan, n_in=len(arrays)),
        grid_spec=pltpu.PrefetchScalarGridSpec(
            num_scalar_prefetch=1,
            grid=(1,),
            in_specs=[pl.BlockSpec(a.shape, lambda i, *_: (0, 0, 0)) for a in arrays],
            out_specs=[pl.BlockSpec(shape, lambda i, *_: (0, 0)) for shape in shapes],
        ),
        out_shape=[jax.ShapeDtypeStruct(shape, f32) for shape in shapes],
        compiler_params=pltpu.CompilerParams(vmem_limit_bytes=VMEM_BYTES),
        name="widen",
    )(info, *arrays)


def body(
    inputs,
    out_grad,
    w_qkv,
    w_attn_out,
    w_up,
    w_down,
    bias_qv,
    bias_out,
    bias_up,
    bias_down,
    norm_gain,
    norm_shift,
    rand_blocks,
):
    _, local_len, width = inputs.shape
    dp = lax.axis_size("dp")
    index = lax.axis_index("dp")
    seat = lax.axis_index("seq")
    y, c = seat // 2, seat % 2
    heads_here = HEADS // 2
    pairs = heads_here // 2
    half = width // 2
    hidden_width = w_up.shape[1]
    middle = hidden_width // 2
    own = 2 * local_len
    shard = width // dp
    ff_shard = hidden_width // dp
    qkv_width = 3 * half
    flip = c * (dp // 2)
    info = jnp.stack([y, c, jnp.int32(heads_here), jnp.int32(0), index, flip]).astype(jnp.int32)
    rand = rand_blocks.reshape(-1)

    def pick(values, which):
        return lax.dynamic_index_in_dim(values, which, 0, keepdims=False)

    def column(value, which):
        return lax.dynamic_slice_in_dim(value, which * (value.shape[1] // 2), value.shape[1] // 2, 1)

    tie = lax.optimization_barrier

    given = pick(inputs, 1 - y)
    qkv_shard = prepare(
        info, w_qkv, bias_qv, norm_gain, norm_shift, bias_out[None], bias_down[None], bias_up[None]
    )
    bits = bits_of(dp)
    cut = local_len // 2
    chip_a = swap_seq(given[:cut], 2)
    mine = pick(inputs, y)
    first_moves = [swap_dp(qkv_shard, bit) for bit in bits]
    up_out = jnp.concatenate([column(w_up, c), column(w_attn_out, c)], axis=1)
    chip_a, rest, up_out, *first_moves = tie((chip_a, given[cut:], up_out, *first_moves))
    chip_b = swap_seq(rest, 2)
    other_mine = swap_seq(mine, 1)
    held = [(0, qkv_shard)] + list(zip(bits, first_moves))
    if dp == 8:
        held = held + [
            (o ^ bit, swap_dp(part, bit))
            for o, part, bit in (
                (bits[0], first_moves[0], bits[1]),
                (bits[1], first_moves[1], bits[2]),
                (bits[0], first_moves[0], bits[2]),
            )
        ]
    else:
        held = [(0, qkv_shard)]
        for bit in bits:
            held = held + [(o ^ bit, swap_dp(part, bit)) for o, part in held]
    offsets = [offset for offset, _ in held]
    chip_b, other_mine, down_shard, *parts = tie(
        (
            chip_b,
            other_mine,
            lax.dynamic_slice(w_down, (y * (ff_shard // 2), c * half), (ff_shard // 2, half)),
            *[part for _, part in held],
        )
    )
    held = list(zip(offsets, parts))
    if dp == 8:
        offset, part = held[4]
        held = held + [(offset ^ bits[2], swap_dp(part, bits[2]))]
    from_chip = jnp.concatenate([chip_a, chip_b], axis=0)
    other_chip = swap_seq(from_chip, 1)
    offsets = [offset for offset, _ in held]
    pieces = [part for _, part in held]
    up_out = lax.all_gather(up_out, "dp", axis=0, tiled=True)
    down_a = first_bits(down_shard)

    cotangent_chip = swap_seq(pick(out_grad, 1 - y), 2)
    qkv, tokens, full_qkv, norms, bias_up_row = project(
        info, inputs, (from_chip, other_mine, other_chip), pieces, offsets, shard, ff_shard
    )
    near, side = bits[-2:]
    down_a, qkv = tied([down_a], qkv)
    down_b, down_a_side = across(down_a, near), across(down_a, side)
    ctx, lse = attend_forward(info, rand, qkv, 0, 1, pairs)
    down_b, down_a_side, qkv, ctx, lse, cotangent_chip = tied(
        [down_b, down_a_side], qkv, ctx, lse, cotangent_chip
    )
    down_b_side = across(down_b, side)
    down_a = widened([down_a, down_a_side])
    down_a_chip = swap_seq(down_a[1], 2)
    ctx, lse = attend_forward(info, rand, qkv, 1, 1, pairs, (ctx, lse))
    down_b_side, qkv, ctx, lse, down_a_chip, up_out = tied(
        [down_b_side], qkv, ctx, lse, down_a_chip, up_out
    )
    up_other = swap_seq(up_out, 1)
    down_b = widened([down_b, down_b_side])
    down_b_chip = swap_seq(down_b[1], 2)
    down_a_core = swap_seq(down_a[1], 1)
    down_a_both = swap_seq(down_a_chip, 1)
    ctx, lse = attend_forward(info, rand, qkv, 2, pairs - 2, pairs, (ctx, lse))
    ctx, lse, down_b_chip, down_a_core, down_a_both, up_other = tie(
        (ctx, lse, down_b_chip, down_a_core, down_a_both, up_other)
    )
    ctx_other = swap_seq(ctx[own:], 1)
    down_groups = [
        (down_a[0], 0, down_a[1]),
        (down_a[0], 1, down_a_core),
        (down_a[0], 2, down_a_chip),
        (down_a[0], 3, down_a_both),
        (down_b[0], 0, down_b[1]),
        (down_b[0], 1, swap_seq(down_b[1], 1)),
        (down_b[0], 2, down_b_chip),
        (down_b[0], 3, swap_seq(down_b_chip, 1)),
    ]
    cotangent = jnp.concatenate([pick(out_grad, y), cotangent_chip], axis=0)
    (
        out_keep,
        out_send,
        ctx_all,
        normed,
        active,
        hidden_mine,
        hidden_other,
        ffn_mine,
        ffn_other,
        pre_first,
        branch_mine,
        branch_other,
        ctx_grad,
        ctx_send,
        sums,
        up_sums,
    ) = feed_forward(
        info, tokens, ctx, ctx_other, cotangent, up_out, up_other, down_groups, norms, bias_up_row
    )
    ctx_other_grad = swap_seq(ctx_send, 1)

    def grad_of(left, right):
        return dot(left, right, TN)

    up_give = swap_seq(grad_of(normed, hidden_other).astype(bf16), 1)
    down_give = swap_seq(grad_of(active, ffn_other).astype(bf16), 1)
    out_give = swap_seq(grad_of(ctx_all, branch_other).astype(bf16), 1)
    up_grad = (grad_of(normed, hidden_mine) + up_give.astype(f32)).astype(bf16)
    up_sum = lax.psum_scatter(up_grad, "dp", scatter_dimension=0, tiled=True)
    down_grad = (grad_of(active, ffn_mine) + down_give.astype(f32)).astype(bf16)
    out_weight_grad = (grad_of(ctx_all, branch_mine) + out_give.astype(f32)).astype(bf16)
    down_reduce = Reduce(
        jnp.concatenate(
            [down_grad.reshape(dp, ff_shard, half), out_weight_grad.reshape(dp, shard, half)],
            axis=1,
        ),
        index,
        y,
    )
    down_reduce.start()
    ctx_grad, ctx_other_grad, _ = tie((ctx_grad, ctx_other_grad, down_reduce.held))

    proj_a, proj_sums_a = attend_backward(
        info, rand, qkv, ctx_grad, ctx_other_grad, ctx, lse, 0, pairs - 1
    )
    proj_a, ctx_grad, down_reduce.moved = tie((proj_a, ctx_grad, down_reduce.moved))
    down_reduce.step()
    out_home = swap_seq(out_send, 2)
    wide_a = 384 * (pairs - 1)
    grad_a = grad_of(tokens, proj_a).astype(bf16)
    reduce_a = Reduce(grad_a.reshape(dp, shard, wide_a), index, y)
    reduce_a.start()
    weight_a, weight_b = full_qkv[:, :wide_a], full_qkv[:, wide_a:]
    input_a = dot(proj_a, weight_a, NT)
    ctx_grad, input_a, _ = tie((ctx_grad, input_a, reduce_a.held))
    proj_b, proj_sums_b = attend_backward(
        info, rand, qkv, ctx_grad, ctx_other_grad, ctx, lse, pairs - 1, 1
    )
    proj_b, reduce_a.moved, down_reduce.moved, out_home = tie(
        (proj_b, reduce_a.moved, down_reduce.moved, out_home)
    )
    output = home_rows(info, [out_home], 1, (out_keep,))
    while len(down_reduce.bits) > 1:
        down_reduce.step()
    while len(reduce_a.bits) > 2:
        reduce_a.step()

    def input_part(start, rows):
        return input_a[start : start + rows] + dot(proj_b[start : start + rows], weight_b, NT)

    give_send = swap_seq(input_part(own + local_len, local_len).astype(bf16), 1)
    give_keep = swap_seq(input_part(own, local_len).astype(bf16), 1)
    grad_b = grad_of(tokens, proj_b).astype(bf16)
    proj_sums = jnp.concatenate([proj_sums_a, proj_sums_b])[:, 0].reshape(pairs, 3, 128)
    my_sums = jnp.stack([proj_sums[:, 0].reshape(-1), proj_sums[:, 2].reshape(-1)])
    bias_qv_grad = lax.dynamic_update_slice(
        jnp.zeros((2, width), f32), my_sums, (jnp.int32(0), c * half)
    )

    rows = jnp.concatenate([bias_qv_grad, sums[2:6], sums[0:2]], axis=0)
    rows = rows.reshape(8, dp, shard).transpose(1, 0, 2)
    small_rows = 16
    small_grads = jnp.concatenate(
        [
            jnp.pad(rows, ((0, 0), (0, 0), (0, 384 - shard))),
            jnp.pad(up_sums[0].reshape(dp, 1, ff_shard), ((0, 0), (0, 7), (0, 384 - ff_shard))),
        ],
        axis=1,
    ).astype(bf16)
    reduce_b = Reduce(
        jnp.concatenate(
            [grad_b.reshape(dp, shard, 384), small_grads], axis=1
        ),
        index,
        y,
    )
    reduce_b.start()
    own_send = pre_first[local_len:] + input_part(local_len, local_len)
    own_keep = pre_first[:local_len] + input_part(0, local_len)
    (
        give_send,
        give_keep,
        own_send,
        own_keep,
        reduce_a.moved,
        reduce_b.moved,
        down_reduce.moved,
        up_sum,
        output,
    ) = tie(
        (
            give_send,
            give_keep,
            own_send,
            own_keep,
            reduce_a.moved,
            reduce_b.moved,
            down_reduce.moved,
            up_sum,
            output,
        )
    )
    grad_send = (own_send + give_send.astype(f32)).astype(bf16)
    moved_a = swap_seq(grad_send[:cut], 2)
    while len(reduce_b.bits) > 2:
        reduce_b.step()
    down_reduce.step()
    up_moved = swap_seq(up_sum, 2)
    reduce_a.add()
    grad_inputs = home_rows(info, [(own_keep + give_keep.astype(f32)).astype(bf16)], 0)
    (
        moved_a,
        grad_rest,
        reduce_a.held,
        reduce_b.moved,
        down_reduce.moved,
        up_moved,
        grad_inputs,
    ) = tie(
        (
            moved_a,
            grad_send[cut:],
            reduce_a.held,
            reduce_b.moved,
            down_reduce.moved,
            up_moved,
            grad_inputs,
        )
    )
    moved_b = swap_seq(grad_rest, 2)
    reduce_b.add()
    down_reduce.add()
    mine, moves = exchange_four(
        jnp.concatenate(
            [reduce_a.held[:, :, k * 384 : (k + 1) * 384] for k in range(pairs - 1)]
            + [reduce_b.held],
            axis=1,
        ),
        index,
    )
    up_shard = (up_sum.astype(f32) + up_moved.astype(f32)).astype(bf16)
    mine, up_shard, down_held, moved_b, *moves = tie(
        (mine, up_shard, down_reduce.held[0], moved_b, *moves)
    )
    up_shard_other = swap_seq(up_shard, 1)
    total = mine.astype(f32)
    for part in moves:
        total = total + part.astype(f32)
    last = jnp.concatenate([down_held, total.astype(bf16)], axis=0)
    last_chip = swap_seq(last, 2)
    (grad_up,) = widen(
        info,
        [up_shard[None], up_shard_other[None]],
        [(which, 0, 0, shard, 0, middle, 0, 0, 0, middle, which) for which in (0, 1)],
        [(shard, hidden_width)],
    )
    grad_inputs = home_rows(info, [moved_a, moved_b], 1, (grad_inputs,))
    last_chip, grad_up, grad_inputs = tie((last_chip, grad_up, grad_inputs))
    last = jnp.where(y == 0, jnp.stack([last, last_chip]), jnp.stack([last_chip, last]))

    plan = []
    part_rows = (ff_shard + shard) // 2
    few = shard // 2
    b_rows = (shard + small_rows) // 2
    for which in (0, 1):
        for slot in (0, 1):

            def put(row, count, out, out_row, base, stride, column=0, wide=384):
                if count > 0:
                    plan.append(
                        (which, slot, row, count, column, wide, out, out_row, base, stride, which)
                    )

            low, high = slot * part_rows, (slot + 1) * part_rows
            cutoff = min(high, ff_shard)
            put(0, cutoff - low, 2, low, 0, half)
            put(cutoff - low, high - cutoff, 1, cutoff - ff_shard, 0, half)
            for pair in range(pairs):
                for kind in range(3):
                    base = kind * width + pair * 128
                    if pair < pairs - 1:
                        row, count, out_row = part_rows + pair * few, few, slot * few
                    else:
                        row, out_row = part_rows + (pairs - 1) * few, slot * b_rows
                        count = min(b_rows, shard - out_row)
                    put(row, count, 0, out_row, base, half, kind * 128, 128)
            start = part_rows + (pairs - 1) * few
            first = max(shard - slot * b_rows, 0)
            put(start + first, b_rows - first, 3, slot * b_rows + first - shard, 0, 384)
    grad_qkv, grad_out, grad_down, small_sums = widen(
        info,
        [last, swap_seq(last, 1)],
        plan,
        [(shard, 3 * width), (shard, width), (ff_shard, width), (small_rows, 2 * 384)],
    )
    small_sums = small_sums[:, :384] + small_sums[:, 384:]

    return (
        output,
        grad_inputs,
        grad_qkv,
        grad_out,
        grad_up,
        grad_down,
        small_sums[0:2, :shard],
        small_sums[6, :shard],
        small_sums[8, :ff_shard],
        small_sums[7, :shard],
        small_sums[2:4, :shard],
        small_sums[4:6, :shard],
    )


def solution(mesh):
    in_specs = (
        P("dp", "seq", None),
        P("dp", "seq", None),
        P("dp", None),
        P("dp", None),
        P("dp", None),
        P("dp", None),
        P(None, "dp"),
        P("dp"),
        P("dp"),
        P("dp"),
        P(None, "dp"),
        P(None, "dp"),
        P(),
    )
    out_specs = (
        P("dp", "seq", None),
        P("dp", "seq", None),
        P("dp", None),
        P("dp", None),
        P("dp", None),
        P("dp", None),
        P(None, "dp"),
        P("dp"),
        P("dp"),
        P("dp"),
        P(None, "dp"),
        P(None, "dp"),
    )
    return jax.shard_map(body, mesh=mesh, in_specs=in_specs, out_specs=out_specs, check_vma=False)
```

```python
import functools

import jax
import jax.numpy as jnp
from jax import lax
from jax.experimental import pallas as pl
from jax.experimental.pallas import tpu as pltpu
from jax.sharding import PartitionSpec as P

HEADS = 12
HEAD_DIM = 64
BLOCK = 64
RAND = 3

norm_eps = 1e-06
bf16 = jnp.bfloat16
f32 = jnp.float32
NN = (((1,), (0,)), ((), ()))
NT = (((1,), (1,)), ((), ()))
TN = (((0,), (0,)), ((), ()))
VMEM_BYTES = 60 << 20


def dot(a, b, dims=NN):
    return lax.dot_general(a, b, dims, preferred_element_type=f32)


def row_of(block, y, c, chunk_blocks):
    chunk = block // chunk_blocks
    place = (((chunk & 1) ^ c) << 1) | ((chunk >> 1) ^ y)
    return pl.multiple_of((place * chunk_blocks + block % chunk_blocks) * BLOCK, BLOCK)


class Rows:
    def __init__(self, info_ref, rand_ref, first_pair, nblocks):
        self.y, self.c = info_ref[0], info_ref[1]
        self.rand_ref = rand_ref
        self.nblocks = nblocks
        self.head = self.c * info_ref[2] + 2 * first_pair
        self.low = lax.broadcasted_iota(jnp.int32, (BLOCK, 128), 1) < HEAD_DIM
        self.low_row = lax.broadcasted_iota(jnp.int32, (1, 128), 1) < HEAD_DIM

    def at(self, block):
        return pl.ds(row_of(block, self.y, self.c, self.nblocks // 4), BLOCK)

    def two(self, tile):
        zero = jnp.zeros_like(tile)
        return jnp.concatenate(
            [jnp.where(self.low, tile, zero), jnp.where(self.low, zero, tile)], axis=0
        )

    def one(self, both):
        return jnp.where(self.low, both[:BLOCK], both[BLOCK:])

    def rand(self, i):
        middle = self.nblocks - 2
        base = (self.head * middle + (i - 1)) * RAND
        return [
            (self.rand_ref[base + t], self.rand_ref[base + middle * RAND + t]) for t in range(RAND)
        ]

    def near(self, load, ends, i, rand):
        mixed = [jnp.where(self.low, load(a), load(b)) for a, b in rand]
        return jnp.concatenate([ends, load(i - 1), load(i + 1), load(i)] + mixed, axis=0)

    def mask(self, scores, i):
        first = jnp.where(i == 1, -1e30, 0.0)
        last = jnp.where(i == self.nblocks - 2, -1e30, 0.0)
        bias = jnp.where(self.low_row, first, last).astype(f32)
        return jnp.concatenate(
            [scores[:, :128], scores[:, 128:256] + bias, scores[:, 256:]], axis=1
        )


def forward_kernel(info_ref, rand_ref, qkv_ref, *refs, nblocks, first, unroll):
    ctx_ref, lse_ref = refs[-2:]
    rows = Rows(info_ref, rand_ref, pl.program_id(0) + first, nblocks)

    def load(block, column):
        return qkv_ref[rows.at(block), column * 128 : (column + 1) * 128]

    def finish(block, scores, values):
        peak = jnp.max(scores, axis=1, keepdims=True)
        powers = jnp.exp(scores - peak).astype(bf16)
        both = dot(powers, jnp.concatenate([values, jnp.ones_like(values)], axis=1))
        totals = both[:, 128:]
        lse = peak + jnp.log(totals)
        ctx_ref[rows.at(block), :] = rows.one(both[:, :128] / totals).astype(bf16)
        lse_ref[rows.at(block), :128] = lse[:BLOCK]
        lse_ref[rows.at(block), 128:] = lse[BLOCK:]

    for edge in (0, nblocks - 1):
        scores = dot(rows.two(load(edge, 0)), qkv_ref[:, 128:256], NT)
        finish(edge, scores, qkv_ref[:, 256:384])
    key_ends = jnp.concatenate([load(0, 1), load(nblocks - 1, 1)], axis=0)
    value_ends = jnp.concatenate([load(0, 2), load(nblocks - 1, 2)], axis=0)

    def row(i):
        rand = rows.rand(i)
        keys = rows.near(lambda b: load(b, 1), key_ends, i, rand)
        values = rows.near(lambda b: load(b, 2), value_ends, i, rand)
        finish(i, rows.mask(dot(rows.two(load(i, 0)), keys, NT), i), values)

    def step(t, carry):
        for u in range(unroll):
            row(1 + t * unroll + u)
        return carry

    lax.fori_loop(0, (nblocks - 2) // unroll, step, 0)


def backward_kernel(
    info_ref, rand_ref, qkv_ref, own_ref, other_ref, ctx_ref, lse_ref, out_ref, sum_ref,
    key_sum, value_sum, grad_ref,
    *, nblocks, first, unroll
):
    rows = Rows(info_ref, rand_ref, pl.program_id(0) + first, nblocks)
    zero = jnp.zeros((BLOCK, 128), f32)
    half_rows = own_ref.shape[0]
    grad_ref[:half_rows] = own_ref[...]
    grad_ref[half_rows:] = other_ref[...]

    def load(block, column):
        return qkv_ref[rows.at(block), column * 128 : (column + 1) * 128]

    ones = jnp.ones((256, 128), bf16)

    def finish(block, scores, keys, values):
        grad = grad_ref[rows.at(block), :]
        both = grad.astype(f32) * ctx_ref[rows.at(block), :].astype(f32)
        high = both.astype(bf16)
        rest = (both - high.astype(f32)).astype(bf16)
        row_dot = dot(jnp.concatenate([rows.two(high), rows.two(rest)], axis=1), ones)
        lse = jnp.concatenate(
            [lse_ref[rows.at(block), :128], lse_ref[rows.at(block), 128:]], axis=0
        )
        grad = rows.two(grad)
        attn_grad = dot(grad, values, NT)
        attention, score_grad = [], []
        for k in range(scores.shape[1] // 128):
            part = slice(k * 128, (k + 1) * 128)
            probs = jnp.exp(scores[:, part] - lse)
            score_grad.append((probs * (attn_grad[:, part] - row_dot)).astype(bf16))
            attention.append(probs.astype(bf16))
        attention = jnp.concatenate(attention, axis=1)
        score_grad = jnp.concatenate(score_grad, axis=1)
        query_grad = dot(score_grad, keys) * HEAD_DIM ** (-0.5)
        out_ref[rows.at(block), 0:128] = rows.one(query_grad).astype(bf16)
        return grad, attention, score_grad

    for edge in (0, nblocks - 1):
        query = rows.two(load(edge, 0))
        keys, values = qkv_ref[:, 128:256], qkv_ref[:, 256:384]
        grad, attention, score_grad = finish(edge, dot(query, keys, NT), keys, values)
        if edge == 0:
            key_sum[...] = dot(score_grad, query, TN)
            value_sum[...] = dot(attention, grad, TN)
        else:
            key_sum[...] += dot(score_grad, query, TN)
            value_sum[...] += dot(attention, grad, TN)
    key_ends = jnp.concatenate([load(0, 1), load(nblocks - 1, 1)], axis=0)
    value_ends = jnp.concatenate([load(0, 2), load(nblocks - 1, 2)], axis=0)

    def row(i):
        rand = rows.rand(i)
        keys = rows.near(lambda b: load(b, 1), key_ends, i, rand)
        values = rows.near(lambda b: load(b, 2), value_ends, i, rand)
        query = rows.two(load(i, 0))
        scores = rows.mask(dot(query, keys, NT), i)
        grad, attention, score_grad = finish(i, scores, keys, values)
        for total, part in (
            (key_sum, dot(score_grad, query, TN)),
            (value_sum, dot(attention, grad, TN)),
        ):
            for slot, block in enumerate((0, nblocks - 1, i - 1, i + 1, i)):
                total[rows.at(block), :] += part[slot * BLOCK : (slot + 1) * BLOCK]
            for slot, (a, b) in enumerate(rand):
                tile = part[(5 + slot) * BLOCK : (6 + slot) * BLOCK]
                total[rows.at(a), :] += jnp.where(rows.low, tile, zero)
                total[rows.at(b), :] += jnp.where(rows.low, zero, tile)

    def step(t, carry):
        for u in range(unroll):
            row(1 + t * unroll + u)
        return carry

    lax.fori_loop(0, (nblocks - 2) // unroll, step, 0)
    out_ref[:, 128:256] = key_sum[...].astype(bf16)
    out_ref[:, 256:384] = value_sum[...].astype(bf16)
    sum_ref[0] = jnp.broadcast_to(
        jnp.sum(out_ref[...].astype(f32), axis=0, keepdims=True), (8, 384)
    )


def attend_forward(info, rand, qkv, first, pairs, total, into=()):
    length = qkv.shape[0]
    wide = pl.BlockSpec((length, 384), lambda p, *_: (0, p + first))
    slim = pl.BlockSpec((length, 128), lambda p, *_: (0, p + first))
    twin = pl.BlockSpec((length, 256), lambda p, *_: (0, p + first))
    return pl.pallas_call(
        functools.partial(forward_kernel, nblocks=length // BLOCK, first=first, unroll=10),
        grid_spec=pltpu.PrefetchScalarGridSpec(
            num_scalar_prefetch=2,
            grid=(pairs,),
            in_specs=[wide] + [pl.BlockSpec(memory_space=pl.ANY)] * len(into),
            out_specs=[slim, twin],
        ),
        out_shape=[
            jax.ShapeDtypeStruct((length, total * 128), bf16),
            jax.ShapeDtypeStruct((length, total * 256), f32),
        ],
        input_output_aliases={3 + k: k for k in range(len(into))},
        compiler_params=pltpu.CompilerParams(vmem_limit_bytes=VMEM_BYTES),
        name="attend_forward",
    )(info, rand, qkv, *into)


def attend_backward(info, rand, qkv, own_grad, other_grad, ctx, lse, first, pairs):
    length = qkv.shape[0]
    wide = pl.BlockSpec((length, 384), lambda p, *_: (0, p + first))
    slim = pl.BlockSpec((length, 128), lambda p, *_: (0, p + first))
    part = pl.BlockSpec((length // 2, 128), lambda p, *_: (0, p + first))
    twin = pl.BlockSpec((length, 256), lambda p, *_: (0, p + first))
    return pl.pallas_call(
        functools.partial(backward_kernel, nblocks=length // BLOCK, first=first, unroll=6),
        grid_spec=pltpu.PrefetchScalarGridSpec(
            num_scalar_prefetch=2,
            grid=(pairs,),
            in_specs=[wide, part, part, slim, twin],
            out_specs=[
                pl.BlockSpec((length, 384), lambda p, *_: (0, p)),
                pl.BlockSpec((1, 8, 384), lambda p, *_: (p, 0, 0)),
            ],
            scratch_shapes=[pltpu.VMEM((length, 128), f32)] * 2 + [pltpu.VMEM((length, 128), bf16)],
        ),
        out_shape=[
            jax.ShapeDtypeStruct((length, pairs * 384), bf16),
            jax.ShapeDtypeStruct((pairs, 8, 384), f32),
        ],
        compiler_params=pltpu.CompilerParams(vmem_limit_bytes=VMEM_BYTES),
        name="attend_backward",
    )(info, rand, qkv, own_grad, other_grad, ctx, lse)


def swap_dp(value, bit):
    size = lax.axis_size("dp")
    return lax.ppermute(value, "dp", [(i, i ^ bit) for i in range(size)])


def swap_seq(value, bit):
    size = lax.axis_size("seq")
    return lax.ppermute(value, "seq", [(i, i ^ bit) for i in range(size)])


def bits_of(size):
    return [size >> (k + 1) for k in range(size.bit_length() - 1)]


def widened(blocks):
    return sum((o for o, _ in blocks), []), jnp.concatenate([a for _, a in blocks], axis=0)


def across(block, bit):
    offsets, array = block
    return [offset ^ bit for offset in offsets], swap_dp(array, bit)


def first_bits(shard):
    block = ([0], shard[None])
    for bit in bits_of(lax.axis_size("dp"))[:-3]:
        block = widened([block, across(block, bit)])
    return block


def tied(blocks, *values):
    arrays = lax.optimization_barrier((*[array for _, array in blocks], *values))
    count = len(blocks)
    return [(blocks[k][0], arrays[k]) for k in range(count)] + list(arrays[count:])


class Reduce:
    def __init__(self, parts, index, y):
        count, rows, columns = parts.shape
        self.held, self.index, self.y = parts.reshape(count, 2, rows // 2, columns), index, y
        self.bits = [0] + bits_of(lax.axis_size("dp"))[::-1]

    def start(self):
        bit = self.bits.pop(0)
        if bit:
            view = self.held.reshape(-1, 2, *self.held.shape[1:])
            mine = (self.index // bit) % 2
        else:
            view, mine = self.held, self.y
        self.held = lax.dynamic_slice_in_dim(view, mine, 1, 1)[:, 0]
        give = lax.dynamic_slice_in_dim(view, 1 - mine, 1, 1)[:, 0]
        self.moved = swap_dp(give, bit) if bit else swap_seq(give, 2)

    def add(self):
        self.held = (self.held.astype(f32) + self.moved.astype(f32)).astype(bf16)

    def step(self):
        self.add()
        self.start()


def exchange_four(held, index):
    unit = lax.axis_size("dp") // 4
    me = index // unit
    mine = lax.dynamic_index_in_dim(held, me, 0, keepdims=False)
    moved = [
        swap_dp(lax.dynamic_index_in_dim(held, me ^ k, 0, keepdims=False), k * unit)
        for k in (1, 2, 3)
    ]
    return mine, moved


def prepare_kernel(info_ref, w_ref, qv_ref, gain_ref, shift_ref, out_ref, down_ref, up_ref, shard_ref):
    c = info_ref[1]
    third = w_ref.shape[1] // 3
    half = third // 2
    depth, few = qv_ref.shape[1], up_ref.shape[1]
    for kind in range(3):
        columns = pl.ds(pl.multiple_of(kind * third + c * half, 128), half)
        part = w_ref[:, columns]
        for pair in range(half // 128):
            at = (pair * 3 + kind) * 128
            shard_ref[0:depth, at : at + 128] = part[:, pair * 128 : (pair + 1) * 128]
    shard_ref[depth:] = jnp.zeros((8, 3 * half), bf16)
    shard_ref[depth : depth + 2, 0:depth] = qv_ref[...]
    shard_ref[depth + 2 : depth + 4, 0:depth] = gain_ref[...]
    shard_ref[depth + 4 : depth + 6, 0:depth] = shift_ref[...]
    shard_ref[depth + 6 : depth + 7, 0:depth] = out_ref[...]
    shard_ref[depth + 7 : depth + 8, 0:depth] = down_ref[...]
    shard_ref[depth : depth + 1, 128 : 128 + few] = up_ref[...]


def prepare(info, w_qkv, *small):
    depth, columns = w_qkv.shape
    arrays = (w_qkv, *small)
    return pl.pallas_call(
        prepare_kernel,
        grid_spec=pltpu.PrefetchScalarGridSpec(
            num_scalar_prefetch=1,
            grid=(1,),
            in_specs=[pl.BlockSpec(a.shape, lambda i, *_: (0, 0)) for a in arrays],
            out_specs=pl.BlockSpec((depth + 8, columns // 2), lambda i, *_: (0, 0)),
        ),
        out_shape=jax.ShapeDtypeStruct((depth + 8, columns // 2), bf16),
        compiler_params=pltpu.CompilerParams(vmem_limit_bytes=VMEM_BYTES),
        name="prepare",
    )(info, *arrays)


def project_kernel(info_ref, inputs_ref, *refs, offsets, shard, ff_shard):
    more, refs = refs[:3], refs[3:]
    pieces, refs = refs[: len(offsets)], refs[len(offsets) :]
    qkv_ref, tokens_ref, weight_ref, norms_ref, up_ref, bias_ref = refs
    step = pl.program_id(0)
    width = weight_ref.shape[0]
    half = width // 2

    def spread(part, size, target, at):
        shape = (part.shape[1], target)
        lane = lax.broadcasted_iota(jnp.int32, shape, 1) - at
        source = lax.broadcasted_iota(jnp.int32, shape, 0)
        return dot(part, jnp.where((lane == source) & (source < size), 1.0, 0.0).astype(bf16))

    @pl.when(step == 0)
    def _():
        norms = jnp.zeros((8, width), f32)
        for offset, piece in zip(offsets, pieces):
            place = info_ref[4] ^ offset
            at = pl.ds(pl.multiple_of(place * shard, 8), shard)
            weight_ref[at, :] = piece[0:shard]
            tail = piece[shard : shard + 8]
            norms = norms + spread(tail[:, :128], shard, width, place * shard)
            if ff_shard % 128 == 0:
                lanes = pl.ds(pl.multiple_of(place * ff_shard, 128), ff_shard)
                up_ref[:, lanes] = tail[:, 128 : 128 + ff_shard].astype(f32)
            else:
                part = spread(tail[:, 128:256], ff_shard, up_ref.shape[1], place * ff_shard)
                if offset == offsets[0]:
                    up_ref[...] = part
                else:
                    up_ref[...] += part
        norms_ref[...] = norms
        bias_ref[...] = jnp.zeros_like(bias_ref)
        for pair in range(half // 128):
            lanes = pl.ds(pl.multiple_of(info_ref[1] * half + pair * 128, 128), 128)
            bias_ref[0:1, pair * 384 : pair * 384 + 128] = norms_ref[0:1, lanes]
            bias_ref[0:1, pair * 384 + 256 : pair * 384 + 384] = norms_ref[1:2, lanes]
        tokens_ref[...] = inputs_ref[0]

    for k in range(3):

        @pl.when(step == k + 1)
        def _():
            tokens_ref[...] = more[k][...]

    wide = dot(tokens_ref[...], weight_ref[...]) + bias_ref[0:1]
    for pair in range(wide.shape[1] // 384):
        at = pair * 384
        query = wide[:, at : at + 128].astype(bf16).astype(f32) * HEAD_DIM ** (-0.5)
        qkv_ref[:, at : at + 128] = query.astype(bf16)
        qkv_ref[:, at + 128 : at + 384] = wide[:, at + 128 : at + 384].astype(bf16)


def project(info, inputs, more, pieces, offsets, shard, ff_shard):
    _, local_len, width = inputs.shape
    columns = pieces[0].shape[1]
    hidden = ff_shard * len(pieces)

    def whole(array):
        return pl.BlockSpec(array.shape, lambda i, *_: (0, 0), pipeline_mode=pl.Buffered(1))

    fixed = [((width, columns), bf16), ((8, width), f32), ((8, hidden), f32)]
    return pl.pallas_call(
        functools.partial(project_kernel, offsets=offsets, shard=shard, ff_shard=ff_shard),
        grid_spec=pltpu.PrefetchScalarGridSpec(
            num_scalar_prefetch=1,
            grid=(4,),
            in_specs=[pl.BlockSpec((1, local_len, width), lambda i, info: (info[0], 0, 0))]
            + [whole(array) for array in (*more, *pieces)],
            out_specs=[
                pl.BlockSpec((local_len, columns), lambda i, *_: (i, 0)),
                pl.BlockSpec((local_len, width), lambda i, *_: (i, 0)),
            ]
            + [pl.BlockSpec(shape, lambda i, *_: (0, 0)) for shape, _ in fixed],
            scratch_shapes=[pltpu.VMEM((8, columns), f32)],
        ),
        out_shape=[
            jax.ShapeDtypeStruct((4 * local_len, columns), bf16),
            jax.ShapeDtypeStruct((4 * local_len, width), bf16),
        ]
        + [jax.ShapeDtypeStruct(shape, kind) for shape, kind in fixed],
        compiler_params=pltpu.CompilerParams(vmem_limit_bytes=VMEM_BYTES),
        name="project",
    )(info, inputs, *more, *pieces)


CHUNK = 768


def gelu_pair(values):
    square = values * values
    inner = values * (0.7978845608028654 + 0.7978845608028654 * 0.044715 * square)
    gate = 0.5 + 0.5 * jnp.tanh(inner)
    active = values * gate
    slope = 2 * 0.7978845608028654 + 6 * 0.7978845608028654 * 0.044715 * square
    return active, gate + (active - active * gate) * slope


def norm_parts(values):
    center = values - jnp.mean(values, axis=-1, keepdims=True)
    spread = jnp.mean(center * center, axis=-1, keepdims=True)
    inverse = lax.rsqrt(spread + norm_eps)
    return center * inverse, inverse


def norm_back(grad, unit, inverse, gain):
    scaled = grad * gain
    return inverse * (
        scaled
        - jnp.mean(scaled, axis=-1, keepdims=True)
        - unit * jnp.mean(scaled * unit, axis=-1, keepdims=True)
    )


def middle_kernel(
    info_ref,
    tokens_ref,
    ctx_ref,
    ctx_other_ref,
    cotangent_ref,
    up_ref,
    up_other_ref,
    *refs,
    down_plan,
    steps,
):
    n_down = 1 + max(entry[0] for entry in down_plan)
    down_refs, refs = refs[:n_down], refs[n_down:]
    (
        norm_ref,
        bias_up_ref,
        keep_ref,
        send_ref,
        ctx_all_ref,
        normed_ref,
        active_ref,
        hidden_mine_ref,
        hidden_other_ref,
        ffn_mine_ref,
        ffn_other_ref,
        first_ref,
        branch_mine_ref,
        branch_other_ref,
        ctx_grad_ref,
        ctx_send_ref,
        sums_ref,
        up_sums_ref,
        down_all,
        out_all,
        change_all,
        wide,
    ) = refs
    c, index, flip = info_ref[1], info_ref[4], info_ref[5]
    step = pl.program_id(0)
    half = ctx_ref.shape[1]
    middle = up_ref.shape[1] - half
    hidden = 2 * middle

    def up_part(k):
        inside = k * CHUNK % middle
        return (up_ref if k * CHUNK < middle else up_other_ref)[:, inside : inside + CHUNK]

    def lanes(which, size):
        return pl.ds(pl.multiple_of(which * size, 128), size)

    def rows(which, size):
        return pl.ds(pl.multiple_of(which * size, 16), size)

    @pl.when(step == 0)
    def _():
        out_all[:, lanes(c, half)] = up_ref[:, middle:]
        out_all[:, lanes(1 - c, half)] = up_other_ref[:, middle:]
        for source, slot, offset, which in down_plan:
            size = down_refs[source].shape[1]
            block = (index ^ offset ^ flip) * 2 + (info_ref[0] ^ (which // 2))
            down_all[rows(block, size), lanes(c ^ (which % 2), half)] = down_refs[source][slot]
        sums_ref[...] = jnp.zeros_like(sums_ref)
        up_sums_ref[...] = jnp.zeros_like(up_sums_ref)

    bias_out, bias_down = norm_ref[6:7], norm_ref[7:8]
    gain_1, gain_2, shift_1, shift_2 = (norm_ref[k : k + 1] for k in (2, 3, 4, 5))
    ctx_all_ref[:, lanes(c, half)] = ctx_ref[...]
    ctx_all_ref[:, lanes(1 - c, half)] = ctx_other_ref[...]
    branch = dot(ctx_all_ref[...], out_all[...]) + bias_out
    unit_1, inverse_1 = norm_parts(tokens_ref[...].astype(f32) + branch)
    normed = unit_1 * gain_1 + shift_1
    normed_low = normed.astype(bf16)
    normed_ref[...] = normed_low

    total = jnp.zeros_like(branch)
    for k in range(hidden // CHUNK):
        part = slice(k * CHUNK, (k + 1) * CHUNK)
        which = c ^ (k * CHUNK // middle)
        inside = k * CHUNK % middle
        at = pl.ds(pl.multiple_of(which * middle + inside, 128), CHUNK)
        bias = bias_up_ref[0:1, at]
        active, change = gelu_pair(dot(normed_low, up_part(k)) + bias)
        active = active.astype(bf16)
        active_ref[:, at] = active
        change_all[:, part] = change.astype(bf16)
        total = total + dot(active, down_all[part])

    unit_2, inverse_2 = norm_parts(normed + total + bias_down)
    result = (unit_2 * gain_2 + shift_2).astype(bf16)

    @pl.when(step < steps // 2)
    def _():
        keep_ref[0] = result

    @pl.when(step >= steps // 2)
    def _():
        send_ref[...] = result


    cotangent = cotangent_ref[...].astype(f32)
    pre_second = norm_back(cotangent, unit_2, inverse_2, gain_2)
    ffn_grad = pre_second.astype(bf16)
    wide[...] = ffn_grad
    ffn_mine_ref[...] = wide[:, lanes(c, half)]
    ffn_other_ref[...] = wide[:, lanes(1 - c, half)]

    def add(row, values):
        sums_ref[row : row + 1] += jnp.sum(values, axis=0, keepdims=True)

    add(1, ffn_grad.astype(f32))
    add(3, cotangent * unit_2)
    add(5, cotangent)

    total = jnp.zeros_like(branch)
    for k in range(hidden // CHUNK):
        part = slice(k * CHUNK, (k + 1) * CHUNK)
        grad = (dot(ffn_grad, down_all[part], NT) * change_all[:, part]).astype(bf16)
        target = hidden_mine_ref if k * CHUNK < middle else hidden_other_ref
        inside = k * CHUNK % middle
        target[:, inside : inside + CHUNK] = grad
        which = c ^ (k * CHUNK // middle)
        at = pl.ds(pl.multiple_of(which * middle + inside, 128), CHUNK)
        up_sums_ref[0:1, at] += jnp.sum(grad.astype(f32), axis=0, keepdims=True)
        total = total + dot(grad, up_part(k), NT)

    normed_grad = pre_second + total
    pre_first = norm_back(normed_grad, unit_1, inverse_1, gain_1)
    first_ref[...] = pre_first
    branch_grad = pre_first.astype(bf16)
    wide[...] = branch_grad
    branch_mine_ref[...] = wide[:, lanes(c, half)]
    branch_other_ref[...] = wide[:, lanes(1 - c, half)]
    add(0, branch_grad.astype(f32))
    add(2, normed_grad * unit_1)
    add(4, normed_grad)
    ctx_grad = dot(branch_grad, out_all[...], NT).astype(bf16)
    wide[...] = ctx_grad
    ctx_grad_ref[...] = wide[:, lanes(c, half)]
    ctx_send_ref[...] = wide[:, lanes(1 - c, half)]


def feed_forward(info, tokens, ctx, ctx_other, cotangent, up, up_other, down_groups, norms, bias_up):
    count, width = cotangent.shape
    half = ctx.shape[1]
    middle = up.shape[1] - half
    hidden = 2 * middle
    tile = 256
    steps = count // tile
    arrays, plan = [], []
    for offsets, which, array in down_groups:
        for slot, offset in enumerate(offsets):
            plan.append((len(arrays), slot, offset, which))
        arrays.append(array)

    def tiled(columns):
        return pl.BlockSpec((tile, columns), lambda i, *_: (i, 0))

    def whole(array):
        rank = len(array.shape)
        return pl.BlockSpec(
            array.shape, lambda i, *_: (0,) * rank, pipeline_mode=pl.Buffered(1)
        )

    outs = [
        ((count, width), bf16),
        ((count, width), bf16),
        ((count, hidden), bf16),
        ((count, middle), bf16),
        ((count, middle), bf16),
        ((count, half), bf16),
        ((count, half), bf16),
        ((count, width), f32),
        ((count, half), bf16),
        ((count, half), bf16),
        ((count, half), bf16),
        ((count, half), bf16),
    ]
    sums = [((8, width), f32), ((8, hidden), f32)]
    return pl.pallas_call(
        functools.partial(middle_kernel, down_plan=plan, steps=steps),
        grid_spec=pltpu.PrefetchScalarGridSpec(
            num_scalar_prefetch=1,
            grid=(steps,),
            in_specs=[tiled(width), tiled(half), tiled(half), tiled(width), whole(up), whole(up_other)]
            + [whole(array) for array in arrays]
            + [whole(norms), whole(bias_up)],
            out_specs=[
                pl.BlockSpec(
                    (1, tile, width), lambda i, info: (info[0], jnp.minimum(i, steps // 2 - 1), 0)
                ),
                pl.BlockSpec((tile, width), lambda i, *_: (jnp.maximum(i - steps // 2, 0), 0)),
            ]
            + [tiled(shape[1]) for shape, _ in outs]
            + [pl.BlockSpec(shape, lambda i, *_: (0, 0)) for shape, _ in sums],
            scratch_shapes=[
                pltpu.VMEM((hidden, width), bf16),
                pltpu.VMEM((width, width), bf16),
                pltpu.VMEM((tile, hidden), bf16),
                pltpu.VMEM((tile, width), bf16),
            ],
        ),
        out_shape=[jax.ShapeDtypeStruct((2, count // 2, width), bf16)]
        + [jax.ShapeDtypeStruct((count // 2, width), bf16)]
        + [jax.ShapeDtypeStruct(shape, kind) for shape, kind in outs + sums],
        compiler_params=pltpu.CompilerParams(vmem_limit_bytes=VMEM_BYTES),
        name="feed_forward",
    )(info, tokens, ctx, ctx_other, cotangent, up, up_other, *arrays, norms, bias_up)


def home_kernel(info_ref, *refs, count):
    start = 0
    for ref in refs[:count]:
        refs[-1][0, start : start + ref.shape[0]] = ref[...]
        start += ref.shape[0]


def home_rows(info, pieces, which, into=()):
    rows = sum(piece.shape[0] for piece in pieces)
    width = pieces[0].shape[1]
    return pl.pallas_call(
        functools.partial(home_kernel, count=len(pieces)),
        grid_spec=pltpu.PrefetchScalarGridSpec(
            num_scalar_prefetch=1,
            grid=(1,),
            in_specs=[pl.BlockSpec(piece.shape, lambda i, *_: (0, 0)) for piece in pieces]
            + [pl.BlockSpec(memory_space=pl.ANY)] * len(into),
            out_specs=pl.BlockSpec((1, rows, width), lambda i, info: (info[0] ^ which, 0, 0)),
        ),
        out_shape=jax.ShapeDtypeStruct((2, rows, width), bf16),
        input_output_aliases={1 + len(pieces): 0} if into else {},
        name="home_rows",
    )(info, *pieces, *into)


def widen_kernel(info_ref, *refs, plan, n_in):
    ins, outs = refs[:n_in], refs[n_in:]
    c = info_ref[1]
    for source, slot, row, rows, column, width, out, out_row, base, stride, which in plan:
        at = pl.ds(pl.multiple_of(base + (c ^ which) * stride, 128), width)
        outs[out][out_row : out_row + rows, at] = ins[source][
            slot, row : row + rows, column : column + width
        ].astype(f32)


def widen(info, arrays, plan, shapes):
    return pl.pallas_call(
        functools.partial(widen_kernel, plan=plan, n_in=len(arrays)),
        grid_spec=pltpu.PrefetchScalarGridSpec(
            num_scalar_prefetch=1,
            grid=(1,),
            in_specs=[pl.BlockSpec(a.shape, lambda i, *_: (0, 0, 0)) for a in arrays],
            out_specs=[pl.BlockSpec(shape, lambda i, *_: (0, 0)) for shape in shapes],
        ),
        out_shape=[jax.ShapeDtypeStruct(shape, f32) for shape in shapes],
        compiler_params=pltpu.CompilerParams(vmem_limit_bytes=VMEM_BYTES),
        name="widen",
    )(info, *arrays)


def body(
    inputs,
    out_grad,
    w_qkv,
    w_attn_out,
    w_up,
    w_down,
    bias_qv,
    bias_out,
    bias_up,
    bias_down,
    norm_gain,
    norm_shift,
    rand_blocks,
):
    _, local_len, width = inputs.shape
    dp = lax.axis_size("dp")
    index = lax.axis_index("dp")
    seat = lax.axis_index("seq")
    y, c = seat // 2, seat % 2
    heads_here = HEADS // 2
    pairs = heads_here // 2
    half = width // 2
    hidden_width = w_up.shape[1]
    middle = hidden_width // 2
    own = 2 * local_len
    shard = width // dp
    ff_shard = hidden_width // dp
    qkv_width = 3 * half
    flip = c * (dp // 2)
    info = jnp.stack([y, c, jnp.int32(heads_here), jnp.int32(0), index, flip]).astype(jnp.int32)
    rand = rand_blocks.reshape(-1)

    def pick(values, which):
        return lax.dynamic_index_in_dim(values, which, 0, keepdims=False)

    def column(value, which):
        return lax.dynamic_slice_in_dim(value, which * (value.shape[1] // 2), value.shape[1] // 2, 1)

    tie = lax.optimization_barrier

    given = pick(inputs, 1 - y)
    qkv_shard = prepare(
        info, w_qkv, bias_qv, norm_gain, norm_shift, bias_out[None], bias_down[None], bias_up[None]
    )
    bits = bits_of(dp)
    cut = local_len // 2
    chip_a = swap_seq(given[:cut], 2)
    mine = pick(inputs, y)
    first_moves = [swap_dp(qkv_shard, bit) for bit in bits]
    up_out = jnp.concatenate([column(w_up, c), column(w_attn_out, c)], axis=1)
    other_mine = swap_seq(mine, 1)
    down_shard = lax.dynamic_slice(w_down, (y * (ff_shard // 2), c * half), (ff_shard // 2, half))
    chip_a, rest, up_out, other_mine, down_shard, *first_moves = tie(
        (chip_a, given[cut:], up_out, other_mine, down_shard, *first_moves)
    )
    down_0 = first_bits(down_shard)
    down_far = across(down_0, bits[-3])
    chip_b = swap_seq(rest, 2)
    held = [(0, qkv_shard)] + list(zip(bits, first_moves))
    if dp == 8:
        held = held + [
            (o ^ bit, swap_dp(part, bit))
            for o, part, bit in (
                (bits[0], first_moves[0], bits[1]),
                (bits[1], first_moves[1], bits[2]),
                (bits[0], first_moves[0], bits[2]),
            )
        ]
    else:
        held = [(0, qkv_shard)]
        for bit in bits:
            held = held + [(o ^ bit, swap_dp(part, bit)) for o, part in held]
    offsets = [offset for offset, _ in held]
    chip_b, cotangent_give, down_moved, *parts = tie(
        (chip_b, out_grad, down_far[1], *[part for _, part in held])
    )
    down_a = widened([down_0, (down_far[0], down_moved)])
    cotangent_chip = swap_seq(pick(cotangent_give, 1 - y), 2)
    held = list(zip(offsets, parts))
    if dp == 8:
        offset, part = held[4]
        held = held + [(offset ^ bits[2], swap_dp(part, bits[2]))]
    from_chip = jnp.concatenate([chip_a, chip_b], axis=0)
    other_chip = swap_seq(from_chip, 1)
    offsets = [offset for offset, _ in held]
    pieces = [part for _, part in held]
    up_out = lax.all_gather(up_out, "dp", axis=0, tiled=True)
    near, side = bits[-2:]
    down_b, down_a_side = across(down_a, near), across(down_a, side)

    qkv, tokens, full_qkv, norms, bias_up_row = project(
        info, inputs, (from_chip, other_mine, other_chip), pieces, offsets, shard, ff_shard
    )
    down_b, down_a_side, qkv, cotangent_chip = tied([down_b, down_a_side], qkv, cotangent_chip)
    down_b_side = across(down_b, side)
    down_a = widened([down_a, down_a_side])
    down_a_chip = swap_seq(down_a[1], 2)
    ctx, lse = attend_forward(info, rand, qkv, 0, 1, pairs)
    down_b_side, qkv, ctx, lse, down_a_chip, up_out = tied(
        [down_b_side], qkv, ctx, lse, down_a_chip, up_out
    )
    up_other = swap_seq(up_out, 1)
    down_b = widened([down_b, down_b_side])
    down_b_chip = swap_seq(down_b[1], 2)
    down_a_core = swap_seq(down_a[1], 1)
    down_a_both = swap_seq(down_a_chip, 1)
    ctx, lse = attend_forward(info, rand, qkv, 1, pairs - 1, pairs, (ctx, lse))
    ctx, lse, down_b_chip, down_a_core, down_a_both, up_other = tie(
        (ctx, lse, down_b_chip, down_a_core, down_a_both, up_other)
    )
    ctx_other = swap_seq(ctx[own:], 1)
    down_groups = [
        (down_a[0], 0, down_a[1]),
        (down_a[0], 1, down_a_core),
        (down_a[0], 2, down_a_chip),
        (down_a[0], 3, down_a_both),
        (down_b[0], 0, down_b[1]),
        (down_b[0], 1, swap_seq(down_b[1], 1)),
        (down_b[0], 2, down_b_chip),
        (down_b[0], 3, swap_seq(down_b_chip, 1)),
    ]
    cotangent = jnp.concatenate([pick(out_grad, y), cotangent_chip], axis=0)
    (
        out_keep,
        out_send,
        ctx_all,
        normed,
        active,
        hidden_mine,
        hidden_other,
        ffn_mine,
        ffn_other,
        pre_first,
        branch_mine,
        branch_other,
        ctx_grad,
        ctx_send,
        sums,
        up_sums,
    ) = feed_forward(
        info, tokens, ctx, ctx_other, cotangent, up_out, up_other, down_groups, norms, bias_up_row
    )
    ctx_other_grad = swap_seq(ctx_send, 1)

    def grad_of(left, right):
        return dot(left, right, TN)

    up_give = swap_seq(grad_of(normed, hidden_other).astype(bf16), 1)
    down_give = swap_seq(grad_of(active, ffn_other).astype(bf16), 1)
    out_give = swap_seq(grad_of(ctx_all, branch_other).astype(bf16), 1)
    up_grad = (grad_of(normed, hidden_mine) + up_give.astype(f32)).astype(bf16)
    up_sum = lax.psum_scatter(up_grad, "dp", scatter_dimension=0, tiled=True)
    down_grad = (grad_of(active, ffn_mine) + down_give.astype(f32)).astype(bf16)
    out_weight_grad = (grad_of(ctx_all, branch_mine) + out_give.astype(f32)).astype(bf16)
    down_reduce = Reduce(
        jnp.concatenate(
            [down_grad.reshape(dp, ff_shard, half), out_weight_grad.reshape(dp, shard, half)],
            axis=1,
        ),
        index,
        y,
    )
    down_reduce.start()
    ctx_grad, ctx_other_grad, _ = tie((ctx_grad, ctx_other_grad, down_reduce.held))

    proj_a, proj_sums_a = attend_backward(
        info, rand, qkv, ctx_grad, ctx_other_grad, ctx, lse, 0, pairs - 1
    )
    proj_a, ctx_grad, down_reduce.moved = tie((proj_a, ctx_grad, down_reduce.moved))
    down_reduce.step()
    out_home = swap_seq(out_send, 2)
    wide_a = 384 * (pairs - 1)
    grad_a = grad_of(tokens, proj_a).astype(bf16)
    reduce_a = Reduce(grad_a.reshape(dp, shard, wide_a), index, y)
    reduce_a.start()
    weight_a, weight_b = full_qkv[:, :wide_a], full_qkv[:, wide_a:]
    input_a = dot(proj_a, weight_a, NT)
    ctx_grad, input_a, _ = tie((ctx_grad, input_a, reduce_a.held))
    proj_b, proj_sums_b = attend_backward(
        info, rand, qkv, ctx_grad, ctx_other_grad, ctx, lse, pairs - 1, 1
    )
    proj_b, reduce_a.moved, down_reduce.moved, out_home = tie(
        (proj_b, reduce_a.moved, down_reduce.moved, out_home)
    )
    output = home_rows(info, [out_home], 1, (out_keep,))
    while len(down_reduce.bits) > 1:
        down_reduce.step()
    while len(reduce_a.bits) > 2:
        reduce_a.step()

    def input_part(start, rows):
        return input_a[start : start + rows] + dot(proj_b[start : start + rows], weight_b, NT)

    give_send = swap_seq(input_part(own + local_len, local_len).astype(bf16), 1)
    give_keep = swap_seq(input_part(own, local_len).astype(bf16), 1)
    grad_b = grad_of(tokens, proj_b).astype(bf16)
    proj_sums = jnp.concatenate([proj_sums_a, proj_sums_b])[:, 0].reshape(pairs, 3, 128)
    my_sums = jnp.stack([proj_sums[:, 0].reshape(-1), proj_sums[:, 2].reshape(-1)])
    bias_qv_grad = lax.dynamic_update_slice(
        jnp.zeros((2, width), f32), my_sums, (jnp.int32(0), c * half)
    )

    rows = jnp.concatenate([bias_qv_grad, sums[2:6], sums[0:2]], axis=0)
    rows = rows.reshape(8, dp, shard).transpose(1, 0, 2)
    small_rows = 16
    small_grads = jnp.concatenate(
        [
            jnp.pad(rows, ((0, 0), (0, 0), (0, 384 - shard))),
            jnp.pad(up_sums[0].reshape(dp, 1, ff_shard), ((0, 0), (0, 7), (0, 384 - ff_shard))),
        ],
        axis=1,
    ).astype(bf16)
    reduce_b = Reduce(
        jnp.concatenate(
            [grad_b.reshape(dp, shard, 384), small_grads], axis=1
        ),
        index,
        y,
    )
    reduce_b.start()
    own_send = pre_first[local_len:] + input_part(local_len, local_len)
    own_keep = pre_first[:local_len] + input_part(0, local_len)
    (
        give_send,
        give_keep,
        own_send,
        own_keep,
        reduce_a.moved,
        reduce_b.moved,
        down_reduce.moved,
        up_sum,
        output,
    ) = tie(
        (
            give_send,
            give_keep,
            own_send,
            own_keep,
            reduce_a.moved,
            reduce_b.moved,
            down_reduce.moved,
            up_sum,
            output,
        )
    )
    grad_send = (own_send + give_send.astype(f32)).astype(bf16)
    moved_a = swap_seq(grad_send[:cut], 2)
    while len(reduce_b.bits) > 2:
        reduce_b.step()
    down_reduce.step()
    up_moved = swap_seq(up_sum, 2)
    reduce_a.add()
    grad_inputs = home_rows(info, [(own_keep + give_keep.astype(f32)).astype(bf16)], 0)
    (
        moved_a,
        grad_rest,
        reduce_a.held,
        reduce_b.moved,
        down_reduce.moved,
        up_moved,
        grad_inputs,
    ) = tie(
        (
            moved_a,
            grad_send[cut:],
            reduce_a.held,
            reduce_b.moved,
            down_reduce.moved,
            up_moved,
            grad_inputs,
        )
    )
    moved_b = swap_seq(grad_rest, 2)
    reduce_b.add()
    down_reduce.add()
    mine, moves = exchange_four(
        jnp.concatenate(
            [reduce_a.held[:, :, k * 384 : (k + 1) * 384] for k in range(pairs - 1)]
            + [reduce_b.held],
            axis=1,
        ),
        index,
    )
    up_shard = (up_sum.astype(f32) + up_moved.astype(f32)).astype(bf16)
    mine, up_shard, down_held, moved_b, *moves = tie(
        (mine, up_shard, down_reduce.held[0], moved_b, *moves)
    )
    up_shard_other = swap_seq(up_shard, 1)
    total = mine.astype(f32)
    for part in moves:
        total = total + part.astype(f32)
    last = jnp.concatenate([down_held, total.astype(bf16)], axis=0)
    last_chip = swap_seq(last, 2)
    (grad_up,) = widen(
        info,
        [up_shard[None], up_shard_other[None]],
        [(which, 0, 0, shard, 0, middle, 0, 0, 0, middle, which) for which in (0, 1)],
        [(shard, hidden_width)],
    )
    grad_inputs = home_rows(info, [moved_a, moved_b], 1, (grad_inputs,))
    last_chip, grad_up, grad_inputs = tie((last_chip, grad_up, grad_inputs))
    last = jnp.where(y == 0, jnp.stack([last, last_chip]), jnp.stack([last_chip, last]))

    plan = []
    part_rows = (ff_shard + shard) // 2
    few = shard // 2
    b_rows = (shard + small_rows) // 2
    for which in (0, 1):
        for slot in (0, 1):

            def put(row, count, out, out_row, base, stride, column=0, wide=384):
                if count > 0:
                    plan.append(
                        (which, slot, row, count, column, wide, out, out_row, base, stride, which)
                    )

            low, high = slot * part_rows, (slot + 1) * part_rows
            cutoff = min(high, ff_shard)
            put(0, cutoff - low, 2, low, 0, half)
            put(cutoff - low, high - cutoff, 1, cutoff - ff_shard, 0, half)
            for pair in range(pairs):
                for kind in range(3):
                    base = kind * width + pair * 128
                    if pair < pairs - 1:
                        row, count, out_row = part_rows + pair * few, few, slot * few
                    else:
                        row, out_row = part_rows + (pairs - 1) * few, slot * b_rows
                        count = min(b_rows, shard - out_row)
                    put(row, count, 0, out_row, base, half, kind * 128, 128)
            start = part_rows + (pairs - 1) * few
            first = max(shard - slot * b_rows, 0)
            put(start + first, b_rows - first, 3, slot * b_rows + first - shard, 0, 384)
    grad_qkv, grad_out, grad_down, small_sums = widen(
        info,
        [last, swap_seq(last, 1)],
        plan,
        [(shard, 3 * width), (shard, width), (ff_shard, width), (small_rows, 2 * 384)],
    )
    small_sums = small_sums[:, :384] + small_sums[:, 384:]

    return (
        output,
        grad_inputs,
        grad_qkv,
        grad_out,
        grad_up,
        grad_down,
        small_sums[0:2, :shard],
        small_sums[6, :shard],
        small_sums[8, :ff_shard],
        small_sums[7, :shard],
        small_sums[2:4, :shard],
        small_sums[4:6, :shard],
    )


def solution(mesh):
    in_specs = (
        P("dp", "seq", None),
        P("dp", "seq", None),
        P("dp", None),
        P("dp", None),
        P("dp", None),
        P("dp", None),
        P(None, "dp"),
        P("dp"),
        P("dp"),
        P("dp"),
        P(None, "dp"),
        P(None, "dp"),
        P(),
    )
    out_specs = (
        P("dp", "seq", None),
        P("dp", "seq", None),
        P("dp", None),
        P("dp", None),
        P("dp", None),
        P("dp", None),
        P(None, "dp"),
        P("dp"),
        P("dp"),
        P("dp"),
        P(None, "dp"),
        P(None, "dp"),
    )
    return jax.shard_map(body, mesh=mesh, in_specs=in_specs, out_specs=out_specs, check_vma=False)
```

```python
import functools

import jax
import jax.numpy as jnp
from jax import lax
from jax.experimental import pallas as pl
from jax.experimental.pallas import tpu as pltpu
from jax.sharding import PartitionSpec as P

HEADS = 12
HEAD_DIM = 64
BLOCK = 64
RAND = 3

norm_eps = 1e-06
bf16 = jnp.bfloat16
f32 = jnp.float32
NN = (((1,), (0,)), ((), ()))
NT = (((1,), (1,)), ((), ()))
TN = (((0,), (0,)), ((), ()))
VMEM_BYTES = 60 << 20


def dot(a, b, dims=NN):
    return lax.dot_general(a, b, dims, preferred_element_type=f32)


def row_of(block, y, c, chunk_blocks):
    chunk = block // chunk_blocks
    place = (((chunk & 1) ^ c) << 1) | ((chunk >> 1) ^ y)
    return pl.multiple_of((place * chunk_blocks + block % chunk_blocks) * BLOCK, BLOCK)


class Rows:
    def __init__(self, info_ref, rand_ref, first_pair, nblocks):
        self.y, self.c = info_ref[0], info_ref[1]
        self.rand_ref = rand_ref
        self.nblocks = nblocks
        self.head = self.c * info_ref[2] + 2 * first_pair
        self.low = lax.broadcasted_iota(jnp.int32, (BLOCK, 128), 1) < HEAD_DIM
        self.low_row = lax.broadcasted_iota(jnp.int32, (1, 128), 1) < HEAD_DIM

    def at(self, block):
        return pl.ds(row_of(block, self.y, self.c, self.nblocks // 4), BLOCK)

    def two(self, tile):
        zero = jnp.zeros_like(tile)
        return jnp.concatenate(
            [jnp.where(self.low, tile, zero), jnp.where(self.low, zero, tile)], axis=0
        )

    def one(self, both):
        return jnp.where(self.low, both[:BLOCK], both[BLOCK:])

    def rand(self, i):
        middle = self.nblocks - 2
        base = (self.head * middle + (i - 1)) * RAND
        return [
            (self.rand_ref[base + t], self.rand_ref[base + middle * RAND + t]) for t in range(RAND)
        ]

    def near(self, load, ends, i, rand):
        mixed = [jnp.where(self.low, load(a), load(b)) for a, b in rand]
        return jnp.concatenate([ends, load(i - 1), load(i + 1), load(i)] + mixed, axis=0)

    def mask(self, scores, i):
        first = jnp.where(i == 1, -1e30, 0.0)
        last = jnp.where(i == self.nblocks - 2, -1e30, 0.0)
        bias = jnp.where(self.low_row, first, last).astype(f32)
        return jnp.concatenate(
            [scores[:, :128], scores[:, 128:256] + bias, scores[:, 256:]], axis=1
        )


def forward_kernel(info_ref, rand_ref, qkv_ref, *refs, nblocks, first, unroll):
    ctx_ref, lse_ref = refs[-2:]
    rows = Rows(info_ref, rand_ref, pl.program_id(0) + first, nblocks)

    def load(block, column):
        return qkv_ref[rows.at(block), column * 128 : (column + 1) * 128]

    def finish(block, scores, values):
        peak = jnp.max(scores, axis=1, keepdims=True)
        powers = jnp.exp(scores - peak).astype(bf16)
        both = dot(powers, jnp.concatenate([values, jnp.ones_like(values)], axis=1))
        totals = both[:, 128:]
        lse = peak + jnp.log(totals)
        ctx_ref[rows.at(block), :] = rows.one(both[:, :128] / totals).astype(bf16)
        lse_ref[rows.at(block), :128] = lse[:BLOCK]
        lse_ref[rows.at(block), 128:] = lse[BLOCK:]

    for edge in (0, nblocks - 1):
        scores = dot(rows.two(load(edge, 0)), qkv_ref[:, 128:256], NT)
        finish(edge, scores, qkv_ref[:, 256:384])
    key_ends = jnp.concatenate([load(0, 1), load(nblocks - 1, 1)], axis=0)
    value_ends = jnp.concatenate([load(0, 2), load(nblocks - 1, 2)], axis=0)

    def row(i):
        rand = rows.rand(i)
        keys = rows.near(lambda b: load(b, 1), key_ends, i, rand)
        values = rows.near(lambda b: load(b, 2), value_ends, i, rand)
        finish(i, rows.mask(dot(rows.two(load(i, 0)), keys, NT), i), values)

    def step(t, carry):
        for u in range(unroll):
            row(1 + t * unroll + u)
        return carry

    lax.fori_loop(0, (nblocks - 2) // unroll, step, 0)


def backward_kernel(
    info_ref, rand_ref, qkv_ref, own_ref, other_ref, ctx_ref, lse_ref, out_ref, sum_ref,
    key_sum, value_sum, grad_ref,
    *, nblocks, first, unroll
):
    rows = Rows(info_ref, rand_ref, pl.program_id(0) + first, nblocks)
    zero = jnp.zeros((BLOCK, 128), f32)
    half_rows = own_ref.shape[0]
    grad_ref[:half_rows] = own_ref[...]
    grad_ref[half_rows:] = other_ref[...]

    def load(block, column):
        return qkv_ref[rows.at(block), column * 128 : (column + 1) * 128]

    ones = jnp.ones((256, 128), bf16)

    def finish(block, scores, keys, values):
        grad = grad_ref[rows.at(block), :]
        both = grad.astype(f32) * ctx_ref[rows.at(block), :].astype(f32)
        high = both.astype(bf16)
        rest = (both - high.astype(f32)).astype(bf16)
        row_dot = dot(jnp.concatenate([rows.two(high), rows.two(rest)], axis=1), ones)
        lse = jnp.concatenate(
            [lse_ref[rows.at(block), :128], lse_ref[rows.at(block), 128:]], axis=0
        )
        grad = rows.two(grad)
        attn_grad = dot(grad, values, NT)
        attention, score_grad = [], []
        for k in range(scores.shape[1] // 128):
            part = slice(k * 128, (k + 1) * 128)
            probs = jnp.exp(scores[:, part] - lse)
            score_grad.append((probs * (attn_grad[:, part] - row_dot)).astype(bf16))
            attention.append(probs.astype(bf16))
        attention = jnp.concatenate(attention, axis=1)
        score_grad = jnp.concatenate(score_grad, axis=1)
        query_grad = dot(score_grad, keys) * HEAD_DIM ** (-0.5)
        out_ref[rows.at(block), 0:128] = rows.one(query_grad).astype(bf16)
        return grad, attention, score_grad

    for edge in (0, nblocks - 1):
        query = rows.two(load(edge, 0))
        keys, values = qkv_ref[:, 128:256], qkv_ref[:, 256:384]
        grad, attention, score_grad = finish(edge, dot(query, keys, NT), keys, values)
        if edge == 0:
            key_sum[...] = dot(score_grad, query, TN)
            value_sum[...] = dot(attention, grad, TN)
        else:
            key_sum[...] += dot(score_grad, query, TN)
            value_sum[...] += dot(attention, grad, TN)
    key_ends = jnp.concatenate([load(0, 1), load(nblocks - 1, 1)], axis=0)
    value_ends = jnp.concatenate([load(0, 2), load(nblocks - 1, 2)], axis=0)

    def row(i):
        rand = rows.rand(i)
        keys = rows.near(lambda b: load(b, 1), key_ends, i, rand)
        values = rows.near(lambda b: load(b, 2), value_ends, i, rand)
        query = rows.two(load(i, 0))
        scores = rows.mask(dot(query, keys, NT), i)
        grad, attention, score_grad = finish(i, scores, keys, values)
        for total, part in (
            (key_sum, dot(score_grad, query, TN)),
            (value_sum, dot(attention, grad, TN)),
        ):
            for slot, block in enumerate((0, nblocks - 1, i - 1, i + 1, i)):
                total[rows.at(block), :] += part[slot * BLOCK : (slot + 1) * BLOCK]
            for slot, (a, b) in enumerate(rand):
                tile = part[(5 + slot) * BLOCK : (6 + slot) * BLOCK]
                total[rows.at(a), :] += jnp.where(rows.low, tile, zero)
                total[rows.at(b), :] += jnp.where(rows.low, zero, tile)

    def step(t, carry):
        for u in range(unroll):
            row(1 + t * unroll + u)
        return carry

    lax.fori_loop(0, (nblocks - 2) // unroll, step, 0)
    out_ref[:, 128:256] = key_sum[...].astype(bf16)
    out_ref[:, 256:384] = value_sum[...].astype(bf16)
    sum_ref[0] = jnp.broadcast_to(
        jnp.sum(out_ref[...].astype(f32), axis=0, keepdims=True), (8, 384)
    )


def attend_forward(info, rand, qkv, first, pairs, total, into=()):
    length = qkv.shape[0]
    wide = pl.BlockSpec((length, 384), lambda p, *_: (0, p + first))
    slim = pl.BlockSpec((length, 128), lambda p, *_: (0, p + first))
    twin = pl.BlockSpec((length, 256), lambda p, *_: (0, p + first))
    return pl.pallas_call(
        functools.partial(forward_kernel, nblocks=length // BLOCK, first=first, unroll=10),
        grid_spec=pltpu.PrefetchScalarGridSpec(
            num_scalar_prefetch=2,
            grid=(pairs,),
            in_specs=[wide] + [pl.BlockSpec(memory_space=pl.ANY)] * len(into),
            out_specs=[slim, twin],
        ),
        out_shape=[
            jax.ShapeDtypeStruct((length, total * 128), bf16),
            jax.ShapeDtypeStruct((length, total * 256), f32),
        ],
        input_output_aliases={3 + k: k for k in range(len(into))},
        compiler_params=pltpu.CompilerParams(vmem_limit_bytes=VMEM_BYTES),
        name="attend_forward",
    )(info, rand, qkv, *into)


def attend_backward(info, rand, qkv, own_grad, other_grad, ctx, lse, first, pairs):
    length = qkv.shape[0]
    wide = pl.BlockSpec((length, 384), lambda p, *_: (0, p + first))
    slim = pl.BlockSpec((length, 128), lambda p, *_: (0, p + first))
    part = pl.BlockSpec((length // 2, 128), lambda p, *_: (0, p + first))
    twin = pl.BlockSpec((length, 256), lambda p, *_: (0, p + first))
    return pl.pallas_call(
        functools.partial(backward_kernel, nblocks=length // BLOCK, first=first, unroll=10),
        grid_spec=pltpu.PrefetchScalarGridSpec(
            num_scalar_prefetch=2,
            grid=(pairs,),
            in_specs=[wide, part, part, slim, twin],
            out_specs=[
                pl.BlockSpec((length, 384), lambda p, *_: (0, p)),
                pl.BlockSpec((1, 8, 384), lambda p, *_: (p, 0, 0)),
            ],
            scratch_shapes=[pltpu.VMEM((length, 128), f32)] * 2 + [pltpu.VMEM((length, 128), bf16)],
        ),
        out_shape=[
            jax.ShapeDtypeStruct((length, pairs * 384), bf16),
            jax.ShapeDtypeStruct((pairs, 8, 384), f32),
        ],
        compiler_params=pltpu.CompilerParams(vmem_limit_bytes=VMEM_BYTES),
        name="attend_backward",
    )(info, rand, qkv, own_grad, other_grad, ctx, lse)


def swap_dp(value, bit):
    size = lax.axis_size("dp")
    return lax.ppermute(value, "dp", [(i, i ^ bit) for i in range(size)])


def swap_seq(value, bit):
    size = lax.axis_size("seq")
    return lax.ppermute(value, "seq", [(i, i ^ bit) for i in range(size)])


def bits_of(size):
    return [size >> (k + 1) for k in range(size.bit_length() - 1)]


def widened(blocks):
    return sum((o for o, _ in blocks), []), jnp.concatenate([a for _, a in blocks], axis=0)


def across(block, bit):
    offsets, array = block
    return [offset ^ bit for offset in offsets], swap_dp(array, bit)


def first_bits(shard):
    block = ([0], shard[None])
    for bit in bits_of(lax.axis_size("dp"))[:-3]:
        block = widened([block, across(block, bit)])
    return block


def tied(blocks, *values):
    arrays = lax.optimization_barrier((*[array for _, array in blocks], *values))
    count = len(blocks)
    return [(blocks[k][0], arrays[k]) for k in range(count)] + list(arrays[count:])


class Reduce:
    def __init__(self, parts, index, y):
        count, rows, columns = parts.shape
        self.held, self.index, self.y = parts.reshape(count, 2, rows // 2, columns), index, y
        self.bits = [0] + bits_of(lax.axis_size("dp"))[::-1]

    def start(self):
        bit = self.bits.pop(0)
        if bit:
            view = self.held.reshape(-1, 2, *self.held.shape[1:])
            mine = (self.index // bit) % 2
        else:
            view, mine = self.held, self.y
        self.held = lax.dynamic_slice_in_dim(view, mine, 1, 1)[:, 0]
        give = lax.dynamic_slice_in_dim(view, 1 - mine, 1, 1)[:, 0]
        self.moved = swap_dp(give, bit) if bit else swap_seq(give, 2)

    def add(self):
        self.held = (self.held.astype(f32) + self.moved.astype(f32)).astype(bf16)

    def step(self):
        self.add()
        self.start()


def exchange_four(held, index):
    unit = lax.axis_size("dp") // 4
    me = index // unit
    mine = lax.dynamic_index_in_dim(held, me, 0, keepdims=False)
    moved = [
        swap_dp(lax.dynamic_index_in_dim(held, me ^ k, 0, keepdims=False), k * unit)
        for k in (1, 2, 3)
    ]
    return mine, moved


def prepare_kernel(info_ref, w_ref, qv_ref, gain_ref, shift_ref, out_ref, down_ref, up_ref, shard_ref):
    c = info_ref[1]
    third = w_ref.shape[1] // 3
    half = third // 2
    depth, few = qv_ref.shape[1], up_ref.shape[1]
    for kind in range(3):
        columns = pl.ds(pl.multiple_of(kind * third + c * half, 128), half)
        part = w_ref[:, columns]
        for pair in range(half // 128):
            at = (pair * 3 + kind) * 128
            shard_ref[0:depth, at : at + 128] = part[:, pair * 128 : (pair + 1) * 128]
    shard_ref[depth:] = jnp.zeros((8, 3 * half), bf16)
    shard_ref[depth : depth + 2, 0:depth] = qv_ref[...]
    shard_ref[depth + 2 : depth + 4, 0:depth] = gain_ref[...]
    shard_ref[depth + 4 : depth + 6, 0:depth] = shift_ref[...]
    shard_ref[depth + 6 : depth + 7, 0:depth] = out_ref[...]
    shard_ref[depth + 7 : depth + 8, 0:depth] = down_ref[...]
    shard_ref[depth : depth + 1, 128 : 128 + few] = up_ref[...]


def prepare(info, w_qkv, *small):
    depth, columns = w_qkv.shape
    arrays = (w_qkv, *small)
    return pl.pallas_call(
        prepare_kernel,
        grid_spec=pltpu.PrefetchScalarGridSpec(
            num_scalar_prefetch=1,
            grid=(1,),
            in_specs=[pl.BlockSpec(a.shape, lambda i, *_: (0, 0)) for a in arrays],
            out_specs=pl.BlockSpec((depth + 8, columns // 2), lambda i, *_: (0, 0)),
        ),
        out_shape=jax.ShapeDtypeStruct((depth + 8, columns // 2), bf16),
        compiler_params=pltpu.CompilerParams(vmem_limit_bytes=VMEM_BYTES),
        name="prepare",
    )(info, *arrays)


def project_kernel(info_ref, inputs_ref, *refs, offsets, shard, ff_shard):
    more, refs = refs[:3], refs[3:]
    pieces, refs = refs[: len(offsets)], refs[len(offsets) :]
    qkv_ref, tokens_ref, weight_ref, norms_ref, up_ref, bias_ref = refs
    step = pl.program_id(0)
    width = weight_ref.shape[0]
    half = width // 2

    def spread(part, size, target, at):
        shape = (part.shape[1], target)
        lane = lax.broadcasted_iota(jnp.int32, shape, 1) - at
        source = lax.broadcasted_iota(jnp.int32, shape, 0)
        return dot(part, jnp.where((lane == source) & (source < size), 1.0, 0.0).astype(bf16))

    @pl.when(step == 0)
    def _():
        norms = jnp.zeros((8, width), f32)
        for offset, piece in zip(offsets, pieces):
            place = info_ref[4] ^ offset
            at = pl.ds(pl.multiple_of(place * shard, 8), shard)
            weight_ref[at, :] = piece[0:shard]
            tail = piece[shard : shard + 8]
            norms = norms + spread(tail[:, :128], shard, width, place * shard)
            if ff_shard % 128 == 0:
                lanes = pl.ds(pl.multiple_of(place * ff_shard, 128), ff_shard)
                up_ref[:, lanes] = tail[:, 128 : 128 + ff_shard].astype(f32)
            else:
                part = spread(tail[:, 128:256], ff_shard, up_ref.shape[1], place * ff_shard)
                if offset == offsets[0]:
                    up_ref[...] = part
                else:
                    up_ref[...] += part
        norms_ref[...] = norms
        bias_ref[...] = jnp.zeros_like(bias_ref)
        for pair in range(half // 128):
            lanes = pl.ds(pl.multiple_of(info_ref[1] * half + pair * 128, 128), 128)
            bias_ref[0:1, pair * 384 : pair * 384 + 128] = norms_ref[0:1, lanes]
            bias_ref[0:1, pair * 384 + 256 : pair * 384 + 384] = norms_ref[1:2, lanes]
        tokens_ref[...] = inputs_ref[0]

    for k in range(3):

        @pl.when(step == k + 1)
        def _():
            tokens_ref[...] = more[k][...]

    wide = dot(tokens_ref[...], weight_ref[...]) + bias_ref[0:1]
    for pair in range(wide.shape[1] // 384):
        at = pair * 384
        query = wide[:, at : at + 128].astype(bf16).astype(f32) * HEAD_DIM ** (-0.5)
        qkv_ref[:, at : at + 128] = query.astype(bf16)
        qkv_ref[:, at + 128 : at + 384] = wide[:, at + 128 : at + 384].astype(bf16)


def project(info, inputs, more, pieces, offsets, shard, ff_shard):
    _, local_len, width = inputs.shape
    columns = pieces[0].shape[1]
    hidden = ff_shard * len(pieces)

    def whole(array):
        return pl.BlockSpec(array.shape, lambda i, *_: (0, 0), pipeline_mode=pl.Buffered(1))

    fixed = [((width, columns), bf16), ((8, width), f32), ((8, hidden), f32)]
    return pl.pallas_call(
        functools.partial(project_kernel, offsets=offsets, shard=shard, ff_shard=ff_shard),
        grid_spec=pltpu.PrefetchScalarGridSpec(
            num_scalar_prefetch=1,
            grid=(4,),
            in_specs=[pl.BlockSpec((1, local_len, width), lambda i, info: (info[0], 0, 0))]
            + [whole(array) for array in (*more, *pieces)],
            out_specs=[
                pl.BlockSpec((local_len, columns), lambda i, *_: (i, 0)),
                pl.BlockSpec((local_len, width), lambda i, *_: (i, 0)),
            ]
            + [pl.BlockSpec(shape, lambda i, *_: (0, 0)) for shape, _ in fixed],
            scratch_shapes=[pltpu.VMEM((8, columns), f32)],
        ),
        out_shape=[
            jax.ShapeDtypeStruct((4 * local_len, columns), bf16),
            jax.ShapeDtypeStruct((4 * local_len, width), bf16),
        ]
        + [jax.ShapeDtypeStruct(shape, kind) for shape, kind in fixed],
        compiler_params=pltpu.CompilerParams(vmem_limit_bytes=VMEM_BYTES),
        name="project",
    )(info, inputs, *more, *pieces)


CHUNK = 768


def gelu_pair(values):
    square = values * values
    inner = values * (0.7978845608028654 + 0.7978845608028654 * 0.044715 * square)
    gate = 0.5 + 0.5 * jnp.tanh(inner)
    active = values * gate
    slope = 2 * 0.7978845608028654 + 6 * 0.7978845608028654 * 0.044715 * square
    return active, gate + (active - active * gate) * slope


def norm_parts(values):
    center = values - jnp.mean(values, axis=-1, keepdims=True)
    spread = jnp.mean(center * center, axis=-1, keepdims=True)
    inverse = lax.rsqrt(spread + norm_eps)
    return center * inverse, inverse


def norm_back(grad, unit, inverse, gain):
    scaled = grad * gain
    return inverse * (
        scaled
        - jnp.mean(scaled, axis=-1, keepdims=True)
        - unit * jnp.mean(scaled * unit, axis=-1, keepdims=True)
    )


def middle_kernel(
    info_ref,
    tokens_ref,
    ctx_ref,
    ctx_other_ref,
    cotangent_ref,
    up_ref,
    up_other_ref,
    *refs,
    down_plan,
    steps,
):
    n_down = 1 + max(entry[0] for entry in down_plan)
    down_refs, refs = refs[:n_down], refs[n_down:]
    (
        norm_ref,
        bias_up_ref,
        keep_ref,
        send_ref,
        ctx_all_ref,
        normed_ref,
        active_ref,
        hidden_mine_ref,
        hidden_other_ref,
        ffn_mine_ref,
        ffn_other_ref,
        first_ref,
        branch_mine_ref,
        branch_other_ref,
        ctx_grad_ref,
        ctx_send_ref,
        sums_ref,
        up_sums_ref,
        down_all,
        out_all,
        change_all,
        wide,
    ) = refs
    c, index, flip = info_ref[1], info_ref[4], info_ref[5]
    step = pl.program_id(0)
    half = ctx_ref.shape[1]
    middle = up_ref.shape[1] - half
    hidden = 2 * middle

    def up_part(k):
        inside = k * CHUNK % middle
        return (up_ref if k * CHUNK < middle else up_other_ref)[:, inside : inside + CHUNK]

    def lanes(which, size):
        return pl.ds(pl.multiple_of(which * size, 128), size)

    def rows(which, size):
        return pl.ds(pl.multiple_of(which * size, 16), size)

    @pl.when(step == 0)
    def _():
        out_all[:, lanes(c, half)] = up_ref[:, middle:]
        out_all[:, lanes(1 - c, half)] = up_other_ref[:, middle:]
        for source, slot, offset, which in down_plan:
            size = down_refs[source].shape[1]
            block = (index ^ offset ^ flip) * 2 + (info_ref[0] ^ (which // 2))
            down_all[rows(block, size), lanes(c ^ (which % 2), half)] = down_refs[source][slot]
        sums_ref[...] = jnp.zeros_like(sums_ref)
        up_sums_ref[...] = jnp.zeros_like(up_sums_ref)

    bias_out, bias_down = norm_ref[6:7], norm_ref[7:8]
    gain_1, gain_2, shift_1, shift_2 = (norm_ref[k : k + 1] for k in (2, 3, 4, 5))
    ctx_all_ref[:, lanes(c, half)] = ctx_ref[...]
    ctx_all_ref[:, lanes(1 - c, half)] = ctx_other_ref[...]
    branch = dot(ctx_all_ref[...], out_all[...]) + bias_out
    unit_1, inverse_1 = norm_parts(tokens_ref[...].astype(f32) + branch)
    normed = unit_1 * gain_1 + shift_1
    normed_low = normed.astype(bf16)
    normed_ref[...] = normed_low

    total = jnp.zeros_like(branch)
    for k in range(hidden // CHUNK):
        part = slice(k * CHUNK, (k + 1) * CHUNK)
        which = c ^ (k * CHUNK // middle)
        inside = k * CHUNK % middle
        at = pl.ds(pl.multiple_of(which * middle + inside, 128), CHUNK)
        bias = bias_up_ref[0:1, at]
        active, change = gelu_pair(dot(normed_low, up_part(k)) + bias)
        active = active.astype(bf16)
        active_ref[:, at] = active
        change_all[:, part] = change.astype(bf16)
        total = total + dot(active, down_all[part])

    unit_2, inverse_2 = norm_parts(normed + total + bias_down)
    result = (unit_2 * gain_2 + shift_2).astype(bf16)

    @pl.when(step < steps // 2)
    def _():
        keep_ref[0] = result

    @pl.when(step >= steps // 2)
    def _():
        send_ref[...] = result


    cotangent = cotangent_ref[...].astype(f32)
    pre_second = norm_back(cotangent, unit_2, inverse_2, gain_2)
    ffn_grad = pre_second.astype(bf16)
    wide[...] = ffn_grad
    ffn_mine_ref[...] = wide[:, lanes(c, half)]
    ffn_other_ref[...] = wide[:, lanes(1 - c, half)]

    def add(row, values):
        sums_ref[row : row + 1] += jnp.sum(values, axis=0, keepdims=True)

    add(1, ffn_grad.astype(f32))
    add(3, cotangent * unit_2)
    add(5, cotangent)

    total = jnp.zeros_like(branch)
    for k in range(hidden // CHUNK):
        part = slice(k * CHUNK, (k + 1) * CHUNK)
        grad = (dot(ffn_grad, down_all[part], NT) * change_all[:, part]).astype(bf16)
        target = hidden_mine_ref if k * CHUNK < middle else hidden_other_ref
        inside = k * CHUNK % middle
        target[:, inside : inside + CHUNK] = grad
        which = c ^ (k * CHUNK // middle)
        at = pl.ds(pl.multiple_of(which * middle + inside, 128), CHUNK)
        up_sums_ref[0:1, at] += jnp.sum(grad.astype(f32), axis=0, keepdims=True)
        total = total + dot(grad, up_part(k), NT)

    normed_grad = pre_second + total
    pre_first = norm_back(normed_grad, unit_1, inverse_1, gain_1)
    first_ref[...] = pre_first
    branch_grad = pre_first.astype(bf16)
    wide[...] = branch_grad
    branch_mine_ref[...] = wide[:, lanes(c, half)]
    branch_other_ref[...] = wide[:, lanes(1 - c, half)]
    add(0, branch_grad.astype(f32))
    add(2, normed_grad * unit_1)
    add(4, normed_grad)
    ctx_grad = dot(branch_grad, out_all[...], NT).astype(bf16)
    wide[...] = ctx_grad
    ctx_grad_ref[...] = wide[:, lanes(c, half)]
    ctx_send_ref[...] = wide[:, lanes(1 - c, half)]


def feed_forward(info, tokens, ctx, ctx_other, cotangent, up, up_other, down_groups, norms, bias_up):
    count, width = cotangent.shape
    half = ctx.shape[1]
    middle = up.shape[1] - half
    hidden = 2 * middle
    tile = 256
    steps = count // tile
    arrays, plan = [], []
    for offsets, which, array in down_groups:
        for slot, offset in enumerate(offsets):
            plan.append((len(arrays), slot, offset, which))
        arrays.append(array)

    def tiled(columns):
        return pl.BlockSpec((tile, columns), lambda i, *_: (i, 0))

    def whole(array):
        rank = len(array.shape)
        return pl.BlockSpec(
            array.shape, lambda i, *_: (0,) * rank, pipeline_mode=pl.Buffered(1)
        )

    outs = [
        ((count, width), bf16),
        ((count, width), bf16),
        ((count, hidden), bf16),
        ((count, middle), bf16),
        ((count, middle), bf16),
        ((count, half), bf16),
        ((count, half), bf16),
        ((count, width), f32),
        ((count, half), bf16),
        ((count, half), bf16),
        ((count, half), bf16),
        ((count, half), bf16),
    ]
    sums = [((8, width), f32), ((8, hidden), f32)]
    return pl.pallas_call(
        functools.partial(middle_kernel, down_plan=plan, steps=steps),
        grid_spec=pltpu.PrefetchScalarGridSpec(
            num_scalar_prefetch=1,
            grid=(steps,),
            in_specs=[tiled(width), tiled(half), tiled(half), tiled(width), whole(up), whole(up_other)]
            + [whole(array) for array in arrays]
            + [whole(norms), whole(bias_up)],
            out_specs=[
                pl.BlockSpec(
                    (1, tile, width), lambda i, info: (info[0], jnp.minimum(i, steps // 2 - 1), 0)
                ),
                pl.BlockSpec((tile, width), lambda i, *_: (jnp.maximum(i - steps // 2, 0), 0)),
            ]
            + [tiled(shape[1]) for shape, _ in outs]
            + [pl.BlockSpec(shape, lambda i, *_: (0, 0)) for shape, _ in sums],
            scratch_shapes=[
                pltpu.VMEM((hidden, width), bf16),
                pltpu.VMEM((width, width), bf16),
                pltpu.VMEM((tile, hidden), bf16),
                pltpu.VMEM((tile, width), bf16),
            ],
        ),
        out_shape=[jax.ShapeDtypeStruct((2, count // 2, width), bf16)]
        + [jax.ShapeDtypeStruct((count // 2, width), bf16)]
        + [jax.ShapeDtypeStruct(shape, kind) for shape, kind in outs + sums],
        compiler_params=pltpu.CompilerParams(vmem_limit_bytes=VMEM_BYTES),
        name="feed_forward",
    )(info, tokens, ctx, ctx_other, cotangent, up, up_other, *arrays, norms, bias_up)


def home_kernel(info_ref, *refs, count):
    start = 0
    for ref in refs[:count]:
        refs[-1][0, start : start + ref.shape[0]] = ref[...]
        start += ref.shape[0]


def home_rows(info, pieces, which, into=()):
    rows = sum(piece.shape[0] for piece in pieces)
    width = pieces[0].shape[1]
    return pl.pallas_call(
        functools.partial(home_kernel, count=len(pieces)),
        grid_spec=pltpu.PrefetchScalarGridSpec(
            num_scalar_prefetch=1,
            grid=(1,),
            in_specs=[pl.BlockSpec(piece.shape, lambda i, *_: (0, 0)) for piece in pieces]
            + [pl.BlockSpec(memory_space=pl.ANY)] * len(into),
            out_specs=pl.BlockSpec((1, rows, width), lambda i, info: (info[0] ^ which, 0, 0)),
        ),
        out_shape=jax.ShapeDtypeStruct((2, rows, width), bf16),
        input_output_aliases={1 + len(pieces): 0} if into else {},
        name="home_rows",
    )(info, *pieces, *into)


def widen_kernel(info_ref, *refs, plan, n_in):
    ins, outs = refs[:n_in], refs[n_in:]
    c = info_ref[1]
    for source, slot, row, rows, column, width, out, out_row, base, stride, which in plan:
        at = pl.ds(pl.multiple_of(base + (c ^ which) * stride, 128), width)
        outs[out][out_row : out_row + rows, at] = ins[source][
            slot, row : row + rows, column : column + width
        ].astype(f32)


def widen(info, arrays, plan, shapes):
    return pl.pallas_call(
        functools.partial(widen_kernel, plan=plan, n_in=len(arrays)),
        grid_spec=pltpu.PrefetchScalarGridSpec(
            num_scalar_prefetch=1,
            grid=(1,),
            in_specs=[pl.BlockSpec(a.shape, lambda i, *_: (0, 0, 0)) for a in arrays],
            out_specs=[pl.BlockSpec(shape, lambda i, *_: (0, 0)) for shape in shapes],
        ),
        out_shape=[jax.ShapeDtypeStruct(shape, f32) for shape in shapes],
        compiler_params=pltpu.CompilerParams(vmem_limit_bytes=VMEM_BYTES),
        name="widen",
    )(info, *arrays)


def body(
    inputs,
    out_grad,
    w_qkv,
    w_attn_out,
    w_up,
    w_down,
    bias_qv,
    bias_out,
    bias_up,
    bias_down,
    norm_gain,
    norm_shift,
    rand_blocks,
):
    _, local_len, width = inputs.shape
    dp = lax.axis_size("dp")
    index = lax.axis_index("dp")
    seat = lax.axis_index("seq")
    y, c = seat // 2, seat % 2
    heads_here = HEADS // 2
    pairs = heads_here // 2
    half = width // 2
    hidden_width = w_up.shape[1]
    middle = hidden_width // 2
    own = 2 * local_len
    shard = width // dp
    ff_shard = hidden_width // dp
    qkv_width = 3 * half
    flip = c * (dp // 2)
    info = jnp.stack([y, c, jnp.int32(heads_here), jnp.int32(0), index, flip]).astype(jnp.int32)
    rand = rand_blocks.reshape(-1)

    def pick(values, which):
        return lax.dynamic_index_in_dim(values, which, 0, keepdims=False)

    def column(value, which):
        return lax.dynamic_slice_in_dim(value, which * (value.shape[1] // 2), value.shape[1] // 2, 1)

    tie = lax.optimization_barrier

    given = pick(inputs, 1 - y)
    qkv_shard = prepare(
        info, w_qkv, bias_qv, norm_gain, norm_shift, bias_out[None], bias_down[None], bias_up[None]
    )
    bits = bits_of(dp)
    cut = local_len // 2
    chip_a = swap_seq(given[:cut], 2)
    mine = pick(inputs, y)
    first_moves = [swap_dp(qkv_shard, bit) for bit in bits]
    up_out = jnp.concatenate([column(w_up, c), column(w_attn_out, c)], axis=1)
    other_mine = swap_seq(mine, 1)
    down_shard = lax.dynamic_slice(w_down, (y * (ff_shard // 2), c * half), (ff_shard // 2, half))
    chip_a, rest, up_out, other_mine, down_shard, *first_moves = tie(
        (chip_a, given[cut:], up_out, other_mine, down_shard, *first_moves)
    )
    down_0 = first_bits(down_shard)
    down_far = across(down_0, bits[-3])
    chip_b = swap_seq(rest, 2)
    held = [(0, qkv_shard)] + list(zip(bits, first_moves))
    if dp == 8:
        held = held + [
            (o ^ bit, swap_dp(part, bit))
            for o, part, bit in (
                (bits[0], first_moves[0], bits[1]),
                (bits[1], first_moves[1], bits[2]),
                (bits[0], first_moves[0], bits[2]),
            )
        ]
    else:
        held = [(0, qkv_shard)]
        for bit in bits:
            held = held + [(o ^ bit, swap_dp(part, bit)) for o, part in held]
    offsets = [offset for offset, _ in held]
    chip_b, cotangent_give, down_moved, *parts = tie(
        (chip_b, out_grad, down_far[1], *[part for _, part in held])
    )
    down_a = widened([down_0, (down_far[0], down_moved)])
    cotangent_chip = swap_seq(pick(cotangent_give, 1 - y), 2)
    held = list(zip(offsets, parts))
    if dp == 8:
        offset, part = held[4]
        held = held + [(offset ^ bits[2], swap_dp(part, bits[2]))]
    from_chip = jnp.concatenate([chip_a, chip_b], axis=0)
    other_chip = swap_seq(from_chip, 1)
    offsets = [offset for offset, _ in held]
    pieces = [part for _, part in held]
    up_out = lax.all_gather(up_out, "dp", axis=0, tiled=True)
    near, side = bits[-2:]
    down_b, down_a_side = across(down_a, near), across(down_a, side)

    qkv, tokens, full_qkv, norms, bias_up_row = project(
        info, inputs, (from_chip, other_mine, other_chip), pieces, offsets, shard, ff_shard
    )
    down_b, down_a_side, qkv, cotangent_chip = tied([down_b, down_a_side], qkv, cotangent_chip)
    down_b_side = across(down_b, side)
    down_a = widened([down_a, down_a_side])
    down_a_chip = swap_seq(down_a[1], 2)
    ctx, lse = attend_forward(info, rand, qkv, 0, 1, pairs)
    down_b_side, qkv, ctx, lse, down_a_chip, up_out = tied(
        [down_b_side], qkv, ctx, lse, down_a_chip, up_out
    )
    up_other = swap_seq(up_out, 1)
    down_b = widened([down_b, down_b_side])
    down_b_chip = swap_seq(down_b[1], 2)
    down_a_core = swap_seq(down_a[1], 1)
    down_a_both = swap_seq(down_a_chip, 1)
    ctx, lse = attend_forward(info, rand, qkv, 1, pairs - 1, pairs, (ctx, lse))
    ctx, lse, down_b_chip, down_a_core, down_a_both, up_other = tie(
        (ctx, lse, down_b_chip, down_a_core, down_a_both, up_other)
    )
    ctx_other = swap_seq(ctx[own:], 1)
    down_groups = [
        (down_a[0], 0, down_a[1]),
        (down_a[0], 1, down_a_core),
        (down_a[0], 2, down_a_chip),
        (down_a[0], 3, down_a_both),
        (down_b[0], 0, down_b[1]),
        (down_b[0], 1, swap_seq(down_b[1], 1)),
        (down_b[0], 2, down_b_chip),
        (down_b[0], 3, swap_seq(down_b_chip, 1)),
    ]
    cotangent = jnp.concatenate([pick(out_grad, y), cotangent_chip], axis=0)
    (
        out_keep,
        out_send,
        ctx_all,
        normed,
        active,
        hidden_mine,
        hidden_other,
        ffn_mine,
        ffn_other,
        pre_first,
        branch_mine,
        branch_other,
        ctx_grad,
        ctx_send,
        sums,
        up_sums,
    ) = feed_forward(
        info, tokens, ctx, ctx_other, cotangent, up_out, up_other, down_groups, norms, bias_up_row
    )
    ctx_other_grad = swap_seq(ctx_send, 1)

    def grad_of(left, right):
        return dot(left, right, TN)

    up_give = swap_seq(grad_of(normed, hidden_other).astype(bf16), 1)
    down_give = swap_seq(grad_of(active, ffn_other).astype(bf16), 1)
    out_give = swap_seq(grad_of(ctx_all, branch_other).astype(bf16), 1)
    up_grad = (grad_of(normed, hidden_mine) + up_give.astype(f32)).astype(bf16)
    up_sum = lax.psum_scatter(up_grad, "dp", scatter_dimension=0, tiled=True)
    down_grad = (grad_of(active, ffn_mine) + down_give.astype(f32)).astype(bf16)
    out_weight_grad = (grad_of(ctx_all, branch_mine) + out_give.astype(f32)).astype(bf16)
    down_reduce = Reduce(
        jnp.concatenate(
            [down_grad.reshape(dp, ff_shard, half), out_weight_grad.reshape(dp, shard, half)],
            axis=1,
        ),
        index,
        y,
    )
    down_reduce.start()
    ctx_grad, ctx_other_grad, _ = tie((ctx_grad, ctx_other_grad, down_reduce.held))

    proj_a, proj_sums_a = attend_backward(
        info, rand, qkv, ctx_grad, ctx_other_grad, ctx, lse, 0, pairs - 1
    )
    proj_a, ctx_grad, down_reduce.moved = tie((proj_a, ctx_grad, down_reduce.moved))
    down_reduce.step()
    out_home = swap_seq(out_send, 2)
    wide_a = 384 * (pairs - 1)
    grad_a = grad_of(tokens, proj_a).astype(bf16)
    reduce_a = Reduce(grad_a.reshape(dp, shard, wide_a), index, y)
    reduce_a.start()
    weight_a, weight_b = full_qkv[:, :wide_a], full_qkv[:, wide_a:]
    input_a = dot(proj_a, weight_a, NT)
    ctx_grad, input_a, _ = tie((ctx_grad, input_a, reduce_a.held))
    proj_b, proj_sums_b = attend_backward(
        info, rand, qkv, ctx_grad, ctx_other_grad, ctx, lse, pairs - 1, 1
    )
    proj_b, reduce_a.moved, down_reduce.moved, out_home = tie(
        (proj_b, reduce_a.moved, down_reduce.moved, out_home)
    )
    output = home_rows(info, [out_home], 1, (out_keep,))
    while len(down_reduce.bits) > 1:
        down_reduce.step()
    while len(reduce_a.bits) > 2:
        reduce_a.step()

    def input_part(start, rows):
        return input_a[start : start + rows] + dot(proj_b[start : start + rows], weight_b, NT)

    give_send = swap_seq(input_part(own + local_len, local_len).astype(bf16), 1)
    give_keep = swap_seq(input_part(own, local_len).astype(bf16), 1)
    grad_b = grad_of(tokens, proj_b).astype(bf16)
    proj_sums = jnp.concatenate([proj_sums_a, proj_sums_b])[:, 0].reshape(pairs, 3, 128)
    my_sums = jnp.stack([proj_sums[:, 0].reshape(-1), proj_sums[:, 2].reshape(-1)])
    bias_qv_grad = lax.dynamic_update_slice(
        jnp.zeros((2, width), f32), my_sums, (jnp.int32(0), c * half)
    )

    rows = jnp.concatenate([bias_qv_grad, sums[2:6], sums[0:2]], axis=0)
    rows = rows.reshape(8, dp, shard).transpose(1, 0, 2)
    small_rows = 16
    small_grads = jnp.concatenate(
        [
            jnp.pad(rows, ((0, 0), (0, 0), (0, 384 - shard))),
            jnp.pad(up_sums[0].reshape(dp, 1, ff_shard), ((0, 0), (0, 7), (0, 384 - ff_shard))),
        ],
        axis=1,
    ).astype(bf16)
    reduce_b = Reduce(
        jnp.concatenate(
            [grad_b.reshape(dp, shard, 384), small_grads], axis=1
        ),
        index,
        y,
    )
    reduce_b.start()
    own_send = pre_first[local_len:] + input_part(local_len, local_len)
    own_keep = pre_first[:local_len] + input_part(0, local_len)
    (
        give_send,
        give_keep,
        own_send,
        own_keep,
        reduce_a.moved,
        reduce_b.moved,
        down_reduce.moved,
        up_sum,
        output,
    ) = tie(
        (
            give_send,
            give_keep,
            own_send,
            own_keep,
            reduce_a.moved,
            reduce_b.moved,
            down_reduce.moved,
            up_sum,
            output,
        )
    )
    grad_send = (own_send + give_send.astype(f32)).astype(bf16)
    moved_a = swap_seq(grad_send[:cut], 2)
    while len(reduce_b.bits) > 2:
        reduce_b.step()
    down_reduce.step()
    up_moved = swap_seq(up_sum, 2)
    reduce_a.add()
    grad_inputs = home_rows(info, [(own_keep + give_keep.astype(f32)).astype(bf16)], 0)
    (
        moved_a,
        grad_rest,
        reduce_a.held,
        reduce_b.moved,
        down_reduce.moved,
        up_moved,
        grad_inputs,
    ) = tie(
        (
            moved_a,
            grad_send[cut:],
            reduce_a.held,
            reduce_b.moved,
            down_reduce.moved,
            up_moved,
            grad_inputs,
        )
    )
    moved_b = swap_seq(grad_rest, 2)
    reduce_b.add()
    down_reduce.add()
    mine, moves = exchange_four(
        jnp.concatenate(
            [reduce_a.held[:, :, k * 384 : (k + 1) * 384] for k in range(pairs - 1)]
            + [reduce_b.held],
            axis=1,
        ),
        index,
    )
    up_shard = (up_sum.astype(f32) + up_moved.astype(f32)).astype(bf16)
    mine, up_shard, down_held, moved_b, *moves = tie(
        (mine, up_shard, down_reduce.held[0], moved_b, *moves)
    )
    up_shard_other = swap_seq(up_shard, 1)
    total = mine.astype(f32)
    for part in moves:
        total = total + part.astype(f32)
    last = jnp.concatenate([down_held, total.astype(bf16)], axis=0)
    last_chip = swap_seq(last, 2)
    (grad_up,) = widen(
        info,
        [up_shard[None], up_shard_other[None]],
        [(which, 0, 0, shard, 0, middle, 0, 0, 0, middle, which) for which in (0, 1)],
        [(shard, hidden_width)],
    )
    grad_inputs = home_rows(info, [moved_a, moved_b], 1, (grad_inputs,))
    last_chip, grad_up, grad_inputs = tie((last_chip, grad_up, grad_inputs))
    last = jnp.where(y == 0, jnp.stack([last, last_chip]), jnp.stack([last_chip, last]))

    plan = []
    part_rows = (ff_shard + shard) // 2
    few = shard // 2
    b_rows = (shard + small_rows) // 2
    for which in (0, 1):
        for slot in (0, 1):

            def put(row, count, out, out_row, base, stride, column=0, wide=384):
                if count > 0:
                    plan.append(
                        (which, slot, row, count, column, wide, out, out_row, base, stride, which)
                    )

            low, high = slot * part_rows, (slot + 1) * part_rows
            cutoff = min(high, ff_shard)
            put(0, cutoff - low, 2, low, 0, half)
            put(cutoff - low, high - cutoff, 1, cutoff - ff_shard, 0, half)
            for pair in range(pairs):
                for kind in range(3):
                    base = kind * width + pair * 128
                    if pair < pairs - 1:
                        row, count, out_row = part_rows + pair * few, few, slot * few
                    else:
                        row, out_row = part_rows + (pairs - 1) * few, slot * b_rows
                        count = min(b_rows, shard - out_row)
                    put(row, count, 0, out_row, base, half, kind * 128, 128)
            start = part_rows + (pairs - 1) * few
            first = max(shard - slot * b_rows, 0)
            put(start + first, b_rows - first, 3, slot * b_rows + first - shard, 0, 384)
    grad_qkv, grad_out, grad_down, small_sums = widen(
        info,
        [last, swap_seq(last, 1)],
        plan,
        [(shard, 3 * width), (shard, width), (ff_shard, width), (small_rows, 2 * 384)],
    )
    small_sums = small_sums[:, :384] + small_sums[:, 384:]

    return (
        output,
        grad_inputs,
        grad_qkv,
        grad_out,
        grad_up,
        grad_down,
        small_sums[0:2, :shard],
        small_sums[6, :shard],
        small_sums[8, :ff_shard],
        small_sums[7, :shard],
        small_sums[2:4, :shard],
        small_sums[4:6, :shard],
    )


def solution(mesh):
    in_specs = (
        P("dp", "seq", None),
        P("dp", "seq", None),
        P("dp", None),
        P("dp", None),
        P("dp", None),
        P("dp", None),
        P(None, "dp"),
        P("dp"),
        P("dp"),
        P("dp"),
        P(None, "dp"),
        P(None, "dp"),
        P(),
    )
    out_specs = (
        P("dp", "seq", None),
        P("dp", "seq", None),
        P("dp", None),
        P("dp", None),
        P("dp", None),
        P("dp", None),
        P(None, "dp"),
        P("dp"),
        P("dp"),
        P("dp"),
        P(None, "dp"),
        P(None, "dp"),
    )
    return jax.shard_map(body, mesh=mesh, in_specs=in_specs, out_specs=out_specs, check_vma=False)
```

```python
import functools

import jax
import jax.numpy as jnp
from jax import lax
from jax.experimental import pallas as pl
from jax.experimental.pallas import tpu as pltpu
from jax.sharding import PartitionSpec as P

HEADS = 12
HEAD_DIM = 64
BLOCK = 64
RAND = 3

norm_eps = 1e-06
bf16 = jnp.bfloat16
f32 = jnp.float32
NN = (((1,), (0,)), ((), ()))
NT = (((1,), (1,)), ((), ()))
TN = (((0,), (0,)), ((), ()))
VMEM_BYTES = 60 << 20


def dot(a, b, dims=NN):
    return lax.dot_general(a, b, dims, preferred_element_type=f32)


def row_of(block, y, c, chunk_blocks):
    chunk = block // chunk_blocks
    place = (((chunk & 1) ^ c) << 1) | ((chunk >> 1) ^ y)
    return pl.multiple_of((place * chunk_blocks + block % chunk_blocks) * BLOCK, BLOCK)


class Rows:
    def __init__(self, info_ref, rand_ref, first_pair, nblocks):
        self.y, self.c = info_ref[0], info_ref[1]
        self.rand_ref = rand_ref
        self.nblocks = nblocks
        self.head = self.c * info_ref[2] + 2 * first_pair
        self.low = lax.broadcasted_iota(jnp.int32, (BLOCK, 128), 1) < HEAD_DIM
        self.low_row = lax.broadcasted_iota(jnp.int32, (1, 128), 1) < HEAD_DIM

    def at(self, block):
        return pl.ds(row_of(block, self.y, self.c, self.nblocks // 4), BLOCK)

    def two(self, tile):
        zero = jnp.zeros_like(tile)
        return jnp.concatenate(
            [jnp.where(self.low, tile, zero), jnp.where(self.low, zero, tile)], axis=0
        )

    def one(self, both):
        return jnp.where(self.low, both[:BLOCK], both[BLOCK:])

    def rand(self, i):
        middle = self.nblocks - 2
        base = (self.head * middle + (i - 1)) * RAND
        return [
            (self.rand_ref[base + t], self.rand_ref[base + middle * RAND + t]) for t in range(RAND)
        ]

    def near(self, load, ends, i, rand):
        mixed = [jnp.where(self.low, load(a), load(b)) for a, b in rand]
        return jnp.concatenate([ends, load(i - 1), load(i + 1), load(i)] + mixed, axis=0)

    def mask(self, scores, i):
        first = jnp.where(i == 1, -1e30, 0.0)
        last = jnp.where(i == self.nblocks - 2, -1e30, 0.0)
        bias = jnp.where(self.low_row, first, last).astype(f32)
        return jnp.concatenate(
            [scores[:, :128], scores[:, 128:256] + bias, scores[:, 256:]], axis=1
        )


def forward_kernel(info_ref, rand_ref, qkv_ref, *refs, nblocks, first, unroll):
    ctx_ref, lse_ref = refs[-2:]
    rows = Rows(info_ref, rand_ref, pl.program_id(0) + first, nblocks)

    def load(block, column):
        return qkv_ref[rows.at(block), column * 128 : (column + 1) * 128]

    def finish(block, scores, values):
        peak = jnp.max(scores, axis=1, keepdims=True)
        powers = jnp.exp(scores - peak).astype(bf16)
        both = dot(powers, jnp.concatenate([values, jnp.ones_like(values)], axis=1))
        totals = both[:, 128:]
        lse = peak + jnp.log(totals)
        ctx_ref[rows.at(block), :] = rows.one(both[:, :128] / totals).astype(bf16)
        lse_ref[rows.at(block), :128] = lse[:BLOCK]
        lse_ref[rows.at(block), 128:] = lse[BLOCK:]

    for edge in (0, nblocks - 1):
        scores = dot(rows.two(load(edge, 0)), qkv_ref[:, 128:256], NT)
        finish(edge, scores, qkv_ref[:, 256:384])
    key_ends = jnp.concatenate([load(0, 1), load(nblocks - 1, 1)], axis=0)
    value_ends = jnp.concatenate([load(0, 2), load(nblocks - 1, 2)], axis=0)

    def row(i):
        rand = rows.rand(i)
        keys = rows.near(lambda b: load(b, 1), key_ends, i, rand)
        values = rows.near(lambda b: load(b, 2), value_ends, i, rand)
        finish(i, rows.mask(dot(rows.two(load(i, 0)), keys, NT), i), values)

    def step(t, carry):
        for u in range(unroll):
            row(1 + t * unroll + u)
        return carry

    lax.fori_loop(0, (nblocks - 2) // unroll, step, 0)


def backward_kernel(
    info_ref, rand_ref, qkv_ref, own_ref, other_ref, ctx_ref, lse_ref, out_ref, sum_ref,
    key_sum, value_sum, grad_ref,
    *, nblocks, first, unroll
):
    rows = Rows(info_ref, rand_ref, pl.program_id(0) + first, nblocks)
    zero = jnp.zeros((BLOCK, 128), f32)
    half_rows = own_ref.shape[0]
    grad_ref[:half_rows] = own_ref[...]
    grad_ref[half_rows:] = other_ref[...]

    def load(block, column):
        return qkv_ref[rows.at(block), column * 128 : (column + 1) * 128]

    ones = jnp.ones((256, 128), bf16)

    def finish(block, scores, keys, values):
        grad = grad_ref[rows.at(block), :]
        both = grad.astype(f32) * ctx_ref[rows.at(block), :].astype(f32)
        high = both.astype(bf16)
        rest = (both - high.astype(f32)).astype(bf16)
        row_dot = dot(jnp.concatenate([rows.two(high), rows.two(rest)], axis=1), ones)
        lse = jnp.concatenate(
            [lse_ref[rows.at(block), :128], lse_ref[rows.at(block), 128:]], axis=0
        )
        grad = rows.two(grad)
        attn_grad = dot(grad, values, NT)
        attention, score_grad = [], []
        for k in range(scores.shape[1] // 128):
            part = slice(k * 128, (k + 1) * 128)
            probs = jnp.exp(scores[:, part] - lse)
            score_grad.append((probs * (attn_grad[:, part] - row_dot)).astype(bf16))
            attention.append(probs.astype(bf16))
        attention = jnp.concatenate(attention, axis=1)
        score_grad = jnp.concatenate(score_grad, axis=1)
        query_grad = dot(score_grad, keys) * HEAD_DIM ** (-0.5)
        out_ref[rows.at(block), 0:128] = rows.one(query_grad).astype(bf16)
        return grad, attention, score_grad

    for edge in (0, nblocks - 1):
        query = rows.two(load(edge, 0))
        keys, values = qkv_ref[:, 128:256], qkv_ref[:, 256:384]
        grad, attention, score_grad = finish(edge, dot(query, keys, NT), keys, values)
        if edge == 0:
            key_sum[...] = dot(score_grad, query, TN)
            value_sum[...] = dot(attention, grad, TN)
        else:
            key_sum[...] += dot(score_grad, query, TN)
            value_sum[...] += dot(attention, grad, TN)
    key_ends = jnp.concatenate([load(0, 1), load(nblocks - 1, 1)], axis=0)
    value_ends = jnp.concatenate([load(0, 2), load(nblocks - 1, 2)], axis=0)

    def row(i):
        rand = rows.rand(i)
        keys = rows.near(lambda b: load(b, 1), key_ends, i, rand)
        values = rows.near(lambda b: load(b, 2), value_ends, i, rand)
        query = rows.two(load(i, 0))
        scores = rows.mask(dot(query, keys, NT), i)
        grad, attention, score_grad = finish(i, scores, keys, values)
        for total, part in (
            (key_sum, dot(score_grad, query, TN)),
            (value_sum, dot(attention, grad, TN)),
        ):
            for slot, block in enumerate((0, nblocks - 1, i - 1, i + 1, i)):
                total[rows.at(block), :] += part[slot * BLOCK : (slot + 1) * BLOCK]
            for slot, (a, b) in enumerate(rand):
                tile = part[(5 + slot) * BLOCK : (6 + slot) * BLOCK]
                total[rows.at(a), :] += jnp.where(rows.low, tile, zero)
                total[rows.at(b), :] += jnp.where(rows.low, zero, tile)

    def step(t, carry):
        for u in range(unroll):
            row(1 + t * unroll + u)
        return carry

    lax.fori_loop(0, (nblocks - 2) // unroll, step, 0)
    out_ref[:, 128:256] = key_sum[...].astype(bf16)
    out_ref[:, 256:384] = value_sum[...].astype(bf16)
    sum_ref[0] = jnp.broadcast_to(
        jnp.sum(out_ref[...].astype(f32), axis=0, keepdims=True), (8, 384)
    )


def attend_forward(info, rand, qkv, first, pairs, total, into=()):
    length = qkv.shape[0]
    wide = pl.BlockSpec((length, 384), lambda p, *_: (0, p + first))
    slim = pl.BlockSpec((length, 128), lambda p, *_: (0, p + first))
    twin = pl.BlockSpec((length, 256), lambda p, *_: (0, p + first))
    return pl.pallas_call(
        functools.partial(forward_kernel, nblocks=length // BLOCK, first=first, unroll=10),
        grid_spec=pltpu.PrefetchScalarGridSpec(
            num_scalar_prefetch=2,
            grid=(pairs,),
            in_specs=[wide] + [pl.BlockSpec(memory_space=pl.ANY)] * len(into),
            out_specs=[slim, twin],
        ),
        out_shape=[
            jax.ShapeDtypeStruct((length, total * 128), bf16),
            jax.ShapeDtypeStruct((length, total * 256), f32),
        ],
        input_output_aliases={3 + k: k for k in range(len(into))},
        compiler_params=pltpu.CompilerParams(vmem_limit_bytes=VMEM_BYTES),
        name="attend_forward",
    )(info, rand, qkv, *into)


def attend_backward(info, rand, qkv, own_grad, other_grad, ctx, lse, first, pairs):
    length = qkv.shape[0]
    wide = pl.BlockSpec((length, 384), lambda p, *_: (0, p + first))
    slim = pl.BlockSpec((length, 128), lambda p, *_: (0, p + first))
    part = pl.BlockSpec((length // 2, 128), lambda p, *_: (0, p + first))
    twin = pl.BlockSpec((length, 256), lambda p, *_: (0, p + first))
    return pl.pallas_call(
        functools.partial(backward_kernel, nblocks=length // BLOCK, first=first, unroll=15),
        grid_spec=pltpu.PrefetchScalarGridSpec(
            num_scalar_prefetch=2,
            grid=(pairs,),
            in_specs=[wide, part, part, slim, twin],
            out_specs=[
                pl.BlockSpec((length, 384), lambda p, *_: (0, p)),
                pl.BlockSpec((1, 8, 384), lambda p, *_: (p, 0, 0)),
            ],
            scratch_shapes=[pltpu.VMEM((length, 128), f32)] * 2 + [pltpu.VMEM((length, 128), bf16)],
        ),
        out_shape=[
            jax.ShapeDtypeStruct((length, pairs * 384), bf16),
            jax.ShapeDtypeStruct((pairs, 8, 384), f32),
        ],
        compiler_params=pltpu.CompilerParams(vmem_limit_bytes=VMEM_BYTES),
        name="attend_backward",
    )(info, rand, qkv, own_grad, other_grad, ctx, lse)


def swap_dp(value, bit):
    size = lax.axis_size("dp")
    return lax.ppermute(value, "dp", [(i, i ^ bit) for i in range(size)])


def swap_seq(value, bit):
    size = lax.axis_size("seq")
    return lax.ppermute(value, "seq", [(i, i ^ bit) for i in range(size)])


def bits_of(size):
    return [size >> (k + 1) for k in range(size.bit_length() - 1)]


def widened(blocks):
    return sum((o for o, _ in blocks), []), jnp.concatenate([a for _, a in blocks], axis=0)


def across(block, bit):
    offsets, array = block
    return [offset ^ bit for offset in offsets], swap_dp(array, bit)


def first_bits(shard):
    block = ([0], shard[None])
    for bit in bits_of(lax.axis_size("dp"))[:-3]:
        block = widened([block, across(block, bit)])
    return block


def tied(blocks, *values):
    arrays = lax.optimization_barrier((*[array for _, array in blocks], *values))
    count = len(blocks)
    return [(blocks[k][0], arrays[k]) for k in range(count)] + list(arrays[count:])


class Reduce:
    def __init__(self, parts, index, y):
        count, rows, columns = parts.shape
        self.held, self.index, self.y = parts.reshape(count, 2, rows // 2, columns), index, y
        self.bits = [0] + bits_of(lax.axis_size("dp"))[::-1]

    def start(self):
        bit = self.bits.pop(0)
        if bit:
            view = self.held.reshape(-1, 2, *self.held.shape[1:])
            mine = (self.index // bit) % 2
        else:
            view, mine = self.held, self.y
        self.held = lax.dynamic_slice_in_dim(view, mine, 1, 1)[:, 0]
        give = lax.dynamic_slice_in_dim(view, 1 - mine, 1, 1)[:, 0]
        self.moved = swap_dp(give, bit) if bit else swap_seq(give, 2)

    def add(self):
        self.held = (self.held.astype(f32) + self.moved.astype(f32)).astype(bf16)

    def step(self):
        self.add()
        self.start()


def exchange_four(held, index):
    unit = lax.axis_size("dp") // 4
    me = index // unit
    mine = lax.dynamic_index_in_dim(held, me, 0, keepdims=False)
    moved = [
        swap_dp(lax.dynamic_index_in_dim(held, me ^ k, 0, keepdims=False), k * unit)
        for k in (1, 2, 3)
    ]
    return mine, moved


def prepare_kernel(info_ref, w_ref, qv_ref, gain_ref, shift_ref, out_ref, down_ref, up_ref, shard_ref):
    c = info_ref[1]
    third = w_ref.shape[1] // 3
    half = third // 2
    depth, few = qv_ref.shape[1], up_ref.shape[1]
    for kind in range(3):
        columns = pl.ds(pl.multiple_of(kind * third + c * half, 128), half)
        part = w_ref[:, columns]
        for pair in range(half // 128):
            at = (pair * 3 + kind) * 128
            shard_ref[0:depth, at : at + 128] = part[:, pair * 128 : (pair + 1) * 128]
    shard_ref[depth:] = jnp.zeros((8, 3 * half), bf16)
    shard_ref[depth : depth + 2, 0:depth] = qv_ref[...]
    shard_ref[depth + 2 : depth + 4, 0:depth] = gain_ref[...]
    shard_ref[depth + 4 : depth + 6, 0:depth] = shift_ref[...]
    shard_ref[depth + 6 : depth + 7, 0:depth] = out_ref[...]
    shard_ref[depth + 7 : depth + 8, 0:depth] = down_ref[...]
    shard_ref[depth : depth + 1, 128 : 128 + few] = up_ref[...]


def prepare(info, w_qkv, *small):
    depth, columns = w_qkv.shape
    arrays = (w_qkv, *small)
    return pl.pallas_call(
        prepare_kernel,
        grid_spec=pltpu.PrefetchScalarGridSpec(
            num_scalar_prefetch=1,
            grid=(1,),
            in_specs=[pl.BlockSpec(a.shape, lambda i, *_: (0, 0)) for a in arrays],
            out_specs=pl.BlockSpec((depth + 8, columns // 2), lambda i, *_: (0, 0)),
        ),
        out_shape=jax.ShapeDtypeStruct((depth + 8, columns // 2), bf16),
        compiler_params=pltpu.CompilerParams(vmem_limit_bytes=VMEM_BYTES),
        name="prepare",
    )(info, *arrays)


def project_kernel(info_ref, inputs_ref, *refs, offsets, shard, ff_shard):
    more, refs = refs[:3], refs[3:]
    pieces, refs = refs[: len(offsets)], refs[len(offsets) :]
    qkv_ref, tokens_ref, weight_ref, norms_ref, up_ref, bias_ref = refs
    step = pl.program_id(0)
    width = weight_ref.shape[0]
    half = width // 2

    def spread(part, size, target, at):
        shape = (part.shape[1], target)
        lane = lax.broadcasted_iota(jnp.int32, shape, 1) - at
        source = lax.broadcasted_iota(jnp.int32, shape, 0)
        return dot(part, jnp.where((lane == source) & (source < size), 1.0, 0.0).astype(bf16))

    @pl.when(step == 0)
    def _():
        norms = jnp.zeros((8, width), f32)
        for offset, piece in zip(offsets, pieces):
            place = info_ref[4] ^ offset
            at = pl.ds(pl.multiple_of(place * shard, 8), shard)
            weight_ref[at, :] = piece[0:shard]
            tail = piece[shard : shard + 8]
            norms = norms + spread(tail[:, :128], shard, width, place * shard)
            if ff_shard % 128 == 0:
                lanes = pl.ds(pl.multiple_of(place * ff_shard, 128), ff_shard)
                up_ref[:, lanes] = tail[:, 128 : 128 + ff_shard].astype(f32)
            else:
                part = spread(tail[:, 128:256], ff_shard, up_ref.shape[1], place * ff_shard)
                if offset == offsets[0]:
                    up_ref[...] = part
                else:
                    up_ref[...] += part
        norms_ref[...] = norms
        bias_ref[...] = jnp.zeros_like(bias_ref)
        for pair in range(half // 128):
            lanes = pl.ds(pl.multiple_of(info_ref[1] * half + pair * 128, 128), 128)
            bias_ref[0:1, pair * 384 : pair * 384 + 128] = norms_ref[0:1, lanes]
            bias_ref[0:1, pair * 384 + 256 : pair * 384 + 384] = norms_ref[1:2, lanes]
        tokens_ref[...] = inputs_ref[0]

    for k in range(3):

        @pl.when(step == k + 1)
        def _():
            tokens_ref[...] = more[k][...]

    wide = dot(tokens_ref[...], weight_ref[...]) + bias_ref[0:1]
    for pair in range(wide.shape[1] // 384):
        at = pair * 384
        query = wide[:, at : at + 128].astype(bf16).astype(f32) * HEAD_DIM ** (-0.5)
        qkv_ref[:, at : at + 128] = query.astype(bf16)
        qkv_ref[:, at + 128 : at + 384] = wide[:, at + 128 : at + 384].astype(bf16)


def project(info, inputs, more, pieces, offsets, shard, ff_shard):
    _, local_len, width = inputs.shape
    columns = pieces[0].shape[1]
    hidden = ff_shard * len(pieces)

    def whole(array):
        return pl.BlockSpec(array.shape, lambda i, *_: (0, 0), pipeline_mode=pl.Buffered(1))

    fixed = [((width, columns), bf16), ((8, width), f32), ((8, hidden), f32)]
    return pl.pallas_call(
        functools.partial(project_kernel, offsets=offsets, shard=shard, ff_shard=ff_shard),
        grid_spec=pltpu.PrefetchScalarGridSpec(
            num_scalar_prefetch=1,
            grid=(4,),
            in_specs=[pl.BlockSpec((1, local_len, width), lambda i, info: (info[0], 0, 0))]
            + [whole(array) for array in (*more, *pieces)],
            out_specs=[
                pl.BlockSpec((local_len, columns), lambda i, *_: (i, 0)),
                pl.BlockSpec((local_len, width), lambda i, *_: (i, 0)),
            ]
            + [pl.BlockSpec(shape, lambda i, *_: (0, 0)) for shape, _ in fixed],
            scratch_shapes=[pltpu.VMEM((8, columns), f32)],
        ),
        out_shape=[
            jax.ShapeDtypeStruct((4 * local_len, columns), bf16),
            jax.ShapeDtypeStruct((4 * local_len, width), bf16),
        ]
        + [jax.ShapeDtypeStruct(shape, kind) for shape, kind in fixed],
        compiler_params=pltpu.CompilerParams(vmem_limit_bytes=VMEM_BYTES),
        name="project",
    )(info, inputs, *more, *pieces)


CHUNK = 768


def gelu_pair(values):
    square = values * values
    inner = values * (0.7978845608028654 + 0.7978845608028654 * 0.044715 * square)
    gate = 0.5 + 0.5 * jnp.tanh(inner)
    active = values * gate
    slope = 2 * 0.7978845608028654 + 6 * 0.7978845608028654 * 0.044715 * square
    return active, gate + (active - active * gate) * slope


def norm_parts(values):
    center = values - jnp.mean(values, axis=-1, keepdims=True)
    spread = jnp.mean(center * center, axis=-1, keepdims=True)
    inverse = lax.rsqrt(spread + norm_eps)
    return center * inverse, inverse


def norm_back(grad, unit, inverse, gain):
    scaled = grad * gain
    return inverse * (
        scaled
        - jnp.mean(scaled, axis=-1, keepdims=True)
        - unit * jnp.mean(scaled * unit, axis=-1, keepdims=True)
    )


def middle_kernel(
    info_ref,
    tokens_ref,
    ctx_ref,
    ctx_other_ref,
    cotangent_ref,
    up_ref,
    up_other_ref,
    *refs,
    down_plan,
    steps,
):
    n_down = 1 + max(entry[0] for entry in down_plan)
    down_refs, refs = refs[:n_down], refs[n_down:]
    (
        norm_ref,
        bias_up_ref,
        keep_ref,
        send_ref,
        ctx_all_ref,
        normed_ref,
        active_ref,
        hidden_mine_ref,
        hidden_other_ref,
        ffn_mine_ref,
        ffn_other_ref,
        first_ref,
        branch_mine_ref,
        branch_other_ref,
        ctx_grad_ref,
        ctx_send_ref,
        sums_ref,
        up_sums_ref,
        down_all,
        out_all,
        change_all,
        wide,
    ) = refs
    c, index, flip = info_ref[1], info_ref[4], info_ref[5]
    step = pl.program_id(0)
    half = ctx_ref.shape[1]
    middle = up_ref.shape[1] - half
    hidden = 2 * middle

    def up_part(k):
        inside = k * CHUNK % middle
        return (up_ref if k * CHUNK < middle else up_other_ref)[:, inside : inside + CHUNK]

    def lanes(which, size):
        return pl.ds(pl.multiple_of(which * size, 128), size)

    def rows(which, size):
        return pl.ds(pl.multiple_of(which * size, 16), size)

    @pl.when(step == 0)
    def _():
        out_all[:, lanes(c, half)] = up_ref[:, middle:]
        out_all[:, lanes(1 - c, half)] = up_other_ref[:, middle:]
        for source, slot, offset, which in down_plan:
            size = down_refs[source].shape[1]
            block = (index ^ offset ^ flip) * 2 + (info_ref[0] ^ (which // 2))
            down_all[rows(block, size), lanes(c ^ (which % 2), half)] = down_refs[source][slot]
        sums_ref[...] = jnp.zeros_like(sums_ref)
        up_sums_ref[...] = jnp.zeros_like(up_sums_ref)

    bias_out, bias_down = norm_ref[6:7], norm_ref[7:8]
    gain_1, gain_2, shift_1, shift_2 = (norm_ref[k : k + 1] for k in (2, 3, 4, 5))
    ctx_all_ref[:, lanes(c, half)] = ctx_ref[...]
    ctx_all_ref[:, lanes(1 - c, half)] = ctx_other_ref[...]
    branch = dot(ctx_all_ref[...], out_all[...]) + bias_out
    unit_1, inverse_1 = norm_parts(tokens_ref[...].astype(f32) + branch)
    normed = unit_1 * gain_1 + shift_1
    normed_low = normed.astype(bf16)
    normed_ref[...] = normed_low

    total = jnp.zeros_like(branch)
    for k in range(hidden // CHUNK):
        part = slice(k * CHUNK, (k + 1) * CHUNK)
        which = c ^ (k * CHUNK // middle)
        inside = k * CHUNK % middle
        at = pl.ds(pl.multiple_of(which * middle + inside, 128), CHUNK)
        bias = bias_up_ref[0:1, at]
        active, change = gelu_pair(dot(normed_low, up_part(k)) + bias)
        active = active.astype(bf16)
        active_ref[:, at] = active
        change_all[:, part] = change.astype(bf16)
        total = total + dot(active, down_all[part])

    unit_2, inverse_2 = norm_parts(normed + total + bias_down)
    result = (unit_2 * gain_2 + shift_2).astype(bf16)

    @pl.when(step < steps // 2)
    def _():
        keep_ref[0] = result

    @pl.when(step >= steps // 2)
    def _():
        send_ref[...] = result


    cotangent = cotangent_ref[...].astype(f32)
    pre_second = norm_back(cotangent, unit_2, inverse_2, gain_2)
    ffn_grad = pre_second.astype(bf16)
    wide[...] = ffn_grad
    ffn_mine_ref[...] = wide[:, lanes(c, half)]
    ffn_other_ref[...] = wide[:, lanes(1 - c, half)]

    def add(row, values):
        sums_ref[row : row + 1] += jnp.sum(values, axis=0, keepdims=True)

    add(1, ffn_grad.astype(f32))
    add(3, cotangent * unit_2)
    add(5, cotangent)

    total = jnp.zeros_like(branch)
    for k in range(hidden // CHUNK):
        part = slice(k * CHUNK, (k + 1) * CHUNK)
        grad = (dot(ffn_grad, down_all[part], NT) * change_all[:, part]).astype(bf16)
        target = hidden_mine_ref if k * CHUNK < middle else hidden_other_ref
        inside = k * CHUNK % middle
        target[:, inside : inside + CHUNK] = grad
        which = c ^ (k * CHUNK // middle)
        at = pl.ds(pl.multiple_of(which * middle + inside, 128), CHUNK)
        up_sums_ref[0:1, at] += jnp.sum(grad.astype(f32), axis=0, keepdims=True)
        total = total + dot(grad, up_part(k), NT)

    normed_grad = pre_second + total
    pre_first = norm_back(normed_grad, unit_1, inverse_1, gain_1)
    first_ref[...] = pre_first
    branch_grad = pre_first.astype(bf16)
    wide[...] = branch_grad
    branch_mine_ref[...] = wide[:, lanes(c, half)]
    branch_other_ref[...] = wide[:, lanes(1 - c, half)]
    add(0, branch_grad.astype(f32))
    add(2, normed_grad * unit_1)
    add(4, normed_grad)
    ctx_grad = dot(branch_grad, out_all[...], NT).astype(bf16)
    wide[...] = ctx_grad
    ctx_grad_ref[...] = wide[:, lanes(c, half)]
    ctx_send_ref[...] = wide[:, lanes(1 - c, half)]


def feed_forward(info, tokens, ctx, ctx_other, cotangent, up, up_other, down_groups, norms, bias_up):
    count, width = cotangent.shape
    half = ctx.shape[1]
    middle = up.shape[1] - half
    hidden = 2 * middle
    tile = 256
    steps = count // tile
    arrays, plan = [], []
    for offsets, which, array in down_groups:
        for slot, offset in enumerate(offsets):
            plan.append((len(arrays), slot, offset, which))
        arrays.append(array)

    def tiled(columns):
        return pl.BlockSpec((tile, columns), lambda i, *_: (i, 0))

    def whole(array):
        rank = len(array.shape)
        return pl.BlockSpec(
            array.shape, lambda i, *_: (0,) * rank, pipeline_mode=pl.Buffered(1)
        )

    outs = [
        ((count, width), bf16),
        ((count, width), bf16),
        ((count, hidden), bf16),
        ((count, middle), bf16),
        ((count, middle), bf16),
        ((count, half), bf16),
        ((count, half), bf16),
        ((count, width), f32),
        ((count, half), bf16),
        ((count, half), bf16),
        ((count, half), bf16),
        ((count, half), bf16),
    ]
    sums = [((8, width), f32), ((8, hidden), f32)]
    return pl.pallas_call(
        functools.partial(middle_kernel, down_plan=plan, steps=steps),
        grid_spec=pltpu.PrefetchScalarGridSpec(
            num_scalar_prefetch=1,
            grid=(steps,),
            in_specs=[tiled(width), tiled(half), tiled(half), tiled(width), whole(up), whole(up_other)]
            + [whole(array) for array in arrays]
            + [whole(norms), whole(bias_up)],
            out_specs=[
                pl.BlockSpec(
                    (1, tile, width), lambda i, info: (info[0], jnp.minimum(i, steps // 2 - 1), 0)
                ),
                pl.BlockSpec((tile, width), lambda i, *_: (jnp.maximum(i - steps // 2, 0), 0)),
            ]
            + [tiled(shape[1]) for shape, _ in outs]
            + [pl.BlockSpec(shape, lambda i, *_: (0, 0)) for shape, _ in sums],
            scratch_shapes=[
                pltpu.VMEM((hidden, width), bf16),
                pltpu.VMEM((width, width), bf16),
                pltpu.VMEM((tile, hidden), bf16),
                pltpu.VMEM((tile, width), bf16),
            ],
        ),
        out_shape=[jax.ShapeDtypeStruct((2, count // 2, width), bf16)]
        + [jax.ShapeDtypeStruct((count // 2, width), bf16)]
        + [jax.ShapeDtypeStruct(shape, kind) for shape, kind in outs + sums],
        compiler_params=pltpu.CompilerParams(vmem_limit_bytes=VMEM_BYTES),
        name="feed_forward",
    )(info, tokens, ctx, ctx_other, cotangent, up, up_other, *arrays, norms, bias_up)


def home_kernel(info_ref, *refs, count):
    start = 0
    for ref in refs[:count]:
        refs[-1][0, start : start + ref.shape[0]] = ref[...]
        start += ref.shape[0]


def home_rows(info, pieces, which, into=()):
    rows = sum(piece.shape[0] for piece in pieces)
    width = pieces[0].shape[1]
    return pl.pallas_call(
        functools.partial(home_kernel, count=len(pieces)),
        grid_spec=pltpu.PrefetchScalarGridSpec(
            num_scalar_prefetch=1,
            grid=(1,),
            in_specs=[pl.BlockSpec(piece.shape, lambda i, *_: (0, 0)) for piece in pieces]
            + [pl.BlockSpec(memory_space=pl.ANY)] * len(into),
            out_specs=pl.BlockSpec((1, rows, width), lambda i, info: (info[0] ^ which, 0, 0)),
        ),
        out_shape=jax.ShapeDtypeStruct((2, rows, width), bf16),
        input_output_aliases={1 + len(pieces): 0} if into else {},
        name="home_rows",
    )(info, *pieces, *into)


def widen_kernel(info_ref, *refs, plan, n_in):
    ins, outs = refs[:n_in], refs[n_in:]
    c = info_ref[1]
    for source, slot, row, rows, column, width, out, out_row, base, stride, which in plan:
        at = pl.ds(pl.multiple_of(base + (c ^ which) * stride, 128), width)
        outs[out][out_row : out_row + rows, at] = ins[source][
            slot, row : row + rows, column : column + width
        ].astype(f32)


def widen(info, arrays, plan, shapes):
    return pl.pallas_call(
        functools.partial(widen_kernel, plan=plan, n_in=len(arrays)),
        grid_spec=pltpu.PrefetchScalarGridSpec(
            num_scalar_prefetch=1,
            grid=(1,),
            in_specs=[pl.BlockSpec(a.shape, lambda i, *_: (0, 0, 0)) for a in arrays],
            out_specs=[pl.BlockSpec(shape, lambda i, *_: (0, 0)) for shape in shapes],
        ),
        out_shape=[jax.ShapeDtypeStruct(shape, f32) for shape in shapes],
        compiler_params=pltpu.CompilerParams(vmem_limit_bytes=VMEM_BYTES),
        name="widen",
    )(info, *arrays)


def body(
    inputs,
    out_grad,
    w_qkv,
    w_attn_out,
    w_up,
    w_down,
    bias_qv,
    bias_out,
    bias_up,
    bias_down,
    norm_gain,
    norm_shift,
    rand_blocks,
):
    _, local_len, width = inputs.shape
    dp = lax.axis_size("dp")
    index = lax.axis_index("dp")
    seat = lax.axis_index("seq")
    y, c = seat // 2, seat % 2
    heads_here = HEADS // 2
    pairs = heads_here // 2
    half = width // 2
    hidden_width = w_up.shape[1]
    middle = hidden_width // 2
    own = 2 * local_len
    shard = width // dp
    ff_shard = hidden_width // dp
    qkv_width = 3 * half
    flip = c * (dp // 2)
    info = jnp.stack([y, c, jnp.int32(heads_here), jnp.int32(0), index, flip]).astype(jnp.int32)
    rand = rand_blocks.reshape(-1)

    def pick(values, which):
        return lax.dynamic_index_in_dim(values, which, 0, keepdims=False)

    def column(value, which):
        return lax.dynamic_slice_in_dim(value, which * (value.shape[1] // 2), value.shape[1] // 2, 1)

    tie = lax.optimization_barrier

    given = pick(inputs, 1 - y)
    qkv_shard = prepare(
        info, w_qkv, bias_qv, norm_gain, norm_shift, bias_out[None], bias_down[None], bias_up[None]
    )
    bits = bits_of(dp)
    cut = local_len // 2
    chip_a = swap_seq(given[:cut], 2)
    mine = pick(inputs, y)
    first_moves = [swap_dp(qkv_shard, bit) for bit in bits]
    up_out = jnp.concatenate([column(w_up, c), column(w_attn_out, c)], axis=1)
    other_mine = swap_seq(mine, 1)
    down_shard = lax.dynamic_slice(w_down, (y * (ff_shard // 2), c * half), (ff_shard // 2, half))
    chip_a, rest, up_out, other_mine, down_shard, *first_moves = tie(
        (chip_a, given[cut:], up_out, other_mine, down_shard, *first_moves)
    )
    down_0 = first_bits(down_shard)
    down_far = across(down_0, bits[-3])
    chip_b = swap_seq(rest, 2)
    held = [(0, qkv_shard)] + list(zip(bits, first_moves))
    if dp == 8:
        held = held + [
            (o ^ bit, swap_dp(part, bit))
            for o, part, bit in (
                (bits[0], first_moves[0], bits[1]),
                (bits[1], first_moves[1], bits[2]),
                (bits[0], first_moves[0], bits[2]),
            )
        ]
    else:
        held = [(0, qkv_shard)]
        for bit in bits:
            held = held + [(o ^ bit, swap_dp(part, bit)) for o, part in held]
    offsets = [offset for offset, _ in held]
    chip_b, cotangent_give, down_moved, *parts = tie(
        (chip_b, out_grad, down_far[1], *[part for _, part in held])
    )
    down_a = widened([down_0, (down_far[0], down_moved)])
    cotangent_chip = swap_seq(pick(cotangent_give, 1 - y), 2)
    held = list(zip(offsets, parts))
    if dp == 8:
        offset, part = held[4]
        held = held + [(offset ^ bits[2], swap_dp(part, bits[2]))]
    from_chip = jnp.concatenate([chip_a, chip_b], axis=0)
    other_chip = swap_seq(from_chip, 1)
    offsets = [offset for offset, _ in held]
    pieces = [part for _, part in held]
    up_out = lax.all_gather(up_out, "dp", axis=0, tiled=True)
    near, side = bits[-2:]
    down_b, down_a_side = across(down_a, near), across(down_a, side)

    qkv, tokens, full_qkv, norms, bias_up_row = project(
        info, inputs, (from_chip, other_mine, other_chip), pieces, offsets, shard, ff_shard
    )
    down_b, down_a_side, qkv, cotangent_chip = tied([down_b, down_a_side], qkv, cotangent_chip)
    down_b_side = across(down_b, side)
    down_a = widened([down_a, down_a_side])
    down_a_chip = swap_seq(down_a[1], 2)
    ctx, lse = attend_forward(info, rand, qkv, 0, 1, pairs)
    down_b_side, qkv, ctx, lse, down_a_chip, up_out = tied(
        [down_b_side], qkv, ctx, lse, down_a_chip, up_out
    )
    up_other = swap_seq(up_out, 1)
    down_b = widened([down_b, down_b_side])
    down_b_chip = swap_seq(down_b[1], 2)
    down_a_core = swap_seq(down_a[1], 1)
    down_a_both = swap_seq(down_a_chip, 1)
    ctx, lse = attend_forward(info, rand, qkv, 1, pairs - 1, pairs, (ctx, lse))
    ctx, lse, down_b_chip, down_a_core, down_a_both, up_other = tie(
        (ctx, lse, down_b_chip, down_a_core, down_a_both, up_other)
    )
    ctx_other = swap_seq(ctx[own:], 1)
    down_groups = [
        (down_a[0], 0, down_a[1]),
        (down_a[0], 1, down_a_core),
        (down_a[0], 2, down_a_chip),
        (down_a[0], 3, down_a_both),
        (down_b[0], 0, down_b[1]),
        (down_b[0], 1, swap_seq(down_b[1], 1)),
        (down_b[0], 2, down_b_chip),
        (down_b[0], 3, swap_seq(down_b_chip, 1)),
    ]
    cotangent = jnp.concatenate([pick(out_grad, y), cotangent_chip], axis=0)
    (
        out_keep,
        out_send,
        ctx_all,
        normed,
        active,
        hidden_mine,
        hidden_other,
        ffn_mine,
        ffn_other,
        pre_first,
        branch_mine,
        branch_other,
        ctx_grad,
        ctx_send,
        sums,
        up_sums,
    ) = feed_forward(
        info, tokens, ctx, ctx_other, cotangent, up_out, up_other, down_groups, norms, bias_up_row
    )
    ctx_other_grad = swap_seq(ctx_send, 1)

    def grad_of(left, right):
        return dot(left, right, TN)

    up_give = swap_seq(grad_of(normed, hidden_other).astype(bf16), 1)
    down_give = swap_seq(grad_of(active, ffn_other).astype(bf16), 1)
    out_give = swap_seq(grad_of(ctx_all, branch_other).astype(bf16), 1)
    up_grad = (grad_of(normed, hidden_mine) + up_give.astype(f32)).astype(bf16)
    up_sum = lax.psum_scatter(up_grad, "dp", scatter_dimension=0, tiled=True)
    down_grad = (grad_of(active, ffn_mine) + down_give.astype(f32)).astype(bf16)
    out_weight_grad = (grad_of(ctx_all, branch_mine) + out_give.astype(f32)).astype(bf16)
    down_reduce = Reduce(
        jnp.concatenate(
            [down_grad.reshape(dp, ff_shard, half), out_weight_grad.reshape(dp, shard, half)],
            axis=1,
        ),
        index,
        y,
    )
    down_reduce.start()
    ctx_grad, ctx_other_grad, _ = tie((ctx_grad, ctx_other_grad, down_reduce.held))

    proj_a, proj_sums_a = attend_backward(
        info, rand, qkv, ctx_grad, ctx_other_grad, ctx, lse, 0, pairs - 1
    )
    proj_a, ctx_grad, down_reduce.moved = tie((proj_a, ctx_grad, down_reduce.moved))
    down_reduce.step()
    out_home = swap_seq(out_send, 2)
    wide_a = 384 * (pairs - 1)
    grad_a = grad_of(tokens, proj_a).astype(bf16)
    reduce_a = Reduce(grad_a.reshape(dp, shard, wide_a), index, y)
    reduce_a.start()
    weight_a, weight_b = full_qkv[:, :wide_a], full_qkv[:, wide_a:]
    input_a = dot(proj_a, weight_a, NT)
    ctx_grad, input_a, _ = tie((ctx_grad, input_a, reduce_a.held))
    proj_b, proj_sums_b = attend_backward(
        info, rand, qkv, ctx_grad, ctx_other_grad, ctx, lse, pairs - 1, 1
    )
    proj_b, reduce_a.moved, down_reduce.moved, out_home = tie(
        (proj_b, reduce_a.moved, down_reduce.moved, out_home)
    )
    output = home_rows(info, [out_home], 1, (out_keep,))
    while len(down_reduce.bits) > 1:
        down_reduce.step()
    while len(reduce_a.bits) > 2:
        reduce_a.step()

    def input_part(start, rows):
        return input_a[start : start + rows] + dot(proj_b[start : start + rows], weight_b, NT)

    give_send = swap_seq(input_part(own + local_len, local_len).astype(bf16), 1)
    give_keep = swap_seq(input_part(own, local_len).astype(bf16), 1)
    grad_b = grad_of(tokens, proj_b).astype(bf16)
    proj_sums = jnp.concatenate([proj_sums_a, proj_sums_b])[:, 0].reshape(pairs, 3, 128)
    my_sums = jnp.stack([proj_sums[:, 0].reshape(-1), proj_sums[:, 2].reshape(-1)])
    bias_qv_grad = lax.dynamic_update_slice(
        jnp.zeros((2, width), f32), my_sums, (jnp.int32(0), c * half)
    )

    rows = jnp.concatenate([bias_qv_grad, sums[2:6], sums[0:2]], axis=0)
    rows = rows.reshape(8, dp, shard).transpose(1, 0, 2)
    small_rows = 16
    small_grads = jnp.concatenate(
        [
            jnp.pad(rows, ((0, 0), (0, 0), (0, 384 - shard))),
            jnp.pad(up_sums[0].reshape(dp, 1, ff_shard), ((0, 0), (0, 7), (0, 384 - ff_shard))),
        ],
        axis=1,
    ).astype(bf16)
    reduce_b = Reduce(
        jnp.concatenate(
            [grad_b.reshape(dp, shard, 384), small_grads], axis=1
        ),
        index,
        y,
    )
    reduce_b.start()
    own_send = pre_first[local_len:] + input_part(local_len, local_len)
    own_keep = pre_first[:local_len] + input_part(0, local_len)
    (
        give_send,
        give_keep,
        own_send,
        own_keep,
        reduce_a.moved,
        reduce_b.moved,
        down_reduce.moved,
        up_sum,
        output,
    ) = tie(
        (
            give_send,
            give_keep,
            own_send,
            own_keep,
            reduce_a.moved,
            reduce_b.moved,
            down_reduce.moved,
            up_sum,
            output,
        )
    )
    grad_send = (own_send + give_send.astype(f32)).astype(bf16)
    moved_a = swap_seq(grad_send[:cut], 2)
    while len(reduce_b.bits) > 2:
        reduce_b.step()
    down_reduce.step()
    up_moved = swap_seq(up_sum, 2)
    reduce_a.add()
    grad_inputs = home_rows(info, [(own_keep + give_keep.astype(f32)).astype(bf16)], 0)
    (
        moved_a,
        grad_rest,
        reduce_a.held,
        reduce_b.moved,
        down_reduce.moved,
        up_moved,
        grad_inputs,
    ) = tie(
        (
            moved_a,
            grad_send[cut:],
            reduce_a.held,
            reduce_b.moved,
            down_reduce.moved,
            up_moved,
            grad_inputs,
        )
    )
    moved_b = swap_seq(grad_rest, 2)
    reduce_b.add()
    down_reduce.add()
    mine, moves = exchange_four(
        jnp.concatenate(
            [reduce_a.held[:, :, k * 384 : (k + 1) * 384] for k in range(pairs - 1)]
            + [reduce_b.held],
            axis=1,
        ),
        index,
    )
    up_shard = (up_sum.astype(f32) + up_moved.astype(f32)).astype(bf16)
    mine, up_shard, down_held, moved_b, *moves = tie(
        (mine, up_shard, down_reduce.held[0], moved_b, *moves)
    )
    up_shard_other = swap_seq(up_shard, 1)
    total = mine.astype(f32)
    for part in moves:
        total = total + part.astype(f32)
    last = jnp.concatenate([down_held, total.astype(bf16)], axis=0)
    last_chip = swap_seq(last, 2)
    (grad_up,) = widen(
        info,
        [up_shard[None], up_shard_other[None]],
        [(which, 0, 0, shard, 0, middle, 0, 0, 0, middle, which) for which in (0, 1)],
        [(shard, hidden_width)],
    )
    grad_inputs = home_rows(info, [moved_a, moved_b], 1, (grad_inputs,))
    last_chip, grad_up, grad_inputs = tie((last_chip, grad_up, grad_inputs))
    last = jnp.where(y == 0, jnp.stack([last, last_chip]), jnp.stack([last_chip, last]))

    plan = []
    part_rows = (ff_shard + shard) // 2
    few = shard // 2
    b_rows = (shard + small_rows) // 2
    for which in (0, 1):
        for slot in (0, 1):

            def put(row, count, out, out_row, base, stride, column=0, wide=384):
                if count > 0:
                    plan.append(
                        (which, slot, row, count, column, wide, out, out_row, base, stride, which)
                    )

            low, high = slot * part_rows, (slot + 1) * part_rows
            cutoff = min(high, ff_shard)
            put(0, cutoff - low, 2, low, 0, half)
            put(cutoff - low, high - cutoff, 1, cutoff - ff_shard, 0, half)
            for pair in range(pairs):
                for kind in range(3):
                    base = kind * width + pair * 128
                    if pair < pairs - 1:
                        row, count, out_row = part_rows + pair * few, few, slot * few
                    else:
                        row, out_row = part_rows + (pairs - 1) * few, slot * b_rows
                        count = min(b_rows, shard - out_row)
                    put(row, count, 0, out_row, base, half, kind * 128, 128)
            start = part_rows + (pairs - 1) * few
            first = max(shard - slot * b_rows, 0)
            put(start + first, b_rows - first, 3, slot * b_rows + first - shard, 0, 384)
    grad_qkv, grad_out, grad_down, small_sums = widen(
        info,
        [last, swap_seq(last, 1)],
        plan,
        [(shard, 3 * width), (shard, width), (ff_shard, width), (small_rows, 2 * 384)],
    )
    small_sums = small_sums[:, :384] + small_sums[:, 384:]

    return (
        output,
        grad_inputs,
        grad_qkv,
        grad_out,
        grad_up,
        grad_down,
        small_sums[0:2, :shard],
        small_sums[6, :shard],
        small_sums[8, :ff_shard],
        small_sums[7, :shard],
        small_sums[2:4, :shard],
        small_sums[4:6, :shard],
    )


def solution(mesh):
    in_specs = (
        P("dp", "seq", None),
        P("dp", "seq", None),
        P("dp", None),
        P("dp", None),
        P("dp", None),
        P("dp", None),
        P(None, "dp"),
        P("dp"),
        P("dp"),
        P("dp"),
        P(None, "dp"),
        P(None, "dp"),
        P(),
    )
    out_specs = (
        P("dp", "seq", None),
        P("dp", "seq", None),
        P("dp", None),
        P("dp", None),
        P("dp", None),
        P("dp", None),
        P(None, "dp"),
        P("dp"),
        P("dp"),
        P("dp"),
        P(None, "dp"),
        P(None, "dp"),
    )
    return jax.shard_map(body, mesh=mesh, in_specs=in_specs, out_specs=out_specs, check_vma=False)
```
